256 devices in a mesh: group: 16 (over z, y_lo), tp: 16 (over x, y_hi, core).
Axes of the slice: x: 4, y: 4 (y_hi: 2, y_lo: 2; y = y_hi * 2 + y_lo), z: 8, core: 2. Of those that a mesh axis runs over, the one named last changes fastest.
Arguments:
- token_ids: int32 [2, 512], P(None, 'group'), may hold values from 0 to 1023
- row_counts: int32 [16], P('group'), may hold values from 8 to 32, as said below
- code_table: bfloat16 [1024, 5120], P(None, 'tp'), may hold values from -6 to 6
- x_weight: bfloat16 [5120, 10240], P('group', 'tp'), may hold values from -0.078125 to 0.078125
- z_weight: bfloat16 [5120, 10240], P('group', 'tp'), may hold values from -0.078125 to 0.078125
- dt_weight: bfloat16 [5120, 160], P('group', 'tp'), may hold values from -0.078125 to 0.078125
- bc_weight: bfloat16 [5120, 512], P('group', 'tp'), may hold values from -0.078125 to 0.078125
- dt_bias: float32 [160], P('tp'), may hold values from -3 to 0.5
- head_rate: float32 [160], P('tp'), may hold values from 0.05 to 8
- skip_gain: float32 [160], P('tp'), may hold values from 0.5 to 2
- norm_gain: float32 [10240], P('tp'), may hold values from 0.25 to 1.75
- out_weight: bfloat16 [10240, 5120], P('tp', 'group'), may hold values from -0.078125 to 0.078125
- ssm_state: bfloat16 [512, 160, 64, 256], P('group', 'tp')
Outputs:
- layer_out: bfloat16 [2, 512, 5120], P(None, 'group', 'tp')
The draws below stay inside these ranges and needn't reach their ends.
Inputs may be any that keep to these rules, and one draw needn't show every extreme that they name: `row_counts`: each count is a multiple of 8, and in every draw some group has all 32 rows live.
All inputs are finite; a program needn't handle non-finite values.
Results may differ from the reference program's by a relative error of at most 0.013.
Values may be sent and summed in bfloat16 or wider, within the bound.
No kernel may reach another device: no remote copies, remote signals or barrier semaphores. Data moves between devices by JAX's collectives and lax.ppermute only.
A program may use at most 128 MiB of HBM per device.

```python
import math
import jax
import jax.numpy as jnp
from jax import lax

D = 5120
INNER = 10240
STATE = 256
HEADDIM = 64
CODES = 1024
ROWS = 32
HEADS = 160
GROUPS = 16


def draw_row_counts(key, part):
    first_key, second_key = jax.random.split(key, 2)
    values = 8 * jax.random.randint(first_key, (GROUPS,), 1, ROWS // 8 + 1)
    chosen = jax.random.randint(second_key, (), 0, GROUPS)
    return jnp.where(jnp.arange(GROUPS) == chosen, ROWS, values).astype(jnp.int32)


def draw_ssm_state(key, part):
    base_key, row_key = jax.random.split(key, 2)
    shape = (GROUPS * ROWS, HEADS, HEADDIM, STATE)
    position = jnp.arange(HEADS, dtype=jnp.float32) / max(HEADS - 1, 1)
    head_scale = jnp.exp(jnp.log(3.0) * position)
    row_scale = jnp.exp(jax.random.uniform(row_key, (GROUPS * ROWS,), minval=0.0, maxval=jnp.log(10.0)))
    base = jax.random.normal(base_key, shape)
    return (base * (row_scale[:, None, None, None] * head_scale[None, :, None, None] / 16.0)).astype(jnp.bfloat16)


def touch_ends(drawn, own_key, smallest, largest):
    longest = drawn.shape.index(max(drawn.shape))
    spots = []
    for shift in (0, 1):
        where = [jax.random.randint(jax.random.fold_in(own_key, axis), (), 0, length) for axis, length in enumerate(drawn.shape)]
        where[longest] = (where[longest] + shift) % drawn.shape[longest]
        spots.append(tuple(where))
    return drawn.at[spots[0]].set(smallest).at[spots[1]].set(largest)


def raised(values, key, source, target, shards_of, factor):
    def block_of(dim):
        return (jnp.arange(values.shape[dim]) // (values.shape[dim] // shards_of)).reshape((-1,) + (1,) * (values.ndim - 1 - dim))

    first = jax.random.permutation(key, shards_of)[block_of(target)]
    far = (block_of(target) + shards_of // 2) % shards_of
    return jnp.where((block_of(source) == first) | (block_of(source) == far), factor * values, values)


def block_scale(key, extent, shards, least, high):
    factor_of = 1.0
    for dim, parts in shards:
        draws = jax.random.uniform(jax.random.fold_in(jax.random.fold_in(key, 6), dim), (parts,), jnp.float32, least / len(shards), high / len(shards))
        factor_of = factor_of * jnp.repeat(jnp.exp(draws), extent[dim] // parts).reshape((-1,) + (1,) * (len(extent) - 1 - dim))
    return factor_of


def normal_values(stream_key, dims, spread, reach, shards=(), held_as=jnp.bfloat16):
    values = jax.random.normal(stream_key, dims, jnp.float32) * spread
    if len(shards) > 0:
        values = block_scale(stream_key, dims, shards, -0.22, 0.18) * values
    return jnp.clip(values, min=-reach, max=reach).astype(held_as)


def noise_with(key, shape, deviation, reach, cuts, heavy, kind=jnp.bfloat16):
    drawn = deviation * jax.random.normal(key, shape, jnp.float32)
    if cuts:
        drawn = drawn * block_scale(key, shape, cuts, -0.22, 0.18)
    return jnp.clip(raised(drawn, jax.random.fold_in(key, 3), *heavy), -reach, reach).astype(kind)


def setup_inputs(seed: int = 0) -> dict:
    keys = jax.random.split(jax.random.key(seed), 14)
    return {
        "token_ids": touch_ends(jax.random.randint(keys[0], (2, GROUPS * ROWS), 0, CODES), jax.random.fold_in(keys[0], 1), 0, CODES - 1).astype(jnp.int32),
        "row_counts": draw_row_counts(jax.random.fold_in(keys[13], 71), 0),
        "code_table": normal_values(keys[2], (CODES, D), 1.0, 6.0, ((1, 16),)),
        "x_weight": normal_values(keys[3], (D, INNER), D ** -0.5, 0.078125, ((0, 16), (1, 16))),
        "z_weight": normal_values(keys[4], (D, INNER), D ** -0.5, 0.078125, ((0, 16), (1, 16))),
        "dt_weight": normal_values(keys[5], (D, HEADS), D ** -0.5, 0.078125, ((0, 16), (1, 16))),
        "bc_weight": normal_values(keys[6], (D, 2 * STATE), D ** -0.5, 0.078125, ((0, 16), (1, 16))),
        "dt_bias": jnp.clip(-3.0 + 3.5 * jax.random.uniform(keys[7], (HEADS,), jnp.float32) ** block_scale(keys[7], (HEADS,), ((0, 16),), -0.2, 0.2), -3.0, 0.5),
        "head_rate": jnp.clip(jnp.exp(math.log(8.0) - 5.075174 * jax.random.uniform(keys[8], (HEADS,), jnp.float32) ** block_scale(keys[8], (HEADS,), ((0, 16),), -0.2, 0.2)), 0.05, 8.0),
        "skip_gain": jnp.clip(0.5 + 1.5 * jax.random.uniform(keys[9], (HEADS,), jnp.float32) ** block_scale(keys[9], (HEADS,), ((0, 16),), -0.2, 0.2), 0.5, 2.0),
        "norm_gain": jnp.clip(1.0 + 0.15 * jax.random.normal(keys[10], (INNER,), jnp.float32), 0.25, 1.75),
        "out_weight": noise_with(keys[11], (INNER, D), INNER ** -0.5, 0.078125, ((0, 16), (1, 16)), (0, 1, 16, 2.0)),
        "ssm_state": draw_ssm_state(jax.random.fold_in(keys[13], 71), 0),
    }


def decode(x_pre, z_pre, dt_pre, bc_all, dt_bias, head_rate, skip_gain, state):
    row_count = state.shape[0]
    head_count = state.shape[1]
    head_size = state.shape[2]
    width = bc_all.shape[1] // 2
    inputs = jax.nn.silu(x_pre).reshape(2, row_count, head_count, head_size)
    step_dt = jax.nn.softplus(dt_pre.reshape(2, row_count, head_count) + dt_bias)
    decay_factor = jnp.exp(-step_dt * head_rate)
    state_in = bc_all[:, :width].reshape(2, row_count, width)
    readout = bc_all[:, width:].reshape(2, row_count, width)
    carried = state.astype(jnp.float32)
    outputs = []
    for decode_step in range(2):
        carried = decay_factor[decode_step][:, :, None, None] * carried + (step_dt[decode_step][:, :, None] * inputs[decode_step])[..., None] * state_in[decode_step][:, None, None, :]
        reading = jnp.einsum('rhpn,rn->rhp', carried, readout[decode_step], precision=lax.Precision.HIGHEST)
        reading = reading + skip_gain[None, :, None] * inputs[decode_step]
        outputs.append(reading.reshape(row_count, head_count * head_size))
    return jnp.concatenate(outputs, 0) * jax.nn.silu(z_pre)

def reference(token_ids, row_counts, code_table, x_weight, z_weight, dt_weight, bc_weight, dt_bias, head_rate, skip_gain, norm_gain, out_weight, ssm_state):

    def one_group(group_index):
        begin = (group_index * ROWS).astype(jnp.int32)
        group_ids = lax.dynamic_slice_in_dim(token_ids, begin, ROWS, 1).reshape(-1)
        embed = jnp.take(code_table, group_ids, axis=0)
        x_pre = jnp.dot(embed, x_weight, preferred_element_type=jnp.float32)
        z_pre = jnp.dot(embed, z_weight, preferred_element_type=jnp.float32)
        dt_pre = jnp.dot(embed, dt_weight, preferred_element_type=jnp.float32)
        bc_all = jnp.dot(embed, bc_weight, preferred_element_type=jnp.float32)
        state = lax.dynamic_slice_in_dim(ssm_state, begin, ROWS, 0)
        gated = decode(x_pre, z_pre, dt_pre, bc_all, dt_bias, head_rate, skip_gain, state)
        squares = lax.optimization_barrier(jnp.sum(gated * gated, axis=1))
        scale = lax.rsqrt(squares / INNER + 1e-05)
        mixed = (gated * scale[:, None] * norm_gain).astype(jnp.bfloat16)
        result = embed.astype(jnp.float32) + jnp.dot(mixed, out_weight, preferred_element_type=jnp.float32)
        result = result.reshape(2, ROWS, D)
        live = jnp.arange(ROWS, dtype=jnp.int32) < row_counts[group_index]
        return jnp.where(live[None, :, None], result, 0.0).astype(jnp.bfloat16)
    stacked = lax.map(one_group, jnp.arange(GROUPS, dtype=jnp.int32))
    return jnp.transpose(stacked, (1, 0, 2, 3)).reshape(2, GROUPS * ROWS, D)
```

```python
import functools

import jax
import jax.numpy as jnp
from jax import lax
from jax.experimental import pallas as pl
from jax.experimental.pallas import tpu as pltpu
from jax.sharding import Mesh
from jax.sharding import PartitionSpec as P

BF = jnp.bfloat16
F32 = jnp.float32
SCALE = 2.0**-20
GROUP = ("z", "yl")
TP = ("x", "yh", "core")
ALL = GROUP + TP
VMEM_LIMIT = 48 * 1024 * 1024


def nt(a, b):
    return lax.dot_general(a, b, (((1,), (1,)), ((), ())), preferred_element_type=F32)


def nn(a, b):
    return jnp.dot(a, b, preferred_element_type=F32)


def call(body, out_shape, args, in_smem=0, flops=1 << 20, grid=None, in_specs=None, out_specs=None):
    if in_specs is None:
        in_specs = [pl.BlockSpec(memory_space=pltpu.SMEM)] * in_smem + [
            pl.BlockSpec(memory_space=pltpu.VMEM)
        ] * (len(args) - in_smem)
        out_specs = jax.tree.map(lambda _: pl.BlockSpec(memory_space=pltpu.VMEM), out_shape)
    kwargs = {} if grid is None else {"grid": grid}
    return pl.pallas_call(
        body,
        out_shape=out_shape,
        in_specs=in_specs,
        out_specs=out_specs,
        compiler_params=pltpu.CompilerParams(vmem_limit_bytes=VMEM_LIMIT),
        cost_estimate=pl.CostEstimate(flops=flops, bytes_accessed=1 << 20, transcendentals=0),
        **kwargs,
    )(*args)


def split2(v):
    hi = v.astype(BF)
    return hi, (v - hi.astype(F32)).astype(BF)


def project_kernel(flag, e_own, e_oth, x_own, x_oth, z_own, z_oth, s_own, s_oth, out):
    inner = x_own.shape[1]
    groups, rows, width = out.shape

    def run(ea, eb):
        a = ea[...]
        b = eb[...]
        px = nn(a, x_own[...]) + nn(b, x_oth[...])
        out[:, :, :inner] = px.astype(BF).reshape(groups, rows, inner)
        pz = nn(a, z_own[...]) + nn(b, z_oth[...])
        out[:, :, inner : 2 * inner] = pz.astype(BF).reshape(groups, rows, inner)
        ps = nt(a, s_own[...]) + nt(b, s_oth[...])
        hi, lo = split2(ps)
        out[:, :, 2 * inner :] = jnp.concatenate([hi, lo], 1).reshape(groups, rows, width - 2 * inner)

    @pl.when(flag[0] == 1)
    def _():
        run(e_own, e_oth)

    @pl.when(flag[0] == 0)
    def _():
        run(e_oth, e_own)


def small_kernel(part, bc, small):
    total = part[0].astype(F32)
    for k in range(1, part.shape[0]):
        total = total + part[k].astype(F32)
    total = total[:, :64] + total[:, 64:]
    hi, lo = split2(total)
    bc[...] = jnp.concatenate([hi, lo], 1)
    small[...] = total


def state_kernel(c, s, out):
    rows = s.shape[0]
    for r in range(rows):
        m = s[r].reshape(s.shape[1] * s.shape[2], s.shape[3])
        g = nt(c[r], m)
        out[r] = g


def decode_kernel(part, small, bcv, g, bias, rate, skip, gain, out):
    heads = bias.shape[1]
    inner = gain.shape[1]
    rows = part.shape[1]
    half = rows // 2
    total = part[0].astype(F32)
    for k in range(1, part.shape[0]):
        total = total + part[k].astype(F32)
    x_pre = total[:, :inner]
    z_pre = total[:, inner:]
    pick = (
        lax.broadcasted_iota(jnp.int32, (heads, inner), 0)
        == lax.broadcasted_iota(jnp.int32, (heads, inner), 1) // (inner // heads)
    ).astype(F32)
    expand = functools.partial(
        jnp.dot, preferred_element_type=F32, precision=lax.Precision.HIGHEST
    )
    dt_pre = expand(small[:, 32 : 32 + heads], pick)
    bias_e = expand(bias[...], pick)
    rate_e = expand(rate[...], pick)
    skip_e = expand(skip[...], pick)
    pre = dt_pre + bias_e
    dt = jnp.maximum(pre, 0.0) + jnp.log1p(jnp.exp(-jnp.abs(pre)))
    decay = jnp.exp(-dt * rate_e)
    inputs = x_pre * jax.nn.sigmoid(x_pre)
    upd = dt * inputs
    gate = z_pre * jax.nn.sigmoid(z_pre)
    width = bcv.shape[1] // 2
    b = bcv[:, :width]
    c = bcv[:, width:]
    b1, b2 = b[:half], b[half:]
    c1, c2 = c[:half], c[half:]
    b11 = jnp.sum(b1 * c1, axis=1, keepdims=True)
    b12 = jnp.sum(b1 * c2, axis=1, keepdims=True)
    b22 = jnp.sum(b2 * c2, axis=1, keepdims=True)
    gs = g[...]
    g1 = gs[:, 0, :] + gs[:, 1, :]
    g2 = gs[:, 2, :] + gs[:, 3, :]
    d1, d2 = decay[:half], decay[half:]
    u1, u2 = upd[:half], upd[half:]
    read1 = (d1 * g1) * (1.0 / SCALE) + u1 * b11 + skip_e * inputs[:half]
    read2 = d2 * ((d1 * g2) * (1.0 / SCALE) + u1 * b12) + u2 * b22 + skip_e * inputs[half:]
    lim = 1e30
    gg1 = jnp.clip(read1 * gate[:half] * gain[...], -lim, lim)
    gg2 = jnp.clip(read2 * gate[half:] * gain[...], -lim, lim)
    out[...] = jnp.concatenate([gg1, gg2], 0).astype(BF)


def output_kernel(own_y, gg, w_own, w_oth, gain, out):
    y = own_y[0]
    groups, rows, inner = gg.shape
    cols = w_own.shape[0]
    v = gg[...].reshape(groups * rows, inner)
    raw = v.astype(F32) / gain[...]
    ss = jnp.sum(raw * raw, axis=1, keepdims=True)
    hi = ss.astype(BF).astype(F32)
    lo = ss - hi
    lane = lax.broadcasted_iota(jnp.int32, (groups * rows, 64), 1)
    tail = jnp.where(lane == 0, hi, jnp.where(lane == 1, lo, 0.0))
    for w, which in ((w_own, y), (w_oth, 1 - y)):
        o = jnp.concatenate([nt(v, w[...]), tail], 1).astype(BF).reshape(groups, rows, cols + 64)
        for k in range(groups):
            out[2 * k + which] = o[k]


def reduce_kernel(part, out, *, count):
    total = part[0].astype(F32)
    for k in range(1, part.shape[0]):
        total = total + part[k].astype(F32)
    cols = out.shape[1]
    ss = total[:, cols : cols + 1] + total[:, cols + 1 : cols + 2]
    out[...] = (total[:, :cols] * lax.rsqrt(ss / count + 1e-05)).astype(BF)


def per_device(
    token_ids,
    row_counts,
    code_table,
    x_weight,
    z_weight,
    dt_weight,
    bc_weight,
    dt_bias,
    head_rate,
    skip_gain,
    norm_gain,
    out_weight,
    ssm_state,
):
    rows = token_ids.shape[1]
    heads = dt_bias.shape[0]
    inner = x_weight.shape[1]
    wide = code_table.shape[1]
    y = lax.axis_index("yl")
    core = lax.axis_index("core")
    swap = []
    for z in range(8):
        for yy in range(2):
            for w in range(8):
                for c in range(2):
                    swap.append(((z * 2 + yy) * 16 + w * 2 + c, (w * 2 + yy) * 16 + z * 2 + c))
    pair = [(0, 1), (1, 0)]

    small_own = jnp.concatenate(
        [bc_weight.T, dt_weight.T, jnp.zeros((64 - 32 - heads, wide), BF)], 0
    )
    out_own = out_weight.T
    x_oth = lax.ppermute(x_weight, "yl", pair)
    z_oth = lax.ppermute(z_weight, "yl", pair)
    small_oth = lax.ppermute(small_own, "yl", pair)
    out_oth = lax.ppermute(out_own, "yl", pair)

    flat_ids = token_ids.reshape(-1)
    one_hot = (flat_ids[:, None] == jnp.arange(code_table.shape[0], dtype=jnp.int32)[None, :]).astype(BF)
    own_embed = jnp.dot(one_hot, code_table, preferred_element_type=F32).astype(BF)
    moved = lax.ppermute(own_embed, ALL, swap)
    e_own = lax.all_to_all(
        jnp.broadcast_to(moved[None], (8,) + moved.shape), ("x", "yh"), 0, 0
    ).reshape(8 * 2 * rows, wide)
    e_oth = lax.ppermute(e_own, "core", pair)
    flag = (y == core).astype(jnp.int32).reshape(1)
    part = call(
        project_kernel,
        jax.ShapeDtypeStruct((8, 2 * rows, 2 * inner + 128), BF),
        (flag, e_own, e_oth, x_weight, x_oth, z_weight, z_oth, small_own, small_oth),
        in_smem=1,
        flops=2 * 16 * rows * 2 * wide * (2 * inner + 128),
    )
    part = lax.all_to_all(part, "z", 0, 0)
    bc, small = call(
        small_kernel,
        (
            jax.ShapeDtypeStruct((2 * rows, 128), BF),
            jax.ShapeDtypeStruct((2 * rows, 64), F32),
        ),
        (part[:, :, 2 * inner :],),
    )
    bc_all = lax.all_to_all(jnp.broadcast_to(bc[None], (16,) + bc.shape), TP, 0, 0)
    bcv = (bc_all[:, :, :32].astype(F32) + bc_all[:, :, 64:96].astype(F32)).transpose(1, 0, 2)
    bcv = bcv.reshape(2 * rows, 512)
    c_hi, c_lo = split2(bcv[:, 256:] * SCALE)
    zero = jnp.zeros_like(c_hi[:rows])
    c_mat = jnp.stack(
        [c_hi[:rows], c_lo[:rows], c_hi[rows:], c_lo[rows:], zero, zero, zero, zero], 1
    )
    step = 4
    g = call(
        state_kernel,
        jax.ShapeDtypeStruct((rows, 8, inner), F32),
        (c_mat, ssm_state),
        grid=(rows // step,),
        in_specs=[
            pl.BlockSpec((step, 8, 256), lambda i: (i, 0, 0)),
            pl.BlockSpec((step,) + ssm_state.shape[1:], lambda i: (i, 0, 0, 0)),
        ],
        out_specs=pl.BlockSpec((step, 8, inner), lambda i: (i, 0, 0)),
        flops=2 * 8 * rows * inner * 256,
    )
    gain = norm_gain.reshape(1, inner)
    gg = call(
        decode_kernel,
        jax.ShapeDtypeStruct((2 * rows, inner), BF),
        (
            part[:, :, : 2 * inner],
            small,
            bcv,
            g,
            dt_bias.reshape(1, heads),
            head_rate.reshape(1, heads),
            skip_gain.reshape(1, heads),
            gain,
        ),
    )
    gg_all = lax.all_to_all(jnp.broadcast_to(gg[None], (8,) + gg.shape), "z", 0, 0)
    partial_out = call(
        output_kernel,
        jax.ShapeDtypeStruct((16, 2 * rows, wide + 64), BF),
        (y.reshape(1), gg_all, out_own, out_oth, gain),
        in_smem=1,
        flops=2 * 16 * rows * inner * 2 * wide,
    )
    partial_out = lax.all_to_all(partial_out, TP, 0, 0)
    mine = call(
        functools.partial(reduce_kernel, count=float(16 * inner)),
        jax.ShapeDtypeStruct((2 * rows, wide), BF),
        (partial_out,),
    )
    back = lax.ppermute(mine, ALL, swap)
    result = (own_embed.astype(F32) + back.astype(F32)).reshape(2, rows, wide)
    live = jnp.arange(rows, dtype=jnp.int32) < row_counts[0]
    return jnp.where(live[None, :, None], result, 0.0).astype(BF)


def solution(mesh):
    fine = Mesh(mesh.devices.reshape(8, 2, 4, 2, 2), ALL)
    return jax.shard_map(
        per_device,
        mesh=fine,
        in_specs=(
            P(None, GROUP),
            P(GROUP),
            P(None, TP),
            P(GROUP, TP),
            P(GROUP, TP),
            P(GROUP, TP),
            P(GROUP, TP),
            P(TP),
            P(TP),
            P(TP),
            P(TP),
            P(TP, GROUP),
            P(GROUP, TP, None, None),
        ),
        out_specs=P(None, GROUP, TP),
        check_vma=False,
    )
```

```python
import functools

import jax
import jax.numpy as jnp
from jax import lax
from jax.experimental import pallas as pl
from jax.experimental.pallas import tpu as pltpu
from jax.sharding import Mesh
from jax.sharding import PartitionSpec as P


BF = jnp.bfloat16
F32 = jnp.float32
SCALE = 2.0**-20
GROUP = ("z", "yl")
TP = ("x", "yh", "core")
ALL = GROUP + TP
VMEM_LIMIT = 48 * 1024 * 1024

FAR_FIRST = (4, 3, 5, 2, 6, 1, 7)


def nt(a, b):
    return lax.dot_general(a, b, (((1,), (1,)), ((), ())), preferred_element_type=F32)


def nn(a, b):
    return jnp.dot(a, b, preferred_element_type=F32)


def call(body, out_shape, args, in_smem=0, flops=1 << 20, grid=None, in_specs=None, out_specs=None, scratch=()):
    if in_specs is None:
        in_specs = [pl.BlockSpec(memory_space=pltpu.SMEM)] * in_smem + [
            pl.BlockSpec(memory_space=pltpu.VMEM)
        ] * (len(args) - in_smem)
        out_specs = jax.tree.map(lambda _: pl.BlockSpec(memory_space=pltpu.VMEM), out_shape)
    kwargs = {} if grid is None else {"grid": grid}
    return pl.pallas_call(
        body,
        out_shape=out_shape,
        in_specs=in_specs,
        out_specs=out_specs,
        scratch_shapes=scratch,
        compiler_params=pltpu.CompilerParams(vmem_limit_bytes=VMEM_LIMIT),
        cost_estimate=pl.CostEstimate(flops=flops, bytes_accessed=1 << 20, transcendentals=0),
        **kwargs,
    )(*args)


def split2(v):
    hi = v.astype(BF)
    return hi, (v - hi.astype(F32)).astype(BF)


def project_small_kernel(flag, e_own, e_oth, s_own, s_oth, out):
    groups, rows, width = out.shape

    def run(ea, eb):
        ps = nt(ea[...], s_own[...]) + nt(eb[...], s_oth[...])
        hi, lo = split2(ps)
        out[...] = jnp.concatenate([hi, lo], 1).reshape(groups, rows, width)

    @pl.when(flag[0] == 1)
    def _():
        run(e_own, e_oth)

    @pl.when(flag[0] == 0)
    def _():
        run(e_oth, e_own)


def project_kernel(place, e_own, e_oth, x_own, x_oth, z_own, z_oth, *outs):
    inner = x_own.shape[1]
    rows = outs[0].shape[0]
    groups = len(outs)

    def turned(ref):
        blocks = []
        for k in range(groups):
            at = lax.rem(place[1] + k, groups) * rows
            blocks.append(ref[pl.ds(pl.multiple_of(at, rows), rows), :])
        return jnp.concatenate(blocks, 0)

    def run(ea, eb):
        a = turned(ea)
        b = turned(eb)
        px = (nn(a, x_own[...]) + nn(b, x_oth[...])).astype(BF)
        for k in range(groups):
            outs[k][:, :inner] = px[k * rows : (k + 1) * rows]
        pz = (nn(a, z_own[...]) + nn(b, z_oth[...])).astype(BF)
        for k in range(groups):
            outs[k][:, inner:] = pz[k * rows : (k + 1) * rows]

    @pl.when(place[0] == 1)
    def _():
        run(e_own, e_oth)

    @pl.when(place[0] == 0)
    def _():
        run(e_oth, e_own)


def small_kernel(part, bc, small):
    total = part[0].astype(F32)
    for k in range(1, part.shape[0]):
        total = total + part[k].astype(F32)
    total = total[:, :64] + total[:, 64:]
    hi, lo = split2(total)
    both = jnp.concatenate([hi, lo], 1)
    for k in range(bc.shape[0]):
        bc[k] = both
    small[...] = total


def state_kernel(bc, s, out, dots, cmat):
    rows = cmat.shape[0]

    @pl.when(pl.program_id(0) == 0)
    def _():
        pieces = [bc[t] for t in range(bc.shape[0])]
        pieces = [p[:, :32].astype(F32) + p[:, 64:96].astype(F32) for p in pieces]
        b = jnp.concatenate(pieces[:8], 1)
        c = jnp.concatenate(pieces[8:], 1)
        b1, b2, c1, c2 = b[:rows], b[rows:], c[:rows], c[rows:]
        lane = lax.broadcasted_iota(jnp.int32, dots.shape, 1)
        b11 = jnp.sum(b1 * c1, axis=1, keepdims=True)
        b12 = jnp.sum(b1 * c2, axis=1, keepdims=True)
        b22 = jnp.sum(b2 * c2, axis=1, keepdims=True)
        dots[...] = jnp.where(lane == 0, b11, jnp.where(lane == 1, b12, b22))
        cmat[...] = jnp.zeros_like(cmat)
        for k, v in enumerate((c1, c2)):
            v = v * SCALE
            hi = v.astype(BF).astype(F32)
            cmat[:, 2 * k, :] = hi
            cmat[:, 2 * k + 1, :] = v - hi

    for r in range(s.shape[0]):
        m = s[r].reshape(s.shape[1] * s.shape[2], s.shape[3])
        g = nt(cmat[pl.program_id(0) * s.shape[0] + r].astype(BF), m)
        out[r] = g


def decode_kernel(*refs):
    parts, (small, dots, g, bias, rate, skip, gain, out) = refs[:8], refs[8:]
    heads = bias.shape[1]
    inner = gain.shape[1]
    half = parts[0].shape[0] // 2
    total = parts[0][...].astype(F32)
    for part in parts[1:]:
        total = total + part[...].astype(F32)
    x_pre = total[:, :inner]
    z_pre = total[:, inner:]
    pick = (
        lax.broadcasted_iota(jnp.int32, (heads, inner), 0)
        == lax.broadcasted_iota(jnp.int32, (heads, inner), 1) // (inner // heads)
    ).astype(F32)
    expand = functools.partial(
        jnp.dot, preferred_element_type=F32, precision=lax.Precision.HIGHEST
    )
    dt_pre = expand(small[:, 32 : 32 + heads], pick)
    bias_e = expand(bias[...], pick)
    rate_e = expand(rate[...], pick)
    skip_e = expand(skip[...], pick)
    pre = dt_pre + bias_e
    dt = jnp.maximum(pre, 0.0) + jnp.log1p(jnp.exp(-jnp.abs(pre)))
    decay = jnp.exp(-dt * rate_e)
    inputs = x_pre * jax.nn.sigmoid(x_pre)
    upd = dt * inputs
    gate = z_pre * jax.nn.sigmoid(z_pre)
    b11 = dots[:, 0:1]
    b12 = dots[:, 1:2]
    b22 = dots[:, 2:3]
    gs = g[...]
    g1 = gs[:, 0, :] + gs[:, 1, :]
    g2 = gs[:, 2, :] + gs[:, 3, :]
    d1, d2 = decay[:half], decay[half:]
    u1, u2 = upd[:half], upd[half:]
    read1 = (d1 * g1) * (1.0 / SCALE) + u1 * b11 + skip_e * inputs[:half]
    read2 = d2 * ((d1 * g2) * (1.0 / SCALE) + u1 * b12) + u2 * b22 + skip_e * inputs[half:]
    lim = 1e30
    gg1 = jnp.clip(read1 * gate[:half] * gain[...], -lim, lim)
    gg2 = jnp.clip(read2 * gate[half:] * gain[...], -lim, lim)
    both = jnp.concatenate([gg1, gg2], 0).astype(BF)
    for k in range(out.shape[0]):
        out[k] = both


def output_kernel(place, gg, w_own, w_oth, gain, keep, send):
    y = place[0]
    core = place[1]
    groups, rows, inner = gg.shape
    cols = w_own.shape[0]
    v = gg[...].reshape(groups * rows, inner)
    raw = v.astype(F32) / gain[...]
    ss = jnp.sum(raw * raw, axis=1, keepdims=True)
    hi = ss.astype(BF).astype(F32)
    lo = ss - hi
    lane = lax.broadcasted_iota(jnp.int32, (groups * rows, 64), 1)
    tail = jnp.where(lane == 0, hi, jnp.where(lane == 1, lo, 0.0))

    def block(w):
        o = jnp.concatenate([nt(v, w[...]), tail], 1)
        return o.reshape(groups, rows, cols + 64)

    @pl.when(y == core)
    def _():
        keep[...] = block(w_own)
        send[...] = block(w_oth).astype(BF)

    @pl.when(y != core)
    def _():
        keep[...] = block(w_oth)
        send[...] = block(w_own).astype(BF)


def pair_kernel(keep, got, out):
    total = keep[...] + got[...].astype(F32)
    cols = out.shape[2] - 64
    lane = lax.broadcasted_iota(jnp.int32, total.shape, 2)
    ss = total[:, :, cols : cols + 1] + total[:, :, cols + 1 : cols + 2]
    hi = ss.astype(BF).astype(F32)
    total = jnp.where(lane == cols, hi, jnp.where(lane == cols + 1, ss - hi, total))
    out[...] = total.astype(BF)


def reduce_kernel(part, out, *, count):
    total = part[0].astype(F32)
    for k in range(1, part.shape[0]):
        total = total + part[k].astype(F32)
    cols = out.shape[1]
    ss = total[:, cols : cols + 1] + total[:, cols + 1 : cols + 2]
    out[...] = (total[:, :cols] * lax.rsqrt(ss / count + 1e-05)).astype(BF)


def per_device(
    token_ids,
    row_counts,
    code_table,
    x_weight,
    z_weight,
    dt_weight,
    bc_weight,
    dt_bias,
    head_rate,
    skip_gain,
    norm_gain,
    out_weight,
    ssm_state,
):
    rows = token_ids.shape[1]
    heads = dt_bias.shape[0]
    inner = x_weight.shape[1]
    wide = code_table.shape[1]
    y = lax.axis_index("yl")
    core = lax.axis_index("core")
    swap = []
    for z in range(8):
        for yy in range(2):
            for w in range(8):
                for c in range(2):
                    swap.append(((z * 2 + yy) * 16 + w * 2 + c, (w * 2 + yy) * 16 + z * 2 + c))
    pair = [(0, 1), (1, 0)]

    x_oth = lax.ppermute(x_weight, "yl", pair)
    z_oth = lax.ppermute(z_weight, "yl", pair)
    small_own = jnp.concatenate(
        [bc_weight.T, dt_weight.T, jnp.zeros((64 - 32 - heads, wide), BF)], 0
    )
    small_oth = lax.ppermute(small_own, "yl", pair)
    out_own = out_weight.T
    out_oth = lax.ppermute(out_own, "yl", pair)

    flat_ids = token_ids.reshape(-1)
    codes = jnp.arange(code_table.shape[0], dtype=jnp.int32)
    one_hot = (flat_ids[:, None] == codes[None, :]).astype(BF)
    own_embed = jnp.dot(one_hot, code_table, preferred_element_type=F32).astype(BF)
    moved = lax.ppermute(own_embed, ALL, swap)
    e_own = lax.all_to_all(
        jnp.broadcast_to(moved[None], (8,) + moved.shape), ("x", "yh"), 0, 0
    ).reshape(8 * 2 * rows, wide)
    e_oth = lax.ppermute(e_own, "core", pair)
    flag = (y == core).astype(jnp.int32).reshape(1)
    part_small = call(
        project_small_kernel,
        jax.ShapeDtypeStruct((8, 2 * rows, 128), BF),
        (flag, e_own, e_oth, small_own, small_oth),
        in_smem=1,
        flops=2 * 16 * rows * 2 * wide * 128,
    )
    part_small = lax.all_to_all(part_small, "z", 0, 0)
    blocks = call(
        project_kernel,
        tuple(jax.ShapeDtypeStruct((2 * rows, 2 * inner), BF) for _ in range(8)),
        (
            jnp.stack([(y == core).astype(jnp.int32), lax.axis_index("z")]),
            e_own,
            e_oth,
            x_weight,
            x_oth,
            z_weight,
            z_oth,
        ),
        in_smem=1,
        flops=2 * 16 * rows * 2 * wide * 2 * inner,
    )
    parts = [blocks[0]]
    for k in FAR_FIRST:
        parts.append(lax.ppermute(blocks[k], "z", [(i, (i + k) % 8) for i in range(8)]))
    bc, small = call(
        small_kernel,
        (jax.ShapeDtypeStruct((16, 2 * rows, 128), BF), jax.ShapeDtypeStruct((2 * rows, 64), F32)),
        (part_small,),
    )
    bc_all = lax.all_to_all(bc, TP, 0, 0)
    step = 4
    g, dots = call(
        state_kernel,
        (jax.ShapeDtypeStruct((rows, 8, inner), F32), jax.ShapeDtypeStruct((rows, 128), F32)),
        (bc_all, ssm_state),
        grid=(rows // step,),
        in_specs=[
            pl.BlockSpec(bc_all.shape, lambda i: (0, 0, 0)),
            pl.BlockSpec((step,) + ssm_state.shape[1:], lambda i: (i, 0, 0, 0)),
        ],
        out_specs=(
            pl.BlockSpec((step, 8, inner), lambda i: (i, 0, 0)),
            pl.BlockSpec((rows, 128), lambda i: (0, 0)),
        ),
        scratch=[pltpu.VMEM((rows, 8, 256), F32)],
        flops=2 * 8 * rows * inner * 256,
    )
    gain = norm_gain.reshape(1, inner)
    gg = call(
        decode_kernel,
        jax.ShapeDtypeStruct((8, 2 * rows, inner), BF),
        (
            *parts,
            small,
            dots,
            g,
            dt_bias.reshape(1, heads),
            head_rate.reshape(1, heads),
            skip_gain.reshape(1, heads),
            gain,
        ),
    )
    gg_all = lax.all_to_all(gg, "z", 0, 0)
    keep, send = call(
        output_kernel,
        (
            jax.ShapeDtypeStruct((8, 2 * rows, wide + 64), F32),
            jax.ShapeDtypeStruct((8, 2 * rows, wide + 64), BF),
        ),
        (jnp.stack([y, core]), gg_all, out_own, out_oth, gain),
        in_smem=1,
        flops=2 * 16 * rows * inner * 2 * wide,
    )
    got = lax.ppermute(send, "core", pair)
    paired = call(pair_kernel, jax.ShapeDtypeStruct((8, 2 * rows, wide + 64), BF), (keep, got))
    partial_out = lax.all_to_all(paired, ("x", "yh"), 0, 0)
    mine = call(
        functools.partial(reduce_kernel, count=float(16 * inner)),
        jax.ShapeDtypeStruct((2 * rows, wide), BF),
        (partial_out,),
    )
    back = lax.ppermute(mine, ALL, swap)
    result = (own_embed.astype(F32) + back.astype(F32)).reshape(2, rows, wide)
    live = jnp.arange(rows, dtype=jnp.int32) < row_counts[0]
    return jnp.where(live[None, :, None], result, 0.0).astype(BF)


def solution(mesh):
    fine = Mesh(mesh.devices.reshape(8, 2, 4, 2, 2), ALL)
    return jax.shard_map(
        per_device,
        mesh=fine,
        in_specs=(
            P(None, GROUP),
            P(GROUP),
            P(None, TP),
            P(GROUP, TP),
            P(GROUP, TP),
            P(GROUP, TP),
            P(GROUP, TP),
            P(TP),
            P(TP),
            P(TP),
            P(TP),
            P(TP, GROUP),
            P(GROUP, TP, None, None),
        ),
        out_specs=P(None, GROUP, TP),
        check_vma=False,
    )
```

```python
import functools

import jax
import jax.numpy as jnp
from jax import lax
from jax.experimental import pallas as pl
from jax.experimental.pallas import tpu as pltpu
from jax.sharding import Mesh
from jax.sharding import PartitionSpec as P


BF = jnp.bfloat16
F32 = jnp.float32
SCALE = 2.0**-20
GROUP = ("z", "yl")
TP = ("x", "yh", "core")
ALL = GROUP + TP
VMEM_LIMIT = 14 * 1024 * 1024

FAR_FIRST = (4, 3, 5, 2, 6, 1, 7)


def nt(a, b):
    return lax.dot_general(a, b, (((1,), (1,)), ((), ())), preferred_element_type=F32)


def nn(a, b):
    return jnp.dot(a, b, preferred_element_type=F32)


def call(body, out_shape, args, in_smem=0, flops=1 << 20, grid=None, in_specs=None, out_specs=None, scratch=()):
    if in_specs is None:
        in_specs = [pl.BlockSpec(memory_space=pltpu.SMEM)] * in_smem + [
            pl.BlockSpec(memory_space=pltpu.VMEM)
        ] * (len(args) - in_smem)
        out_specs = jax.tree.map(lambda _: pl.BlockSpec(memory_space=pltpu.VMEM), out_shape)
    kwargs = {} if grid is None else {"grid": grid}
    return pl.pallas_call(
        body,
        out_shape=out_shape,
        in_specs=in_specs,
        out_specs=out_specs,
        scratch_shapes=scratch,
        compiler_params=pltpu.CompilerParams(vmem_limit_bytes=VMEM_LIMIT),
        cost_estimate=pl.CostEstimate(flops=flops, bytes_accessed=1 << 20, transcendentals=0),
        **kwargs,
    )(*args)


def split2(v):
    hi = v.astype(BF)
    return hi, (v - hi.astype(F32)).astype(BF)


def project_small_kernel(flag, e_own, e_oth, s_own, s_oth, out):
    groups, rows, width = out.shape

    def run(ea, eb):
        ps = nt(ea[...], s_own[...]) + nt(eb[...], s_oth[...])
        hi, lo = split2(ps)
        out[...] = jnp.concatenate([hi, lo], 1).reshape(groups, rows, width)

    @pl.when(flag[0] == 1)
    def _():
        run(e_own, e_oth)

    @pl.when(flag[0] == 0)
    def _():
        run(e_oth, e_own)


def project_kernel(place, e_own, e_oth, x_own, x_oth, z_own, z_oth, *outs):
    inner = x_own.shape[1]
    rows = outs[0].shape[0]
    groups = len(outs)

    def turned(ref):
        blocks = []
        for k in range(groups):
            at = lax.rem(place[1] + k, groups) * rows
            blocks.append(ref[pl.ds(pl.multiple_of(at, rows), rows), :])
        return jnp.concatenate(blocks, 0)

    def run(ea, eb):
        a = turned(ea)
        b = turned(eb)
        px = (nn(a, x_own[...]) + nn(b, x_oth[...])).astype(BF)
        for k in range(groups):
            outs[k][:, :inner] = px[k * rows : (k + 1) * rows]
        pz = (nn(a, z_own[...]) + nn(b, z_oth[...])).astype(BF)
        for k in range(groups):
            outs[k][:, inner:] = pz[k * rows : (k + 1) * rows]

    @pl.when(place[0] == 1)
    def _():
        run(e_own, e_oth)

    @pl.when(place[0] == 0)
    def _():
        run(e_oth, e_own)


def small_kernel(part, bc, small):
    total = part[0].astype(F32)
    for k in range(1, part.shape[0]):
        total = total + part[k].astype(F32)
    total = total[:, :64] + total[:, 64:]
    hi, lo = split2(total)
    both = jnp.concatenate([hi, lo], 1)
    for k in range(bc.shape[0]):
        bc[k] = both
    small[...] = total


def state_kernel(bc, s, out, dots, cmat):
    rows = cmat.shape[0]

    @pl.when(pl.program_id(0) == 0)
    def _():
        pieces = [bc[t] for t in range(bc.shape[0])]
        pieces = [p[:, :32].astype(F32) + p[:, 64:96].astype(F32) for p in pieces]
        b = jnp.concatenate(pieces[:8], 1)
        c = jnp.concatenate(pieces[8:], 1)
        b1, b2, c1, c2 = b[:rows], b[rows:], c[:rows], c[rows:]
        lane = lax.broadcasted_iota(jnp.int32, dots.shape, 1)
        b11 = jnp.sum(b1 * c1, axis=1, keepdims=True)
        b12 = jnp.sum(b1 * c2, axis=1, keepdims=True)
        b22 = jnp.sum(b2 * c2, axis=1, keepdims=True)
        dots[...] = jnp.where(lane == 0, b11, jnp.where(lane == 1, b12, b22))
        cmat[...] = jnp.zeros_like(cmat)
        for k, v in enumerate((c1, c2)):
            v = v * SCALE
            hi = v.astype(BF).astype(F32)
            cmat[:, 2 * k, :] = hi
            cmat[:, 2 * k + 1, :] = v - hi

    for r in range(s.shape[0]):
        m = s[r].reshape(s.shape[1] * s.shape[2], s.shape[3])
        g = nt(cmat[pl.program_id(0) * s.shape[0] + r].astype(BF), m)
        out[r] = g


def decode_kernel(*refs):
    parts, (small, dots, g, bias, rate, skip, gain, out) = refs[:8], refs[8:]
    heads = bias.shape[1]
    inner = gain.shape[1]
    half = parts[0].shape[0] // 2
    total = parts[0][...].astype(F32)
    for part in parts[1:]:
        total = total + part[...].astype(F32)
    x_pre = total[:, :inner]
    z_pre = total[:, inner:]
    pick = (
        lax.broadcasted_iota(jnp.int32, (heads, inner), 0)
        == lax.broadcasted_iota(jnp.int32, (heads, inner), 1) // (inner // heads)
    ).astype(F32)
    expand = functools.partial(
        jnp.dot, preferred_element_type=F32, precision=lax.Precision.HIGHEST
    )
    dt_pre = expand(small[:, 32 : 32 + heads], pick)
    bias_e = expand(bias[...], pick)
    rate_e = expand(rate[...], pick)
    skip_e = expand(skip[...], pick)
    pre = dt_pre + bias_e
    dt = jnp.maximum(pre, 0.0) + jnp.log1p(jnp.exp(-jnp.abs(pre)))
    decay = jnp.exp(-dt * rate_e)
    inputs = x_pre * jax.nn.sigmoid(x_pre)
    upd = dt * inputs
    gate = z_pre * jax.nn.sigmoid(z_pre)
    b11 = dots[:, 0:1]
    b12 = dots[:, 1:2]
    b22 = dots[:, 2:3]
    gs = g[...]
    g1 = gs[:, 0, :] + gs[:, 1, :]
    g2 = gs[:, 2, :] + gs[:, 3, :]
    d1, d2 = decay[:half], decay[half:]
    u1, u2 = upd[:half], upd[half:]
    read1 = (d1 * g1) * (1.0 / SCALE) + u1 * b11 + skip_e * inputs[:half]
    read2 = d2 * ((d1 * g2) * (1.0 / SCALE) + u1 * b12) + u2 * b22 + skip_e * inputs[half:]
    lim = 1e30
    gg1 = jnp.clip(read1 * gate[:half] * gain[...], -lim, lim)
    gg2 = jnp.clip(read2 * gate[half:] * gain[...], -lim, lim)
    out[...] = jnp.concatenate([gg1, gg2], 0).astype(BF)


def output_kernel(place, mine, other, gain, own, r1, l1, r2, l2, r3, l3, r4, keep, send):
    swapped = place[0]
    z = place[1]
    groups, rows, _ = keep.shape
    m = mine[...]
    o = other[...]
    v = jnp.concatenate([jnp.where(swapped == 0, m, o), jnp.where(swapped == 0, o, m)], 0)
    raw = v.astype(F32) / gain[...]
    ss = jnp.sum(raw * raw, axis=1, keepdims=True)
    hi = ss.astype(BF).astype(F32)
    lane = lax.broadcasted_iota(jnp.int32, (2 * rows, 64), 1)
    tail = jnp.where(lane == 0, hi, jnp.where(lane == 1, ss - hi, 0.0))
    order = ((0, own), (7, r1), (1, l1), (6, r2), (2, l2), (5, r3), (3, l3), (4, r4))
    for shift, w in order:
        block = jnp.concatenate([nt(v, w[...]), tail], 1)
        at = lax.rem(z + shift, groups)
        keep[at] = block[:rows]
        send[at] = block[rows:].astype(BF)


def pair_kernel(keep, got, out):
    total = keep[...] + got[...].astype(F32)
    cols = out.shape[2] - 64
    lane = lax.broadcasted_iota(jnp.int32, total.shape, 2)
    ss = total[:, :, cols : cols + 1] + total[:, :, cols + 1 : cols + 2]
    hi = ss.astype(BF).astype(F32)
    total = jnp.where(lane == cols, hi, jnp.where(lane == cols + 1, ss - hi, total))
    out[...] = total.astype(BF)


def reduce_kernel(part, out, *, count):
    total = part[0].astype(F32)
    for k in range(1, part.shape[0]):
        total = total + part[k].astype(F32)
    cols = out.shape[1]
    ss = total[:, cols : cols + 1] + total[:, cols + 1 : cols + 2]
    out[...] = (total[:, :cols] * lax.rsqrt(ss / count + 1e-05)).astype(BF)


def per_device(
    token_ids,
    row_counts,
    code_table,
    x_weight,
    z_weight,
    dt_weight,
    bc_weight,
    dt_bias,
    head_rate,
    skip_gain,
    norm_gain,
    out_weight,
    ssm_state,
):
    rows = token_ids.shape[1]
    heads = dt_bias.shape[0]
    inner = x_weight.shape[1]
    wide = code_table.shape[1]
    y = lax.axis_index("yl")
    core = lax.axis_index("core")
    swap = []
    for z in range(8):
        for yy in range(2):
            for w in range(8):
                for c in range(2):
                    swap.append(((z * 2 + yy) * 16 + w * 2 + c, (w * 2 + yy) * 16 + z * 2 + c))
    pair = [(0, 1), (1, 0)]

    gain = norm_gain.reshape(1, inner)
    right = [(i, (i + 1) % 8) for i in range(8)]
    left = [(i, (i + 7) % 8) for i in range(8)]
    out_own = out_weight.T
    ring_r = [out_own]
    ring_l = [out_own]
    for _ in range(1, 4):
        ring_r.append(lax.ppermute(ring_r[-1], "z", right))
        ring_l.append(lax.ppermute(ring_l[-1], "z", left))
    ring_r.append(lax.ppermute(ring_r[-1], "z", right))
    x_oth = lax.ppermute(x_weight, "yl", pair)
    z_oth = lax.ppermute(z_weight, "yl", pair)
    small_own = jnp.concatenate(
        [bc_weight.T, dt_weight.T, jnp.zeros((64 - 32 - heads, wide), BF)], 0
    )
    small_oth = lax.ppermute(small_own, "yl", pair)

    flat_ids = token_ids.reshape(-1)
    codes = jnp.arange(code_table.shape[0], dtype=jnp.int32)
    one_hot = (flat_ids[:, None] == codes[None, :]).astype(BF)
    own_embed = jnp.dot(one_hot, code_table, preferred_element_type=F32).astype(BF)
    moved = lax.ppermute(own_embed, ALL, swap)
    e_own = lax.all_to_all(
        jnp.broadcast_to(moved[None], (8,) + moved.shape), ("x", "yh"), 0, 0
    ).reshape(8 * 2 * rows, wide)
    e_oth = lax.ppermute(e_own, "core", pair)
    flag = (y == core).astype(jnp.int32).reshape(1)
    part_small = call(
        project_small_kernel,
        jax.ShapeDtypeStruct((8, 2 * rows, 128), BF),
        (flag, e_own, e_oth, small_own, small_oth),
        in_smem=1,
        flops=2 * 16 * rows * 2 * wide * 128,
    )
    part_small = lax.all_to_all(part_small, "z", 0, 0)
    blocks = call(
        project_kernel,
        tuple(jax.ShapeDtypeStruct((2 * rows, 2 * inner), BF) for _ in range(8)),
        (
            jnp.stack([(y == core).astype(jnp.int32), lax.axis_index("z")]),
            e_own,
            e_oth,
            x_weight,
            x_oth,
            z_weight,
            z_oth,
        ),
        in_smem=1,
        flops=2 * 16 * rows * 2 * wide * 2 * inner,
    )
    parts = [blocks[0]]
    for k in FAR_FIRST:
        parts.append(lax.ppermute(blocks[k], "z", [(i, (i + k) % 8) for i in range(8)]))
    bc, small = call(
        small_kernel,
        (jax.ShapeDtypeStruct((16, 2 * rows, 128), BF), jax.ShapeDtypeStruct((2 * rows, 64), F32)),
        (part_small,),
    )
    bc_all = lax.all_to_all(bc, TP, 0, 0)
    step = 4
    g, dots = call(
        state_kernel,
        (jax.ShapeDtypeStruct((rows, 8, inner), F32), jax.ShapeDtypeStruct((rows, 128), F32)),
        (bc_all, ssm_state),
        grid=(rows // step,),
        in_specs=[
            pl.BlockSpec(bc_all.shape, lambda i: (0, 0, 0)),
            pl.BlockSpec((step,) + ssm_state.shape[1:], lambda i: (i, 0, 0, 0)),
        ],
        out_specs=(
            pl.BlockSpec((step, 8, inner), lambda i: (i, 0, 0)),
            pl.BlockSpec((rows, 128), lambda i: (0, 0)),
        ),
        scratch=[pltpu.VMEM((rows, 8, 256), F32)],
        flops=2 * 8 * rows * inner * 256,
    )
    gg = call(
        decode_kernel,
        jax.ShapeDtypeStruct((2 * rows, inner), BF),
        (
            *parts,
            small,
            dots,
            g,
            dt_bias.reshape(1, heads),
            head_rate.reshape(1, heads),
            skip_gain.reshape(1, heads),
            gain,
        ),
    )
    gg_oth = lax.ppermute(gg, "yl", pair)
    keep, send = call(
        output_kernel,
        (
            jax.ShapeDtypeStruct((8, 2 * rows, wide + 64), F32),
            jax.ShapeDtypeStruct((8, 2 * rows, wide + 64), BF),
        ),
        (
            jnp.stack([(y != core).astype(jnp.int32), lax.axis_index("z")]),
            gg,
            gg_oth,
            gain,
            out_own,
            ring_r[1],
            ring_l[1],
            ring_r[2],
            ring_l[2],
            ring_r[3],
            ring_l[3],
            ring_r[4],
        ),
        in_smem=1,
        flops=2 * 4 * rows * inner * 8 * wide,
    )
    got = lax.ppermute(send, "core", pair)
    paired = call(pair_kernel, jax.ShapeDtypeStruct((8, 2 * rows, wide + 64), BF), (keep, got))
    partial_out = lax.all_to_all(paired, ("x", "yh"), 0, 0)
    mine = call(
        functools.partial(reduce_kernel, count=float(16 * inner)),
        jax.ShapeDtypeStruct((2 * rows, wide), BF),
        (partial_out,),
    )
    back = lax.ppermute(mine, ("yl", "core"), [(0, 0), (1, 2), (2, 1), (3, 3)])
    result = (own_embed.astype(F32) + back.astype(F32)).reshape(2, rows, wide)
    live = jnp.arange(rows, dtype=jnp.int32) < row_counts[0]
    return jnp.where(live[None, :, None], result, 0.0).astype(BF)


def solution(mesh):
    fine = Mesh(mesh.devices.reshape(8, 2, 4, 2, 2), ALL)
    return jax.shard_map(
        per_device,
        mesh=fine,
        in_specs=(
            P(None, GROUP),
            P(GROUP),
            P(None, TP),
            P(GROUP, TP),
            P(GROUP, TP),
            P(GROUP, TP),
            P(GROUP, TP),
            P(TP),
            P(TP),
            P(TP),
            P(TP),
            P(TP, GROUP),
            P(GROUP, TP, None, None),
        ),
        out_specs=P(None, GROUP, TP),
        check_vma=False,
    )
```

```python
import functools

import jax
import jax.numpy as jnp
from jax import lax
from jax.experimental import pallas as pl
from jax.experimental.pallas import tpu as pltpu
from jax.sharding import Mesh
from jax.sharding import PartitionSpec as P


BF = jnp.bfloat16
F32 = jnp.float32
SCALE = 2.0**-20
GROUP = ("z", "yl")
TP = ("x", "yh", "core")
ALL = GROUP + TP
VMEM_LIMIT = 14 * 1024 * 1024
PROJECT_LIMIT = 58 * 1024 * 1024
STATE_LIMIT = 52 * 1024 * 1024

FAR_FIRST = (4, 3, 5, 2, 6, 1, 7)


def nt(a, b):
    return lax.dot_general(a, b, (((1,), (1,)), ((), ())), preferred_element_type=F32)


def nn(a, b):
    return jnp.dot(a, b, preferred_element_type=F32)


def call(body, out_shape, args, in_smem=0, flops=1 << 20, grid=None, in_specs=None, out_specs=None, scratch=(), limit=VMEM_LIMIT):
    if in_specs is None:
        in_specs = [pl.BlockSpec(memory_space=pltpu.SMEM)] * in_smem + [
            pl.BlockSpec(memory_space=pltpu.VMEM)
        ] * (len(args) - in_smem)
        out_specs = jax.tree.map(lambda _: pl.BlockSpec(memory_space=pltpu.VMEM), out_shape)
    kwargs = {} if grid is None else {"grid": grid}
    return pl.pallas_call(
        body,
        out_shape=out_shape,
        in_specs=in_specs,
        out_specs=out_specs,
        scratch_shapes=scratch,
        compiler_params=pltpu.CompilerParams(vmem_limit_bytes=limit),
        cost_estimate=pl.CostEstimate(flops=flops, bytes_accessed=1 << 20, transcendentals=0),
        **kwargs,
    )(*args)


def split2(v):
    hi = v.astype(BF)
    return hi, (v - hi.astype(F32)).astype(BF)


def project_small_kernel(flag, e_own, e_oth, s_own, s_oth, out):
    groups, rows, width = out.shape

    def run(ea, eb):
        ps = nt(ea[...], s_own[...]) + nt(eb[...], s_oth[...])
        hi, lo = split2(ps)
        out[...] = jnp.concatenate([hi, lo], 1).reshape(groups, rows, width)

    @pl.when(flag[0] == 1)
    def _():
        run(e_own, e_oth)

    @pl.when(flag[0] == 0)
    def _():
        run(e_oth, e_own)


def project_kernel(place, e_own, e_oth, *refs):
    outs, held, sems = refs[4:12], refs[12:16], refs[16]
    x_own, x_oth, z_own, z_oth = held
    inner = x_own.shape[1]
    copies = [
        pltpu.make_async_copy(refs[k], held[k], sems.at[k]) for k in range(4)
    ]
    for copy in copies:
        copy.start()
    rows = outs[0].shape[0]
    groups = len(outs)

    def turned(ref):
        blocks = []
        for k in range(groups):
            at = lax.rem(place[1] + k, groups) * rows
            blocks.append(ref[pl.ds(pl.multiple_of(at, rows), rows), :])
        return jnp.concatenate(blocks, 0)

    def run(ea, eb):
        a = turned(ea)
        b = turned(eb)
        copies[0].wait()
        copies[1].wait()
        px = (nn(a, x_own[...]) + nn(b, x_oth[...])).astype(BF)
        for k in range(groups):
            outs[k][:, :inner] = px[k * rows : (k + 1) * rows]
        copies[2].wait()
        copies[3].wait()
        pz = (nn(a, z_own[...]) + nn(b, z_oth[...])).astype(BF)
        for k in range(groups):
            outs[k][:, inner:] = pz[k * rows : (k + 1) * rows]

    @pl.when(place[0] == 1)
    def _():
        run(e_own, e_oth)

    @pl.when(place[0] == 0)
    def _():
        run(e_oth, e_own)


def small_kernel(part, bc, small):
    total = part[0].astype(F32)
    for k in range(1, part.shape[0]):
        total = total + part[k].astype(F32)
    total = total[:, :64] + total[:, 64:]
    hi, lo = split2(total)
    both = jnp.concatenate([hi, lo], 1)
    for k in range(bc.shape[0]):
        bc[k] = both
    small[...] = total


def state_kernel(bc, s, out, dots, cmat, held, sems):
    rows = cmat.shape[0]
    chunks = sems.shape[0]
    step = rows // chunks
    copies = [
        pltpu.make_async_copy(
            s.at[pl.ds(k * step, step)], held.at[pl.ds(k * step, step)], sems.at[k]
        )
        for k in range(chunks)
    ]
    for copy in copies:
        copy.start()
    pieces = [bc[t] for t in range(bc.shape[0])]
    pieces = [p[:, :32].astype(F32) + p[:, 64:96].astype(F32) for p in pieces]
    b = jnp.concatenate(pieces[:8], 1)
    c = jnp.concatenate(pieces[8:], 1)
    b1, b2, c1, c2 = b[:rows], b[rows:], c[:rows], c[rows:]
    lane = lax.broadcasted_iota(jnp.int32, dots.shape, 1)
    b11 = jnp.sum(b1 * c1, axis=1, keepdims=True)
    b12 = jnp.sum(b1 * c2, axis=1, keepdims=True)
    b22 = jnp.sum(b2 * c2, axis=1, keepdims=True)
    dots[...] = jnp.where(lane == 0, b11, jnp.where(lane == 1, b12, b22))
    cmat[...] = jnp.zeros_like(cmat)
    for k, v in enumerate((c1, c2)):
        v = v * SCALE
        hi = v.astype(BF).astype(F32)
        cmat[:, 2 * k, :] = hi
        cmat[:, 2 * k + 1, :] = v - hi
    for k in range(chunks):
        copies[k].wait()
        for r in range(k * step, (k + 1) * step):
            m = held[r].reshape(s.shape[1] * s.shape[2], s.shape[3])
            out[r] = nt(cmat[r].astype(BF), m)


def decode_kernel(*refs):
    parts, (small, dots, g, bias, rate, skip, gain, out) = refs[:8], refs[8:]
    heads = bias.shape[1]
    inner = gain.shape[1]
    half = parts[0].shape[0] // 2
    total = parts[0][...].astype(F32)
    for part in parts[1:]:
        total = total + part[...].astype(F32)
    x_pre = total[:, :inner]
    z_pre = total[:, inner:]
    pick = (
        lax.broadcasted_iota(jnp.int32, (heads, inner), 0)
        == lax.broadcasted_iota(jnp.int32, (heads, inner), 1) // (inner // heads)
    ).astype(F32)
    expand = functools.partial(
        jnp.dot, preferred_element_type=F32, precision=lax.Precision.HIGHEST
    )
    dt_pre = expand(small[:, 32 : 32 + heads], pick)
    bias_e = expand(bias[...], pick)
    rate_e = expand(rate[...], pick)
    skip_e = expand(skip[...], pick)
    pre = dt_pre + bias_e
    dt = jnp.maximum(pre, 0.0) + jnp.log1p(jnp.exp(-jnp.abs(pre)))
    decay = jnp.exp(-dt * rate_e)
    inputs = x_pre * jax.nn.sigmoid(x_pre)
    upd = dt * inputs
    gate = z_pre * jax.nn.sigmoid(z_pre)
    b11 = dots[:, 0:1]
    b12 = dots[:, 1:2]
    b22 = dots[:, 2:3]
    gs = g[...]
    g1 = gs[:, 0, :] + gs[:, 1, :]
    g2 = gs[:, 2, :] + gs[:, 3, :]
    d1, d2 = decay[:half], decay[half:]
    u1, u2 = upd[:half], upd[half:]
    read1 = (d1 * g1) * (1.0 / SCALE) + u1 * b11 + skip_e * inputs[:half]
    read2 = d2 * ((d1 * g2) * (1.0 / SCALE) + u1 * b12) + u2 * b22 + skip_e * inputs[half:]
    lim = 1e30
    gg1 = jnp.clip(read1 * gate[:half] * gain[...], -lim, lim)
    gg2 = jnp.clip(read2 * gate[half:] * gain[...], -lim, lim)
    out[...] = jnp.concatenate([gg1, gg2], 0).astype(BF)


def output_kernel(place, mine, other, gain, own, r1, l1, r2, l2, r3, l3, r4, keep, send):
    same = place[0]
    z = place[1]
    groups, rows, _ = keep.shape
    m = mine[...]
    o = other[...]
    v = jnp.concatenate([jnp.where(same == 1, m, o), jnp.where(same == 1, o, m)], 0)
    raw = v.astype(F32) / gain[...]
    ss = jnp.sum(raw * raw, axis=1, keepdims=True)
    hi = ss.astype(BF).astype(F32)
    lane = lax.broadcasted_iota(jnp.int32, (2 * rows, 64), 1)
    tail = jnp.where(lane == 0, hi, jnp.where(lane == 1, ss - hi, 0.0))
    order = ((0, own), (7, r1), (1, l1), (6, r2), (2, l2), (5, r3), (3, l3), (4, r4))
    for shift, w in order:
        block = jnp.concatenate([nt(v, w[...]), tail], 1)
        at = lax.rem(z + shift, groups)
        keep[at] = block[:rows]
        send[at] = block[rows:].astype(BF)


def pair_kernel(keep, got, out):
    total = keep[...] + got[...].astype(F32)
    cols = out.shape[2] - 64
    lane = lax.broadcasted_iota(jnp.int32, total.shape, 2)
    ss = total[:, :, cols : cols + 1] + total[:, :, cols + 1 : cols + 2]
    hi = ss.astype(BF).astype(F32)
    total = jnp.where(lane == cols, hi, jnp.where(lane == cols + 1, ss - hi, total))
    out[...] = total.astype(BF)


def reduce_kernel(part, out, *, count):
    total = part[0].astype(F32)
    for k in range(1, part.shape[0]):
        total = total + part[k].astype(F32)
    cols = out.shape[1]
    ss = total[:, cols : cols + 1] + total[:, cols + 1 : cols + 2]
    out[...] = (total[:, :cols] * lax.rsqrt(ss / count + 1e-05)).astype(BF)


def per_device(
    token_ids,
    row_counts,
    code_table,
    x_weight,
    z_weight,
    dt_weight,
    bc_weight,
    dt_bias,
    head_rate,
    skip_gain,
    norm_gain,
    out_weight,
    ssm_state,
):
    rows = token_ids.shape[1]
    heads = dt_bias.shape[0]
    inner = x_weight.shape[1]
    wide = code_table.shape[1]
    y = lax.axis_index("yl")
    core = lax.axis_index("core")
    swap = []
    for z in range(8):
        for yy in range(2):
            for w in range(8):
                for c in range(2):
                    swap.append(((z * 2 + yy) * 16 + w * 2 + c, (w * 2 + yy) * 16 + z * 2 + c))
    pair = [(0, 1), (1, 0)]

    gain = norm_gain.reshape(1, inner)
    right = [(i, (i + 1) % 8) for i in range(8)]
    left = [(i, (i + 7) % 8) for i in range(8)]
    out_own = out_weight.T
    ring_r = [out_own]
    ring_l = [out_own]
    for _ in range(1, 4):
        ring_r.append(lax.ppermute(ring_r[-1], "z", right))
        ring_l.append(lax.ppermute(ring_l[-1], "z", left))
    ring_r.append(lax.ppermute(ring_r[-1], "z", right))
    x_oth = lax.ppermute(x_weight, "yl", pair)
    z_oth = lax.ppermute(z_weight, "yl", pair)
    small_own = jnp.concatenate(
        [bc_weight.T, dt_weight.T, jnp.zeros((64 - 32 - heads, wide), BF)], 0
    )
    small_oth = lax.ppermute(small_own, "yl", pair)

    flat_ids = token_ids.reshape(-1)
    codes = jnp.arange(code_table.shape[0], dtype=jnp.int32)
    one_hot = (flat_ids[:, None] == codes[None, :]).astype(BF)
    own_embed = jnp.dot(one_hot, code_table, preferred_element_type=F32).astype(BF)
    moved = lax.ppermute(own_embed, ALL, swap)
    e_own = lax.all_to_all(
        jnp.broadcast_to(moved[None], (8,) + moved.shape), ("x", "yh"), 0, 0
    ).reshape(8 * 2 * rows, wide)
    e_oth = lax.ppermute(e_own, "core", pair)
    place = jnp.stack([(y == core).astype(jnp.int32), lax.axis_index("z")])
    part_small = call(
        project_small_kernel,
        jax.ShapeDtypeStruct((8, 2 * rows, 128), BF),
        (place, e_own, e_oth, small_own, small_oth),
        in_smem=1,
        flops=2 * 16 * rows * 2 * wide * 128,
    )
    part_small = lax.all_to_all(part_small, "z", 0, 0)
    blocks = call(
        project_kernel,
        tuple(jax.ShapeDtypeStruct((2 * rows, 2 * inner), BF) for _ in range(8)),
        (
            place,
            e_own,
            e_oth,
            x_weight,
            x_oth,
            z_weight,
            z_oth,
        ),
        in_specs=[pl.BlockSpec(memory_space=pltpu.SMEM)]
        + [pl.BlockSpec(memory_space=pltpu.VMEM)] * 2
        + [pl.BlockSpec(memory_space=pltpu.HBM)] * 4,
        out_specs=tuple(pl.BlockSpec(memory_space=pltpu.VMEM) for _ in range(8)),
        scratch=[pltpu.VMEM((wide, inner), BF)] * 4 + [pltpu.SemaphoreType.DMA((4,))],
        limit=PROJECT_LIMIT,
        flops=2 * 16 * rows * 2 * wide * 2 * inner,
    )
    parts = [blocks[0]]
    for k in FAR_FIRST:
        parts.append(lax.ppermute(blocks[k], "z", [(i, (i + k) % 8) for i in range(8)]))
    bc, small = call(
        small_kernel,
        (jax.ShapeDtypeStruct((16, 2 * rows, 128), BF), jax.ShapeDtypeStruct((2 * rows, 64), F32)),
        (part_small,),
    )
    bc_all = lax.all_to_all(bc, TP, 0, 0)
    g, dots = call(
        state_kernel,
        (jax.ShapeDtypeStruct((rows, 8, inner), F32), jax.ShapeDtypeStruct((rows, 128), F32)),
        (bc_all, ssm_state),
        in_specs=[
            pl.BlockSpec(memory_space=pltpu.VMEM),
            pl.BlockSpec(memory_space=pl.ANY),
        ],
        out_specs=(pl.BlockSpec(memory_space=pltpu.VMEM), pl.BlockSpec(memory_space=pltpu.VMEM)),
        scratch=[
            pltpu.VMEM((rows, 8, 256), F32),
            pltpu.VMEM(ssm_state.shape, BF),
            pltpu.SemaphoreType.DMA((8,)),
        ],
        limit=STATE_LIMIT,
        flops=2 * 8 * rows * inner * 256,
    )
    gg = call(
        decode_kernel,
        jax.ShapeDtypeStruct((2 * rows, inner), BF),
        (
            *parts,
            small,
            dots,
            g,
            dt_bias.reshape(1, heads),
            head_rate.reshape(1, heads),
            skip_gain.reshape(1, heads),
            gain,
        ),
    )
    gg_oth = lax.ppermute(gg, "yl", pair)
    keep, send = call(
        output_kernel,
        (
            jax.ShapeDtypeStruct((8, 2 * rows, wide + 64), F32),
            jax.ShapeDtypeStruct((8, 2 * rows, wide + 64), BF),
        ),
        (
            place,
            gg,
            gg_oth,
            gain,
            out_own,
            ring_r[1],
            ring_l[1],
            ring_r[2],
            ring_l[2],
            ring_r[3],
            ring_l[3],
            ring_r[4],
        ),
        in_smem=1,
        flops=2 * 4 * rows * inner * 8 * wide,
    )
    got = lax.ppermute(send, "core", pair)
    paired = call(pair_kernel, jax.ShapeDtypeStruct((8, 2 * rows, wide + 64), BF), (keep, got))
    partial_out = lax.all_to_all(paired, ("x", "yh"), 0, 0)
    mine = call(
        functools.partial(reduce_kernel, count=float(16 * inner)),
        jax.ShapeDtypeStruct((2 * rows, wide), BF),
        (partial_out,),
    )
    back = lax.ppermute(mine, ("yl", "core"), [(0, 0), (1, 2), (2, 1), (3, 3)])
    result = (own_embed.astype(F32) + back.astype(F32)).reshape(2, rows, wide)
    live = jnp.arange(rows, dtype=jnp.int32) < row_counts[0]
    return jnp.where(live[None, :, None], result, 0.0).astype(BF)


def solution(mesh):
    fine = Mesh(mesh.devices.reshape(8, 2, 4, 2, 2), ALL)
    return jax.shard_map(
        per_device,
        mesh=fine,
        in_specs=(
            P(None, GROUP),
            P(GROUP),
            P(None, TP),
            P(GROUP, TP),
            P(GROUP, TP),
            P(GROUP, TP),
            P(GROUP, TP),
            P(TP),
            P(TP),
            P(TP),
            P(TP),
            P(TP, GROUP),
            P(GROUP, TP, None, None),
        ),
        out_specs=P(None, GROUP, TP),
        check_vma=False,
    )
```

```python
import functools

import jax
import jax.numpy as jnp
from jax import lax
from jax.experimental import pallas as pl
from jax.experimental.pallas import tpu as pltpu
from jax.sharding import Mesh
from jax.sharding import PartitionSpec as P


BF = jnp.bfloat16
F32 = jnp.float32
SCALE = 2.0**-20
GROUP = ("z", "yl")
TP = ("x", "yh", "core")
ALL = GROUP + TP
VMEM_LIMIT = 14 * 1024 * 1024
PROJECT_LIMIT = 58 * 1024 * 1024
STATE_LIMIT = 52 * 1024 * 1024


def nt(a, b):
    return lax.dot_general(a, b, (((1,), (1,)), ((), ())), preferred_element_type=F32)


def nn(a, b):
    return jnp.dot(a, b, preferred_element_type=F32)


def call(body, out_shape, args, in_smem=0, flops=1 << 20, grid=None, in_specs=None, out_specs=None, scratch=(), limit=VMEM_LIMIT):
    if in_specs is None:
        in_specs = [pl.BlockSpec(memory_space=pltpu.SMEM)] * in_smem + [
            pl.BlockSpec(memory_space=pltpu.VMEM)
        ] * (len(args) - in_smem)
        out_specs = jax.tree.map(lambda _: pl.BlockSpec(memory_space=pltpu.VMEM), out_shape)
    kwargs = {} if grid is None else {"grid": grid}
    return pl.pallas_call(
        body,
        out_shape=out_shape,
        in_specs=in_specs,
        out_specs=out_specs,
        scratch_shapes=scratch,
        compiler_params=pltpu.CompilerParams(vmem_limit_bytes=limit),
        cost_estimate=pl.CostEstimate(flops=flops, bytes_accessed=1 << 20, transcendentals=0),
        **kwargs,
    )(*args)


def split2(v):
    hi = v.astype(BF)
    return hi, (v - hi.astype(F32)).astype(BF)


def project_small_kernel(flag, e_own, e_oth, s_own, s_oth, out):
    groups, rows, width = out.shape

    def run(ea, eb):
        ps = nt(ea[...], s_own[...]) + nt(eb[...], s_oth[...])
        hi, lo = split2(ps)
        out[...] = jnp.concatenate([hi, lo], 1).reshape(groups, rows, width)

    @pl.when(flag[0] == 1)
    def _():
        run(e_own, e_oth)

    @pl.when(flag[0] == 0)
    def _():
        run(e_oth, e_own)


def project_kernel(place, e_own, e_oth, *refs):
    out, held, sems = refs[4], refs[5:9], refs[9]
    x_own, x_oth, z_own, z_oth = held
    inner = x_own.shape[1]
    groups, rows = out.shape[:2]
    copies = [pltpu.make_async_copy(refs[k], held[k], sems.at[k]) for k in range(4)]
    for copy in copies:
        copy.start()

    def run(ea, eb):
        a = ea[...]
        b = eb[...]
        copies[0].wait()
        copies[1].wait()
        px = (nn(a, x_own[...]) + nn(b, x_oth[...])).astype(BF)
        out[:, :, :inner] = px.reshape(groups, rows, inner)
        copies[2].wait()
        copies[3].wait()
        pz = (nn(a, z_own[...]) + nn(b, z_oth[...])).astype(BF)
        out[:, :, inner:] = pz.reshape(groups, rows, inner)

    @pl.when(place[0] == 1)
    def _():
        run(e_own, e_oth)

    @pl.when(place[0] == 0)
    def _():
        run(e_oth, e_own)


def small_kernel(part, bc, small):
    total = part[0].astype(F32)
    for k in range(1, part.shape[0]):
        total = total + part[k].astype(F32)
    total = total[:, :64] + total[:, 64:]
    hi, lo = split2(total)
    bc[...] = jnp.concatenate([hi, lo], 1)
    small[...] = total


def state_kernel(place, bc0, bc1, bc2, bc3, s, out, dots, cmat, pieces_ref, held, sems):
    rows = cmat.shape[0]
    chunks = sems.shape[0]
    step = rows // chunks
    copies = [
        pltpu.make_async_copy(
            s.at[pl.ds(k * step, step)], held.at[pl.ds(k * step, step)], sems.at[k]
        )
        for k in range(chunks)
    ]
    for copy in copies:
        copy.start()
    for shift, bc in ((0, bc0), (1, bc1), (2, bc2), (3, bc3)):
        x = lax.rem(place[2] + shift, 4)
        for k in range(4):
            yh = lax.rem(place[3] + k // 2, 2)
            core = lax.rem(place[4] + k % 2, 2)
            pieces_ref[(x * 2 + yh) * 2 + core] = bc[k]
    pieces = [pieces_ref[t] for t in range(16)]
    pieces = [p[:, :32].astype(F32) + p[:, 64:96].astype(F32) for p in pieces]
    b = jnp.concatenate(pieces[:8], 1)
    c = jnp.concatenate(pieces[8:], 1)
    b1, b2, c1, c2 = b[:rows], b[rows:], c[:rows], c[rows:]
    lane = lax.broadcasted_iota(jnp.int32, dots.shape, 1)
    b11 = jnp.sum(b1 * c1, axis=1, keepdims=True)
    b12 = jnp.sum(b1 * c2, axis=1, keepdims=True)
    b22 = jnp.sum(b2 * c2, axis=1, keepdims=True)
    dots[...] = jnp.where(lane == 0, b11, jnp.where(lane == 1, b12, b22))
    cmat[...] = jnp.zeros_like(cmat)
    for k, v in enumerate((c1, c2)):
        v = v * SCALE
        hi = v.astype(BF).astype(F32)
        cmat[:, 2 * k, :] = hi
        cmat[:, 2 * k + 1, :] = v - hi
    for k in range(chunks):
        copies[k].wait()
        for r in range(k * step, (k + 1) * step):
            m = held[r].reshape(s.shape[1] * s.shape[2], s.shape[3])
            out[r] = nt(cmat[r].astype(BF), m)


def decode_kernel(part, small, dots, g, bias, rate, skip, gain, out):
    heads = bias.shape[1]
    inner = gain.shape[1]
    half = part.shape[1] // 2
    total = part[0].astype(F32)
    for k in range(1, part.shape[0]):
        total = total + part[k].astype(F32)
    x_pre = total[:, :inner]
    z_pre = total[:, inner:]
    pick = (
        lax.broadcasted_iota(jnp.int32, (heads, inner), 0)
        == lax.broadcasted_iota(jnp.int32, (heads, inner), 1) // (inner // heads)
    ).astype(F32)
    expand = functools.partial(
        jnp.dot, preferred_element_type=F32, precision=lax.Precision.HIGHEST
    )
    dt_pre = expand(small[:, 32 : 32 + heads], pick)
    bias_e = expand(bias[...], pick)
    rate_e = expand(rate[...], pick)
    skip_e = expand(skip[...], pick)
    pre = dt_pre + bias_e
    dt = jnp.maximum(pre, 0.0) + jnp.log1p(jnp.exp(-jnp.abs(pre)))
    decay = jnp.exp(-dt * rate_e)
    inputs = x_pre * jax.nn.sigmoid(x_pre)
    upd = dt * inputs
    gate = z_pre * jax.nn.sigmoid(z_pre)
    b11 = dots[:, 0:1]
    b12 = dots[:, 1:2]
    b22 = dots[:, 2:3]
    gs = g[...]
    g1 = gs[:, 0, :] + gs[:, 1, :]
    g2 = gs[:, 2, :] + gs[:, 3, :]
    d1, d2 = decay[:half], decay[half:]
    u1, u2 = upd[:half], upd[half:]
    read1 = (d1 * g1) * (1.0 / SCALE) + u1 * b11 + skip_e * inputs[:half]
    read2 = d2 * ((d1 * g2) * (1.0 / SCALE) + u1 * b12) + u2 * b22 + skip_e * inputs[half:]
    lim = 1e30
    gg1 = jnp.clip(read1 * gate[:half] * gain[...], -lim, lim)
    gg2 = jnp.clip(read2 * gate[half:] * gain[...], -lim, lim)
    out[...] = jnp.concatenate([gg1, gg2], 0).astype(BF)


def output_kernel(place, mine, other, gain, own, r1, l1, r2, l2, r3, l3, r4, keep, send):
    same = place[0]
    z = place[1]
    groups, rows, _ = keep.shape
    m = mine[...]
    o = other[...]
    v = jnp.concatenate([jnp.where(same == 1, m, o), jnp.where(same == 1, o, m)], 0)
    raw = v.astype(F32) / gain[...]
    ss = jnp.sum(raw * raw, axis=1, keepdims=True)
    hi = ss.astype(BF).astype(F32)
    lane = lax.broadcasted_iota(jnp.int32, (2 * rows, 64), 1)
    tail = jnp.where(lane == 0, hi, jnp.where(lane == 1, ss - hi, 0.0))
    order = ((0, own), (7, r1), (1, l1), (6, r2), (2, l2), (5, r3), (3, l3), (4, r4))
    for shift, w in order:
        block = jnp.concatenate([nt(v, w[...]), tail], 1)
        at = lax.rem(z + shift, groups)
        keep[at] = block[:rows]
        send[at] = block[rows:].astype(BF)


def pair_kernel(keep, got, out):
    total = keep[...] + got[...].astype(F32)
    cols = out.shape[2] - 64
    lane = lax.broadcasted_iota(jnp.int32, total.shape, 2)
    ss = total[:, :, cols : cols + 1] + total[:, :, cols + 1 : cols + 2]
    hi = ss.astype(BF).astype(F32)
    total = jnp.where(lane == cols, hi, jnp.where(lane == cols + 1, ss - hi, total))
    out[...] = total.astype(BF)


def reduce_kernel(part, out, *, count):
    total = part[0].astype(F32)
    for k in range(1, part.shape[0]):
        total = total + part[k].astype(F32)
    cols = out.shape[1]
    ss = total[:, cols : cols + 1] + total[:, cols + 1 : cols + 2]
    out[...] = (total[:, :cols] * lax.rsqrt(ss / count + 1e-05)).astype(BF)


def per_device(
    token_ids,
    row_counts,
    code_table,
    x_weight,
    z_weight,
    dt_weight,
    bc_weight,
    dt_bias,
    head_rate,
    skip_gain,
    norm_gain,
    out_weight,
    ssm_state,
):
    rows = token_ids.shape[1]
    heads = dt_bias.shape[0]
    inner = x_weight.shape[1]
    wide = code_table.shape[1]
    y = lax.axis_index("yl")
    core = lax.axis_index("core")
    swap = []
    for z in range(8):
        for yy in range(2):
            for w in range(8):
                for c in range(2):
                    swap.append(((z * 2 + yy) * 16 + w * 2 + c, (w * 2 + yy) * 16 + z * 2 + c))
    pair = [(0, 1), (1, 0)]

    gain = norm_gain.reshape(1, inner)
    right = [(i, (i + 1) % 8) for i in range(8)]
    left = [(i, (i + 7) % 8) for i in range(8)]
    out_own = out_weight.T
    ring_r = [out_own]
    ring_l = [out_own]
    for _ in range(1, 4):
        ring_r.append(lax.ppermute(ring_r[-1], "z", right))
        ring_l.append(lax.ppermute(ring_l[-1], "z", left))
    ring_r.append(lax.ppermute(ring_r[-1], "z", right))
    x_oth = lax.ppermute(x_weight, "yl", pair)
    z_oth = lax.ppermute(z_weight, "yl", pair)
    small_own = jnp.concatenate(
        [bc_weight.T, dt_weight.T, jnp.zeros((64 - 32 - heads, wide), BF)], 0
    )
    small_oth = lax.ppermute(small_own, "yl", pair)

    flat_ids = token_ids.reshape(-1)
    codes = jnp.arange(code_table.shape[0], dtype=jnp.int32)
    one_hot = (flat_ids[:, None] == codes[None, :]).astype(BF)
    own_embed = jnp.dot(one_hot, code_table, preferred_element_type=F32).astype(BF)
    moved = lax.ppermute(own_embed, ALL, swap)
    e_own = lax.all_to_all(
        jnp.broadcast_to(moved[None], (8,) + moved.shape), ("x", "yh"), 0, 0
    ).reshape(8 * 2 * rows, wide)
    e_oth = lax.ppermute(e_own, "core", pair)
    place = jnp.stack(
        [(y == core).astype(jnp.int32), lax.axis_index("z"), lax.axis_index("x"), lax.axis_index("yh"), core]
    )
    part_small = call(
        project_small_kernel,
        jax.ShapeDtypeStruct((8, 2 * rows, 128), BF),
        (place, e_own, e_oth, small_own, small_oth),
        in_smem=1,
        flops=2 * 16 * rows * 2 * wide * 128,
    )
    part_small = lax.all_to_all(part_small, "z", 0, 0)
    part = call(
        project_kernel,
        jax.ShapeDtypeStruct((8, 2 * rows, 2 * inner), BF),
        (place, e_own, e_oth, x_weight, x_oth, z_weight, z_oth),
        in_specs=[pl.BlockSpec(memory_space=pltpu.SMEM)]
        + [pl.BlockSpec(memory_space=pltpu.VMEM)] * 2
        + [pl.BlockSpec(memory_space=pl.ANY)] * 4,
        out_specs=pl.BlockSpec(memory_space=pltpu.VMEM),
        scratch=[pltpu.VMEM((wide, inner), BF)] * 4 + [pltpu.SemaphoreType.DMA((4,))],
        limit=PROJECT_LIMIT,
        flops=2 * 16 * rows * 2 * wide * 2 * inner,
    )
    part = lax.all_to_all(part, "z", 0, 0)
    bc, small = call(
        small_kernel,
        (jax.ShapeDtypeStruct((2 * rows, 128), BF), jax.ShapeDtypeStruct((2 * rows, 64), F32)),
        (part_small,),
    )
    bc2 = jnp.stack([bc, lax.ppermute(bc, "core", pair)])
    bc4 = jnp.concatenate([bc2, lax.ppermute(bc2, "yh", pair)], 0)
    bc_all = [bc4]
    for k in (1, 2, 3):
        bc_all.append(lax.ppermute(bc4, "x", [((i + k) % 4, i) for i in range(4)]))
    g, dots = call(
        state_kernel,
        (jax.ShapeDtypeStruct((rows, 8, inner), F32), jax.ShapeDtypeStruct((rows, 128), F32)),
        (place, *bc_all, ssm_state),
        in_specs=[pl.BlockSpec(memory_space=pltpu.SMEM)]
        + [pl.BlockSpec(memory_space=pltpu.VMEM)] * 4
        + [pl.BlockSpec(memory_space=pl.ANY)],
        out_specs=(pl.BlockSpec(memory_space=pltpu.VMEM), pl.BlockSpec(memory_space=pltpu.VMEM)),
        scratch=[
            pltpu.VMEM((rows, 8, 256), F32),
            pltpu.VMEM((16, 2 * rows, 128), BF),
            pltpu.VMEM(ssm_state.shape, BF),
            pltpu.SemaphoreType.DMA((8,)),
        ],
        limit=STATE_LIMIT,
        flops=2 * 8 * rows * inner * 256,
    )
    gg = call(
        decode_kernel,
        jax.ShapeDtypeStruct((2 * rows, inner), BF),
        (
            part,
            small,
            dots,
            g,
            dt_bias.reshape(1, heads),
            head_rate.reshape(1, heads),
            skip_gain.reshape(1, heads),
            gain,
        ),
    )
    gg_oth = lax.ppermute(gg, "yl", pair)
    keep, send = call(
        output_kernel,
        (
            jax.ShapeDtypeStruct((8, 2 * rows, wide + 64), F32),
            jax.ShapeDtypeStruct((8, 2 * rows, wide + 64), BF),
        ),
        (
            place,
            gg,
            gg_oth,
            gain,
            out_own,
            ring_r[1],
            ring_l[1],
            ring_r[2],
            ring_l[2],
            ring_r[3],
            ring_l[3],
            ring_r[4],
        ),
        in_smem=1,
        flops=2 * 4 * rows * inner * 8 * wide,
    )
    got = lax.ppermute(send, "core", pair)
    paired = call(pair_kernel, jax.ShapeDtypeStruct((8, 2 * rows, wide + 64), BF), (keep, got))
    partial_out = lax.all_to_all(paired, ("x", "yh"), 0, 0)
    mine = call(
        functools.partial(reduce_kernel, count=float(16 * inner)),
        jax.ShapeDtypeStruct((2 * rows, wide), BF),
        (partial_out,),
    )
    back = lax.ppermute(mine, ("yl", "core"), [(0, 0), (1, 2), (2, 1), (3, 3)])
    result = (own_embed.astype(F32) + back.astype(F32)).reshape(2, rows, wide)
    live = jnp.arange(rows, dtype=jnp.int32) < row_counts[0]
    return jnp.where(live[None, :, None], result, 0.0).astype(BF)


def solution(mesh):
    fine = Mesh(mesh.devices.reshape(8, 2, 4, 2, 2), ALL)
    return jax.shard_map(
        per_device,
        mesh=fine,
        in_specs=(
            P(None, GROUP),
            P(GROUP),
            P(None, TP),
            P(GROUP, TP),
            P(GROUP, TP),
            P(GROUP, TP),
            P(GROUP, TP),
            P(TP),
            P(TP),
            P(TP),
            P(TP),
            P(TP, GROUP),
            P(GROUP, TP, None, None),
        ),
        out_specs=P(None, GROUP, TP),
        check_vma=False,
    )
```

```python
import functools

import jax
import jax.numpy as jnp
from jax import lax
from jax.experimental import pallas as pl
from jax.experimental.pallas import tpu as pltpu
from jax.sharding import Mesh
from jax.sharding import PartitionSpec as P


BF = jnp.bfloat16
F32 = jnp.float32
SCALE = 2.0**-20
GROUP = ("z", "yl")
TP = ("x", "yh", "core")
ALL = GROUP + TP
VMEM_LIMIT = 14 * 1024 * 1024
PROJECT_LIMIT = 58 * 1024 * 1024
STATE_LIMIT = 52 * 1024 * 1024


def nt(a, b):
    return lax.dot_general(a, b, (((1,), (1,)), ((), ())), preferred_element_type=F32)


def nn(a, b):
    return jnp.dot(a, b, preferred_element_type=F32)


def call(body, out_shape, args, in_smem=0, flops=1 << 20, grid=None, in_specs=None, out_specs=None, scratch=(), limit=VMEM_LIMIT):
    if in_specs is None:
        in_specs = [pl.BlockSpec(memory_space=pltpu.SMEM)] * in_smem + [
            pl.BlockSpec(memory_space=pltpu.VMEM)
        ] * (len(args) - in_smem)
        out_specs = jax.tree.map(lambda _: pl.BlockSpec(memory_space=pltpu.VMEM), out_shape)
    kwargs = {} if grid is None else {"grid": grid}
    return pl.pallas_call(
        body,
        out_shape=out_shape,
        in_specs=in_specs,
        out_specs=out_specs,
        scratch_shapes=scratch,
        compiler_params=pltpu.CompilerParams(vmem_limit_bytes=limit),
        cost_estimate=pl.CostEstimate(flops=flops, bytes_accessed=1 << 20, transcendentals=0),
        **kwargs,
    )(*args)


def split2(v):
    hi = v.astype(BF)
    return hi, (v - hi.astype(F32)).astype(BF)


def project_small_kernel(flag, e_own, e_oth, s_own, s_oth, out):
    groups, rows, width = out.shape

    def run(ea, eb):
        ps = nt(ea[...], s_own[...]) + nt(eb[...], s_oth[...])
        hi, lo = split2(ps)
        out[...] = jnp.concatenate([hi, lo], 1).reshape(groups, rows, width)

    @pl.when(flag[0] == 1)
    def _():
        run(e_own, e_oth)

    @pl.when(flag[0] == 0)
    def _():
        run(e_oth, e_own)


def project_kernel(place, e_own, e_oth, x_own, x_oth, z_own, z_oth, out, both):
    depth = x_own.shape[0]

    def fill(ea, eb):
        both[:, :depth] = ea[...]
        both[:, depth:] = eb[...]

    @pl.when((pl.program_id(0) == 0) & (place[0] == 1))
    def _():
        fill(e_own, e_oth)

    @pl.when((pl.program_id(0) == 0) & (place[0] == 0))
    def _():
        fill(e_oth, e_own)

    own = jnp.concatenate([x_own[...], z_own[...]], 1)
    oth = jnp.concatenate([x_oth[...], z_oth[...]], 1)
    total = nn(both[...], jnp.concatenate([own, oth], 0))
    out[...] = total.astype(BF).reshape(out.shape)


def small_kernel(part, bc, small):
    total = part[0].astype(F32)
    for k in range(1, part.shape[0]):
        total = total + part[k].astype(F32)
    total = total[:, :64] + total[:, 64:]
    hi, lo = split2(total)
    bc[...] = jnp.concatenate([hi, lo], 1)
    small[...] = total


def state_kernel(place, bc0, bc1, bc2, bc3, s, out, dots, cmat, pieces_ref, held, sems):
    rows = cmat.shape[0]
    chunks = sems.shape[0]
    step = rows // chunks
    copies = [
        pltpu.make_async_copy(
            s.at[pl.ds(k * step, step)], held.at[pl.ds(k * step, step)], sems.at[k]
        )
        for k in range(chunks)
    ]
    for copy in copies:
        copy.start()
    for shift, bc in ((0, bc0), (1, bc1), (2, bc2), (3, bc3)):
        x = lax.rem(place[2] + shift, 4)
        for k in range(4):
            yh = lax.rem(place[3] + k // 2, 2)
            core = lax.rem(place[4] + k % 2, 2)
            pieces_ref[(x * 2 + yh) * 2 + core] = bc[k]
    pieces = [pieces_ref[t] for t in range(16)]
    pieces = [p[:, :32].astype(F32) + p[:, 64:96].astype(F32) for p in pieces]
    b = jnp.concatenate(pieces[:8], 1)
    c = jnp.concatenate(pieces[8:], 1)
    b1, b2, c1, c2 = b[:rows], b[rows:], c[:rows], c[rows:]
    lane = lax.broadcasted_iota(jnp.int32, dots.shape, 1)
    b11 = jnp.sum(b1 * c1, axis=1, keepdims=True)
    b12 = jnp.sum(b1 * c2, axis=1, keepdims=True)
    b22 = jnp.sum(b2 * c2, axis=1, keepdims=True)
    dots[...] = jnp.where(lane == 0, b11, jnp.where(lane == 1, b12, b22))
    cmat[...] = jnp.zeros_like(cmat)
    for k, v in enumerate((c1, c2)):
        v = v * SCALE
        hi = v.astype(BF).astype(F32)
        cmat[:, 2 * k, :] = hi
        cmat[:, 2 * k + 1, :] = v - hi
    for k in range(chunks):
        copies[k].wait()
        for r in range(k * step, (k + 1) * step):
            m = held[r].reshape(s.shape[1] * s.shape[2], s.shape[3])
            out[r] = nt(cmat[r].astype(BF), m)


def decode_kernel(part, small, dots, g, bias, rate, skip, gain, out):
    heads = bias.shape[1]
    inner = gain.shape[1]
    half = part.shape[1] // 2
    total = part[0].astype(F32)
    for k in range(1, part.shape[0]):
        total = total + part[k].astype(F32)
    x_pre = jnp.concatenate([total[:, k : k + 128] for k in range(0, 2 * inner, 256)], 1)
    z_pre = jnp.concatenate([total[:, k + 128 : k + 256] for k in range(0, 2 * inner, 256)], 1)
    pick = (
        lax.broadcasted_iota(jnp.int32, (heads, inner), 0)
        == lax.broadcasted_iota(jnp.int32, (heads, inner), 1) // (inner // heads)
    ).astype(F32)
    expand = functools.partial(
        jnp.dot, preferred_element_type=F32, precision=lax.Precision.HIGHEST
    )
    dt_pre = expand(small[:, 32 : 32 + heads], pick)
    bias_e = expand(bias[...], pick)
    rate_e = expand(rate[...], pick)
    skip_e = expand(skip[...], pick)
    pre = dt_pre + bias_e
    dt = jnp.maximum(pre, 0.0) + jnp.log1p(jnp.exp(-jnp.abs(pre)))
    decay = jnp.exp(-dt * rate_e)
    inputs = x_pre * jax.nn.sigmoid(x_pre)
    upd = dt * inputs
    gate = z_pre * jax.nn.sigmoid(z_pre)
    b11 = dots[:, 0:1]
    b12 = dots[:, 1:2]
    b22 = dots[:, 2:3]
    gs = g[...]
    g1 = gs[:, 0, :] + gs[:, 1, :]
    g2 = gs[:, 2, :] + gs[:, 3, :]
    d1, d2 = decay[:half], decay[half:]
    u1, u2 = upd[:half], upd[half:]
    read1 = (d1 * g1) * (1.0 / SCALE) + u1 * b11 + skip_e * inputs[:half]
    read2 = d2 * ((d1 * g2) * (1.0 / SCALE) + u1 * b12) + u2 * b22 + skip_e * inputs[half:]
    lim = 1e30
    gg1 = jnp.clip(read1 * gate[:half] * gain[...], -lim, lim)
    gg2 = jnp.clip(read2 * gate[half:] * gain[...], -lim, lim)
    out[...] = jnp.concatenate([gg1, gg2], 0).astype(BF)


def output_kernel(place, mine, other, gain, own, r1, l1, r2, l2, r3, l3, r4, out):
    z = place[1]
    groups = out.shape[0] // 2
    rows = out.shape[1]
    m = mine[...]
    o = other[...]
    v = jnp.concatenate([jnp.where(place[5] == 0, m, o), jnp.where(place[5] == 0, o, m)], 0)
    raw = v.astype(F32) / gain[...]
    ss = jnp.sum(raw * raw, axis=1, keepdims=True)
    hi = ss.astype(BF).astype(F32)
    lane = lax.broadcasted_iota(jnp.int32, (2 * rows, 64), 1)
    tail = jnp.where(lane == 0, hi, jnp.where(lane == 1, ss - hi, 0.0))
    order = ((0, own), (7, r1), (1, l1), (6, r2), (2, l2), (5, r3), (3, l3), (4, r4))
    for shift, w in order:
        block = jnp.concatenate([nt(v, w[...]), tail], 1)
        at = lax.rem(z + shift, groups)
        out[2 * at] = block[:rows].astype(BF)
        out[2 * at + 1] = block[rows:].astype(BF)


def reduce_kernel(part, out, *, count):
    total = part[0].astype(F32)
    for k in range(1, part.shape[0]):
        total = total + part[k].astype(F32)
    cols = out.shape[1]
    ss = total[:, cols : cols + 1] + total[:, cols + 1 : cols + 2]
    out[...] = (total[:, :cols] * lax.rsqrt(ss / count + 1e-05)).astype(BF)


def per_device(
    token_ids,
    row_counts,
    code_table,
    x_weight,
    z_weight,
    dt_weight,
    bc_weight,
    dt_bias,
    head_rate,
    skip_gain,
    norm_gain,
    out_weight,
    ssm_state,
):
    rows = token_ids.shape[1]
    heads = dt_bias.shape[0]
    inner = x_weight.shape[1]
    wide = code_table.shape[1]
    y = lax.axis_index("yl")
    core = lax.axis_index("core")
    swap = []
    for z in range(8):
        for yy in range(2):
            for w in range(8):
                for c in range(2):
                    swap.append(((z * 2 + yy) * 16 + w * 2 + c, (w * 2 + yy) * 16 + z * 2 + c))
    pair = [(0, 1), (1, 0)]

    gain = norm_gain.reshape(1, inner)
    right = [(i, (i + 1) % 8) for i in range(8)]
    left = [(i, (i + 7) % 8) for i in range(8)]
    out_own = out_weight.T
    ring_r = [out_own]
    ring_l = [out_own]
    for _ in range(1, 4):
        ring_r.append(lax.ppermute(ring_r[-1], "z", right))
        ring_l.append(lax.ppermute(ring_l[-1], "z", left))
    ring_r.append(lax.ppermute(ring_r[-1], "z", right))
    x_oth = lax.ppermute(x_weight, "yl", pair)
    z_oth = lax.ppermute(z_weight, "yl", pair)
    small_own = jnp.concatenate(
        [bc_weight.T, dt_weight.T, jnp.zeros((64 - 32 - heads, wide), BF)], 0
    )
    small_oth = lax.ppermute(small_own, "yl", pair)

    flat_ids = token_ids.reshape(-1)
    codes = jnp.arange(code_table.shape[0], dtype=jnp.int32)
    one_hot = (flat_ids[:, None] == codes[None, :]).astype(BF)
    own_embed = jnp.dot(one_hot, code_table, preferred_element_type=F32).astype(BF)
    moved = lax.ppermute(own_embed, ALL, swap)
    e_own = lax.all_to_all(
        jnp.broadcast_to(moved[None], (8,) + moved.shape), ("x", "yh"), 0, 0
    ).reshape(8 * 2 * rows, wide)
    e_oth = lax.ppermute(e_own, "core", pair)
    place = jnp.stack(
        [(y == core).astype(jnp.int32), lax.axis_index("z"), lax.axis_index("x"), lax.axis_index("yh"), core, y]
    )
    part_small = call(
        project_small_kernel,
        jax.ShapeDtypeStruct((8, 2 * rows, 128), BF),
        (place, e_own, e_oth, small_own, small_oth),
        in_smem=1,
        flops=2 * 16 * rows * 2 * wide * 128,
    )
    part_small = lax.all_to_all(part_small, "z", 0, 0)
    part = call(
        project_kernel,
        jax.ShapeDtypeStruct((8, 2 * rows, 2 * inner), BF),
        (place, e_own, e_oth, x_weight, x_oth, z_weight, z_oth),
        grid=(inner // 128,),
        in_specs=[pl.BlockSpec(memory_space=pltpu.SMEM)]
        + [pl.BlockSpec((16 * rows, wide), lambda i: (0, 0))] * 2
        + [pl.BlockSpec((wide, 128), lambda i: (0, i))] * 4,
        out_specs=pl.BlockSpec((8, 2 * rows, 256), lambda i: (0, 0, i)),
        scratch=[pltpu.VMEM((16 * rows, 2 * wide), BF)],
        limit=PROJECT_LIMIT,
        flops=2 * 16 * rows * 2 * wide * 2 * inner,
    )
    part = lax.all_to_all(part, "z", 0, 0)
    bc, small = call(
        small_kernel,
        (jax.ShapeDtypeStruct((2 * rows, 128), BF), jax.ShapeDtypeStruct((2 * rows, 64), F32)),
        (part_small,),
    )
    bc2 = jnp.stack([bc, lax.ppermute(bc, "core", pair)])
    bc4 = jnp.concatenate([bc2, lax.ppermute(bc2, "yh", pair)], 0)
    bc_all = [bc4]
    for k in (1, 2, 3):
        bc_all.append(lax.ppermute(bc4, "x", [((i + k) % 4, i) for i in range(4)]))
    g, dots = call(
        state_kernel,
        (jax.ShapeDtypeStruct((rows, 8, inner), F32), jax.ShapeDtypeStruct((rows, 128), F32)),
        (place, *bc_all, ssm_state),
        in_specs=[pl.BlockSpec(memory_space=pltpu.SMEM)]
        + [pl.BlockSpec(memory_space=pltpu.VMEM)] * 4
        + [pl.BlockSpec(memory_space=pl.ANY)],
        out_specs=(pl.BlockSpec(memory_space=pltpu.VMEM), pl.BlockSpec(memory_space=pltpu.VMEM)),
        scratch=[
            pltpu.VMEM((rows, 8, 256), F32),
            pltpu.VMEM((16, 2 * rows, 128), BF),
            pltpu.VMEM(ssm_state.shape, BF),
            pltpu.SemaphoreType.DMA((8,)),
        ],
        limit=STATE_LIMIT,
        flops=2 * 8 * rows * inner * 256,
    )
    gg = call(
        decode_kernel,
        jax.ShapeDtypeStruct((2 * rows, inner), BF),
        (
            part,
            small,
            dots,
            g,
            dt_bias.reshape(1, heads),
            head_rate.reshape(1, heads),
            skip_gain.reshape(1, heads),
            gain,
        ),
    )
    gg_oth = lax.ppermute(gg, "yl", pair)
    out_part = call(
        output_kernel,
        jax.ShapeDtypeStruct((16, 2 * rows, wide + 64), BF),
        (
            place,
            gg,
            gg_oth,
            gain,
            out_own,
            ring_r[1],
            ring_l[1],
            ring_r[2],
            ring_l[2],
            ring_r[3],
            ring_l[3],
            ring_r[4],
        ),
        in_smem=1,
        flops=2 * 4 * rows * inner * 8 * wide,
    )
    partial_out = lax.all_to_all(out_part, TP, 0, 0)
    mine = call(
        functools.partial(reduce_kernel, count=float(16 * inner)),
        jax.ShapeDtypeStruct((2 * rows, wide), BF),
        (partial_out,),
    )
    back = lax.ppermute(mine, ("yl", "core"), [(0, 0), (1, 2), (2, 1), (3, 3)])
    result = (own_embed.astype(F32) + back.astype(F32)).reshape(2, rows, wide)
    live = jnp.arange(rows, dtype=jnp.int32) < row_counts[0]
    return jnp.where(live[None, :, None], result, 0.0).astype(BF)


def solution(mesh):
    fine = Mesh(mesh.devices.reshape(8, 2, 4, 2, 2), ALL)
    return jax.shard_map(
        per_device,
        mesh=fine,
        in_specs=(
            P(None, GROUP),
            P(GROUP),
            P(None, TP),
            P(GROUP, TP),
            P(GROUP, TP),
            P(GROUP, TP),
            P(GROUP, TP),
            P(TP),
            P(TP),
            P(TP),
            P(TP),
            P(TP, GROUP),
            P(GROUP, TP, None, None),
        ),
        out_specs=P(None, GROUP, TP),
        check_vma=False,
    )
```

```python
import functools

import jax
import jax.numpy as jnp
from jax import lax
from jax.experimental import pallas as pl
from jax.experimental.pallas import tpu as pltpu
from jax.sharding import Mesh
from jax.sharding import PartitionSpec as P


BF = jnp.bfloat16
F32 = jnp.float32
SCALE = 2.0**-20
GROUP = ("z", "yl")
TP = ("x", "yh", "core")
ALL = GROUP + TP
VMEM_LIMIT = 14 * 1024 * 1024
PROJECT_LIMIT = 58 * 1024 * 1024
STATE_LIMIT = 52 * 1024 * 1024


def nt(a, b):
    return lax.dot_general(a, b, (((1,), (1,)), ((), ())), preferred_element_type=F32)


def nn(a, b):
    return jnp.dot(a, b, preferred_element_type=F32)


def call(body, out_shape, args, in_smem=0, flops=1 << 20, grid=None, in_specs=None, out_specs=None, scratch=(), limit=VMEM_LIMIT):
    if in_specs is None:
        in_specs = [pl.BlockSpec(memory_space=pltpu.SMEM)] * in_smem + [
            pl.BlockSpec(memory_space=pltpu.VMEM)
        ] * (len(args) - in_smem)
        out_specs = jax.tree.map(lambda _: pl.BlockSpec(memory_space=pltpu.VMEM), out_shape)
    kwargs = {} if grid is None else {"grid": grid}
    return pl.pallas_call(
        body,
        out_shape=out_shape,
        in_specs=in_specs,
        out_specs=out_specs,
        scratch_shapes=scratch,
        compiler_params=pltpu.CompilerParams(vmem_limit_bytes=limit),
        cost_estimate=pl.CostEstimate(flops=flops, bytes_accessed=1 << 20, transcendentals=0),
        **kwargs,
    )(*args)


def split2(v):
    hi = v.astype(BF)
    return hi, (v - hi.astype(F32)).astype(BF)


def project_small_kernel(flag, e_own, e_oth, s_own, s_oth, out):
    groups, rows, width = out.shape

    def run(ea, eb):
        ps = nt(ea[...], s_own[...]) + nt(eb[...], s_oth[...])
        hi, lo = split2(ps)
        out[...] = jnp.concatenate([hi, lo], 1).reshape(groups, rows, width)

    @pl.when(flag[0] == 1)
    def _():
        run(e_own, e_oth)

    @pl.when(flag[0] == 0)
    def _():
        run(e_oth, e_own)


def project_kernel(place, e_own, e_oth, x_own, x_oth, z_own, z_oth, out, both, held, done, sems):
    depth, inner = x_own.shape
    groups, rows = out.shape[:2]
    sources = ((x_own, x_oth), (z_own, z_oth))
    loads = [
        [
            pltpu.make_async_copy(ref, held.at[k, pl.ds(j * depth, depth)], sems.at[2 * k + j])
            for j, ref in enumerate(refs)
        ]
        for k, refs in enumerate(sources)
    ]
    for pair in loads:
        for load in pair:
            load.start()

    def fill(ea, eb):
        both[:, :depth] = ea[...]
        both[:, depth:] = eb[...]

    @pl.when(place[0] == 1)
    def _():
        fill(e_own, e_oth)

    @pl.when(place[0] == 0)
    def _():
        fill(e_oth, e_own)

    stores = []
    for k in range(2):
        for load in loads[k]:
            load.wait()
        total = nn(both[...], held[k])
        done[k] = total.astype(BF).reshape(groups, rows, inner)
        stores.append(
            pltpu.make_async_copy(
                done.at[k], out.at[:, :, pl.ds(k * inner, inner)], sems.at[4 + k]
            )
        )
        stores[k].start()
    for store in stores:
        store.wait()


def small_kernel(part, bc, small):
    total = part[0].astype(F32)
    for k in range(1, part.shape[0]):
        total = total + part[k].astype(F32)
    total = total[:, :64] + total[:, 64:]
    hi, lo = split2(total)
    bc[...] = jnp.concatenate([hi, lo], 1)
    small[...] = total


def state_kernel(place, bc0, bc1, bc2, bc3, s, out, dots, cmat, pieces_ref, held, sems):
    rows = cmat.shape[0]
    chunks = sems.shape[0]
    step = rows // chunks
    copies = [
        pltpu.make_async_copy(
            s.at[pl.ds(k * step, step)], held.at[pl.ds(k * step, step)], sems.at[k]
        )
        for k in range(chunks)
    ]
    for copy in copies:
        copy.start()
    for shift, bc in ((0, bc0), (1, bc1), (2, bc2), (3, bc3)):
        x = lax.rem(place[2] + shift, 4)
        for k in range(4):
            yh = lax.rem(place[3] + k // 2, 2)
            core = lax.rem(place[4] + k % 2, 2)
            pieces_ref[(x * 2 + yh) * 2 + core] = bc[k]
    pieces = [pieces_ref[t] for t in range(16)]
    pieces = [p[:, :32].astype(F32) + p[:, 64:96].astype(F32) for p in pieces]
    b = jnp.concatenate(pieces[:8], 1)
    c = jnp.concatenate(pieces[8:], 1)
    b1, b2, c1, c2 = b[:rows], b[rows:], c[:rows], c[rows:]
    lane = lax.broadcasted_iota(jnp.int32, dots.shape, 1)
    b11 = jnp.sum(b1 * c1, axis=1, keepdims=True)
    b12 = jnp.sum(b1 * c2, axis=1, keepdims=True)
    b22 = jnp.sum(b2 * c2, axis=1, keepdims=True)
    dots[...] = jnp.where(lane == 0, b11, jnp.where(lane == 1, b12, b22))
    cmat[...] = jnp.zeros_like(cmat)
    for k, v in enumerate((c1, c2)):
        v = v * SCALE
        hi = v.astype(BF).astype(F32)
        cmat[:, 2 * k, :] = hi
        cmat[:, 2 * k + 1, :] = v - hi
    for k in range(chunks):
        copies[k].wait()
        for r in range(k * step, (k + 1) * step):
            m = held[r].reshape(s.shape[1] * s.shape[2], s.shape[3])
            out[r] = nt(cmat[r].astype(BF), m)


def decode_kernel(part, small, dots, g, bias, rate, skip, gain, out):
    heads = bias.shape[1]
    inner = gain.shape[1]
    half = part.shape[1] // 2
    total = part[0].astype(F32)
    for k in range(1, part.shape[0]):
        total = total + part[k].astype(F32)
    x_pre = total[:, :inner]
    z_pre = total[:, inner:]
    pick = (
        lax.broadcasted_iota(jnp.int32, (heads, inner), 0)
        == lax.broadcasted_iota(jnp.int32, (heads, inner), 1) // (inner // heads)
    ).astype(F32)
    expand = functools.partial(
        jnp.dot, preferred_element_type=F32, precision=lax.Precision.HIGHEST
    )
    dt_pre = expand(small[:, 32 : 32 + heads], pick)
    bias_e = expand(bias[...], pick)
    rate_e = expand(rate[...], pick)
    skip_e = expand(skip[...], pick)
    pre = dt_pre + bias_e
    dt = jnp.maximum(pre, 0.0) + jnp.log1p(jnp.exp(-jnp.abs(pre)))
    decay = jnp.exp(-dt * rate_e)
    inputs = x_pre * jax.nn.sigmoid(x_pre)
    upd = dt * inputs
    gate = z_pre * jax.nn.sigmoid(z_pre)
    b11 = dots[:, 0:1]
    b12 = dots[:, 1:2]
    b22 = dots[:, 2:3]
    gs = g[...]
    g1 = gs[:, 0, :] + gs[:, 1, :]
    g2 = gs[:, 2, :] + gs[:, 3, :]
    d1, d2 = decay[:half], decay[half:]
    u1, u2 = upd[:half], upd[half:]
    read1 = (d1 * g1) * (1.0 / SCALE) + u1 * b11 + skip_e * inputs[:half]
    read2 = d2 * ((d1 * g2) * (1.0 / SCALE) + u1 * b12) + u2 * b22 + skip_e * inputs[half:]
    lim = 1e30
    gg1 = jnp.clip(read1 * gate[:half] * gain[...], -lim, lim)
    gg2 = jnp.clip(read2 * gate[half:] * gain[...], -lim, lim)
    out[...] = jnp.concatenate([gg1, gg2], 0).astype(BF)


def output_kernel(place, mine, other, gain, own, r1, l1, r2, l2, r3, l3, r4, keep, send):
    same = place[0]
    z = place[1]
    groups, rows, _ = keep.shape
    m = mine[...]
    o = other[...]
    v = jnp.concatenate([jnp.where(same == 1, m, o), jnp.where(same == 1, o, m)], 0)
    raw = v.astype(F32) / gain[...]
    ss = jnp.sum(raw * raw, axis=1, keepdims=True)
    hi = ss.astype(BF).astype(F32)
    lane = lax.broadcasted_iota(jnp.int32, (2 * rows, 64), 1)
    tail = jnp.where(lane == 0, hi, jnp.where(lane == 1, ss - hi, 0.0))
    order = ((0, own), (7, r1), (1, l1), (6, r2), (2, l2), (5, r3), (3, l3), (4, r4))
    for shift, w in order:
        block = jnp.concatenate([nt(v, w[...]), tail], 1)
        at = lax.rem(z + shift, groups)
        keep[at] = block[:rows]
        send[at] = block[rows:].astype(BF)


def pair_kernel(keep, got, out):
    total = keep[...] + got[...].astype(F32)
    cols = out.shape[2] - 64
    lane = lax.broadcasted_iota(jnp.int32, total.shape, 2)
    ss = total[:, :, cols : cols + 1] + total[:, :, cols + 1 : cols + 2]
    hi = ss.astype(BF).astype(F32)
    total = jnp.where(lane == cols, hi, jnp.where(lane == cols + 1, ss - hi, total))
    out[...] = total.astype(BF)


def reduce_kernel(part, out, *, count):
    total = part[0].astype(F32)
    for k in range(1, part.shape[0]):
        total = total + part[k].astype(F32)
    cols = out.shape[1]
    ss = total[:, cols : cols + 1] + total[:, cols + 1 : cols + 2]
    out[...] = (total[:, :cols] * lax.rsqrt(ss / count + 1e-05)).astype(BF)


def per_device(
    token_ids,
    row_counts,
    code_table,
    x_weight,
    z_weight,
    dt_weight,
    bc_weight,
    dt_bias,
    head_rate,
    skip_gain,
    norm_gain,
    out_weight,
    ssm_state,
):
    rows = token_ids.shape[1]
    heads = dt_bias.shape[0]
    inner = x_weight.shape[1]
    wide = code_table.shape[1]
    y = lax.axis_index("yl")
    core = lax.axis_index("core")
    swap = []
    for z in range(8):
        for yy in range(2):
            for w in range(8):
                for c in range(2):
                    swap.append(((z * 2 + yy) * 16 + w * 2 + c, (w * 2 + yy) * 16 + z * 2 + c))
    pair = [(0, 1), (1, 0)]

    gain = norm_gain.reshape(1, inner)
    right = [(i, (i + 1) % 8) for i in range(8)]
    left = [(i, (i + 7) % 8) for i in range(8)]
    out_own = out_weight.T
    ring_r = [out_own]
    ring_l = [out_own]
    for _ in range(1, 4):
        ring_r.append(lax.ppermute(ring_r[-1], "z", right))
        ring_l.append(lax.ppermute(ring_l[-1], "z", left))
    ring_r.append(lax.ppermute(ring_r[-1], "z", right))
    x_oth = lax.ppermute(x_weight, "yl", pair)
    z_oth = lax.ppermute(z_weight, "yl", pair)
    small_own = jnp.concatenate(
        [bc_weight.T, dt_weight.T, jnp.zeros((64 - 32 - heads, wide), BF)], 0
    )
    small_oth = lax.ppermute(small_own, "yl", pair)

    flat_ids = token_ids.reshape(-1)
    codes = jnp.arange(code_table.shape[0], dtype=jnp.int32)
    one_hot = (flat_ids[:, None] == codes[None, :]).astype(BF)
    own_embed = jnp.dot(one_hot, code_table, preferred_element_type=F32).astype(BF)
    moved = lax.ppermute(own_embed, ALL, swap)
    e_own = lax.all_to_all(
        jnp.broadcast_to(moved[None], (8,) + moved.shape), ("x", "yh"), 0, 0
    ).reshape(8 * 2 * rows, wide)
    e_oth = lax.ppermute(e_own, "core", pair)
    place = jnp.stack(
        [(y == core).astype(jnp.int32), lax.axis_index("z"), lax.axis_index("x"), lax.axis_index("yh"), core]
    )
    part_small = call(
        project_small_kernel,
        jax.ShapeDtypeStruct((8, 2 * rows, 128), BF),
        (place, e_own, e_oth, small_own, small_oth),
        in_smem=1,
        flops=2 * 16 * rows * 2 * wide * 128,
    )
    part_small = lax.all_to_all(part_small, "z", 0, 0)
    part = call(
        project_kernel,
        jax.ShapeDtypeStruct((8, 2 * rows, 2 * inner), BF),
        (place, e_own, e_oth, x_weight, x_oth, z_weight, z_oth),
        in_specs=[pl.BlockSpec(memory_space=pltpu.SMEM)]
        + [pl.BlockSpec(memory_space=pltpu.VMEM)] * 2
        + [pl.BlockSpec(memory_space=pl.ANY)] * 4,
        out_specs=pl.BlockSpec(memory_space=pl.ANY),
        scratch=[
            pltpu.VMEM((16 * rows, 2 * wide), BF),
            pltpu.VMEM((2, 2 * wide, inner), BF),
            pltpu.VMEM((2, 8, 2 * rows, inner), BF),
            pltpu.SemaphoreType.DMA((6,)),
        ],
        limit=PROJECT_LIMIT,
        flops=2 * 16 * rows * 2 * wide * 2 * inner,
    )
    part = lax.all_to_all(part, "z", 0, 0)
    bc, small = call(
        small_kernel,
        (jax.ShapeDtypeStruct((2 * rows, 128), BF), jax.ShapeDtypeStruct((2 * rows, 64), F32)),
        (part_small,),
    )
    bc2 = jnp.stack([bc, lax.ppermute(bc, "core", pair)])
    bc4 = jnp.concatenate([bc2, lax.ppermute(bc2, "yh", pair)], 0)
    bc_all = [bc4]
    for k in (1, 2, 3):
        bc_all.append(lax.ppermute(bc4, "x", [((i + k) % 4, i) for i in range(4)]))
    g, dots = call(
        state_kernel,
        (jax.ShapeDtypeStruct((rows, 8, inner), F32), jax.ShapeDtypeStruct((rows, 128), F32)),
        (place, *bc_all, ssm_state),
        in_specs=[pl.BlockSpec(memory_space=pltpu.SMEM)]
        + [pl.BlockSpec(memory_space=pltpu.VMEM)] * 4
        + [pl.BlockSpec(memory_space=pl.ANY)],
        out_specs=(pl.BlockSpec(memory_space=pltpu.VMEM), pl.BlockSpec(memory_space=pltpu.VMEM)),
        scratch=[
            pltpu.VMEM((rows, 8, 256), F32),
            pltpu.VMEM((16, 2 * rows, 128), BF),
            pltpu.VMEM(ssm_state.shape, BF),
            pltpu.SemaphoreType.DMA((8,)),
        ],
        limit=STATE_LIMIT,
        flops=2 * 8 * rows * inner * 256,
    )
    gg = call(
        decode_kernel,
        jax.ShapeDtypeStruct((2 * rows, inner), BF),
        (
            part,
            small,
            dots,
            g,
            dt_bias.reshape(1, heads),
            head_rate.reshape(1, heads),
            skip_gain.reshape(1, heads),
            gain,
        ),
    )
    gg_oth = lax.ppermute(gg, "yl", pair)
    keep, send = call(
        output_kernel,
        (
            jax.ShapeDtypeStruct((8, 2 * rows, wide + 64), F32),
            jax.ShapeDtypeStruct((8, 2 * rows, wide + 64), BF),
        ),
        (
            place,
            gg,
            gg_oth,
            gain,
            out_own,
            ring_r[1],
            ring_l[1],
            ring_r[2],
            ring_l[2],
            ring_r[3],
            ring_l[3],
            ring_r[4],
        ),
        in_smem=1,
        flops=2 * 4 * rows * inner * 8 * wide,
    )
    got = lax.ppermute(send, "core", pair)
    paired = call(pair_kernel, jax.ShapeDtypeStruct((8, 2 * rows, wide + 64), BF), (keep, got))
    partial_out = lax.all_to_all(paired, ("x", "yh"), 0, 0)
    mine = call(
        functools.partial(reduce_kernel, count=float(16 * inner)),
        jax.ShapeDtypeStruct((2 * rows, wide), BF),
        (partial_out,),
    )
    back = lax.ppermute(mine, ("yl", "core"), [(0, 0), (1, 2), (2, 1), (3, 3)])
    result = (own_embed.astype(F32) + back.astype(F32)).reshape(2, rows, wide)
    live = jnp.arange(rows, dtype=jnp.int32) < row_counts[0]
    return jnp.where(live[None, :, None], result, 0.0).astype(BF)


def solution(mesh):
    fine = Mesh(mesh.devices.reshape(8, 2, 4, 2, 2), ALL)
    return jax.shard_map(
        per_device,
        mesh=fine,
        in_specs=(
            P(None, GROUP),
            P(GROUP),
            P(None, TP),
            P(GROUP, TP),
            P(GROUP, TP),
            P(GROUP, TP),
            P(GROUP, TP),
            P(TP),
            P(TP),
            P(TP),
            P(TP),
            P(TP, GROUP),
            P(GROUP, TP, None, None),
        ),
        out_specs=P(None, GROUP, TP),
        check_vma=False,
    )
```

```python
import functools

import jax
import jax.numpy as jnp
from jax import lax
from jax.experimental import pallas as pl
from jax.experimental.pallas import tpu as pltpu
from jax.sharding import Mesh
from jax.sharding import PartitionSpec as P


BF = jnp.bfloat16
F32 = jnp.float32
SCALE = 2.0**-20
GROUP = ("z", "yl")
TP = ("x", "yh", "core")
ALL = GROUP + TP
VMEM_LIMIT = 14 * 1024 * 1024
PROJECT_LIMIT = 58 * 1024 * 1024
STATE_LIMIT = 52 * 1024 * 1024


def nt(a, b):
    return lax.dot_general(a, b, (((1,), (1,)), ((), ())), preferred_element_type=F32)


def nn(a, b):
    return jnp.dot(a, b, preferred_element_type=F32)


def call(body, out_shape, args, in_smem=0, flops=1 << 20, grid=None, in_specs=None, out_specs=None, scratch=(), limit=VMEM_LIMIT):
    if in_specs is None:
        in_specs = [pl.BlockSpec(memory_space=pltpu.SMEM)] * in_smem + [
            pl.BlockSpec(memory_space=pltpu.VMEM)
        ] * (len(args) - in_smem)
        out_specs = jax.tree.map(lambda _: pl.BlockSpec(memory_space=pltpu.VMEM), out_shape)
    kwargs = {} if grid is None else {"grid": grid}
    return pl.pallas_call(
        body,
        out_shape=out_shape,
        in_specs=in_specs,
        out_specs=out_specs,
        scratch_shapes=scratch,
        compiler_params=pltpu.CompilerParams(vmem_limit_bytes=limit),
        cost_estimate=pl.CostEstimate(flops=flops, bytes_accessed=1 << 20, transcendentals=0),
        **kwargs,
    )(*args)


def split2(v):
    hi = v.astype(BF)
    return hi, (v - hi.astype(F32)).astype(BF)


def project_small_kernel(flag, e_own, e_oth, s_own, s_oth, out):
    groups, rows, width = out.shape

    def run(ea, eb):
        ps = nt(ea[...], s_own[...]) + nt(eb[...], s_oth[...])
        hi, lo = split2(ps)
        out[...] = jnp.concatenate([hi, lo], 1).reshape(groups, rows, width)

    @pl.when(flag[0] == 1)
    def _():
        run(e_own, e_oth)

    @pl.when(flag[0] == 0)
    def _():
        run(e_oth, e_own)


def project_kernel(place, e_own, e_oth, x_own, x_oth, z_own, z_oth, out, both, held, done, sems):
    depth, inner = x_own.shape
    groups, rows = out.shape[:2]
    sources = ((x_own, x_oth), (z_own, z_oth))
    loads = [
        [
            pltpu.make_async_copy(ref, held.at[k, pl.ds(j * depth, depth)], sems.at[2 * k + j])
            for j, ref in enumerate(refs)
        ]
        for k, refs in enumerate(sources)
    ]
    for pair in loads:
        for load in pair:
            load.start()

    def fill(ea, eb):
        both[:, :depth] = ea[...]
        both[:, depth:] = eb[...]

    @pl.when(place[0] == 1)
    def _():
        fill(e_own, e_oth)

    @pl.when(place[0] == 0)
    def _():
        fill(e_oth, e_own)

    stores = []
    for k in range(2):
        for load in loads[k]:
            load.wait()
        total = nn(both[...], held[k])
        done[k] = total.astype(BF).reshape(groups, rows, inner)
        stores.append(
            pltpu.make_async_copy(
                done.at[k], out.at[:, :, pl.ds(k * inner, inner)], sems.at[4 + k]
            )
        )
        stores[k].start()
    for store in stores:
        store.wait()


def small_kernel(part, bc, small):
    total = part[0].astype(F32)
    for k in range(1, part.shape[0]):
        total = total + part[k].astype(F32)
    total = total[:, :64] + total[:, 64:]
    hi, lo = split2(total)
    bc[...] = jnp.concatenate([hi, lo], 1)
    small[...] = total


def state_kernel(place, bc0, bc1, bc2, bc3, s, out, dots, cmat, pieces_ref, held, sems):
    rows = cmat.shape[0]
    chunks = sems.shape[0]
    step = rows // chunks
    copies = [
        pltpu.make_async_copy(
            s.at[pl.ds(k * step, step)], held.at[pl.ds(k * step, step)], sems.at[k]
        )
        for k in range(chunks)
    ]
    for copy in copies:
        copy.start()
    for shift, bc in ((0, bc0), (1, bc1), (2, bc2), (3, bc3)):
        x = lax.rem(place[2] + shift, 4)
        for k in range(4):
            yh = lax.rem(place[3] + k // 2, 2)
            core = lax.rem(place[4] + k % 2, 2)
            pieces_ref[(x * 2 + yh) * 2 + core] = bc[k]
    pieces = [pieces_ref[t] for t in range(16)]
    pieces = [p[:, :32].astype(F32) + p[:, 64:96].astype(F32) for p in pieces]
    b = jnp.concatenate(pieces[:8], 1)
    c = jnp.concatenate(pieces[8:], 1)
    b1, b2, c1, c2 = b[:rows], b[rows:], c[:rows], c[rows:]
    lane = lax.broadcasted_iota(jnp.int32, dots.shape, 1)
    b11 = jnp.sum(b1 * c1, axis=1, keepdims=True)
    b12 = jnp.sum(b1 * c2, axis=1, keepdims=True)
    b22 = jnp.sum(b2 * c2, axis=1, keepdims=True)
    dots[...] = jnp.where(lane == 0, b11, jnp.where(lane == 1, b12, b22))
    cmat[...] = jnp.zeros_like(cmat)
    for k, v in enumerate((c1, c2)):
        v = v * SCALE
        hi = v.astype(BF).astype(F32)
        cmat[:, 2 * k, :] = hi
        cmat[:, 2 * k + 1, :] = v - hi
    for k in range(chunks):
        copies[k].wait()
        for r in range(k * step, (k + 1) * step):
            m = held[r].reshape(s.shape[1] * s.shape[2], s.shape[3])
            out[r] = nt(cmat[r].astype(BF), m)


def decode_kernel(part, small, dots, g, bias, rate, skip, gain, out):
    heads = bias.shape[1]
    inner = gain.shape[1]
    half = part.shape[1] // 2
    total = part[0].astype(F32)
    for k in range(1, part.shape[0]):
        total = total + part[k].astype(F32)
    x_pre = total[:, :inner]
    z_pre = total[:, inner:]
    pick = (
        lax.broadcasted_iota(jnp.int32, (heads, inner), 0)
        == lax.broadcasted_iota(jnp.int32, (heads, inner), 1) // (inner // heads)
    ).astype(F32)
    expand = functools.partial(
        jnp.dot, preferred_element_type=F32, precision=lax.Precision.HIGHEST
    )
    dt_pre = expand(small[:, 32 : 32 + heads], pick)
    bias_e = expand(bias[...], pick)
    rate_e = expand(rate[...], pick)
    skip_e = expand(skip[...], pick)
    pre = dt_pre + bias_e
    dt = jnp.maximum(pre, 0.0) + jnp.log1p(jnp.exp(-jnp.abs(pre)))
    decay = jnp.exp(-dt * rate_e)
    inputs = x_pre * jax.nn.sigmoid(x_pre)
    upd = dt * inputs
    gate = z_pre * jax.nn.sigmoid(z_pre)
    b11 = dots[:, 0:1]
    b12 = dots[:, 1:2]
    b22 = dots[:, 2:3]
    gs = g[...]
    g1 = gs[:, 0, :] + gs[:, 1, :]
    g2 = gs[:, 2, :] + gs[:, 3, :]
    d1, d2 = decay[:half], decay[half:]
    u1, u2 = upd[:half], upd[half:]
    read1 = (d1 * g1) * (1.0 / SCALE) + u1 * b11 + skip_e * inputs[:half]
    read2 = d2 * ((d1 * g2) * (1.0 / SCALE) + u1 * b12) + u2 * b22 + skip_e * inputs[half:]
    lim = 1e30
    gg1 = jnp.clip(read1 * gate[:half] * gain[...], -lim, lim)
    gg2 = jnp.clip(read2 * gate[half:] * gain[...], -lim, lim)
    out[...] = jnp.concatenate([gg1, gg2], 0).astype(BF)


def output_kernel(place, mine, other, gain, own, r1, l1, r2, l2, r3, l3, r4, l4, keep, send):
    same = place[0]
    z = place[1]
    groups, rows, _ = keep.shape
    m = mine[...]
    o = other[...]
    v = jnp.concatenate([jnp.where(same == 1, m, o), jnp.where(same == 1, o, m)], 0)
    raw = v.astype(F32) / gain[...]
    ss = jnp.sum(raw * raw, axis=1, keepdims=True)
    hi = ss.astype(BF).astype(F32)
    lane = lax.broadcasted_iota(jnp.int32, (2 * rows, 64), 1)
    tail = jnp.where(lane == 0, hi, jnp.where(lane == 1, ss - hi, 0.0))
    order = ((0, own), (7, r1), (1, l1), (6, r2), (2, l2), (5, r3), (3, l3), (4, None))
    for shift, w in order:
        w = jnp.concatenate([r4[...], l4[...]], 0) if w is None else w[...]
        block = jnp.concatenate([nt(v, w), tail], 1)
        at = lax.rem(z + shift, groups)
        keep[at] = block[:rows]
        send[at] = block[rows:].astype(BF)


def pair_kernel(keep, got, out):
    total = keep[...] + got[...].astype(F32)
    cols = out.shape[2] - 64
    lane = lax.broadcasted_iota(jnp.int32, total.shape, 2)
    ss = total[:, :, cols : cols + 1] + total[:, :, cols + 1 : cols + 2]
    hi = ss.astype(BF).astype(F32)
    total = jnp.where(lane == cols, hi, jnp.where(lane == cols + 1, ss - hi, total))
    out[...] = total.astype(BF)


def reduce_kernel(part, out, *, count):
    total = part[0].astype(F32)
    for k in range(1, part.shape[0]):
        total = total + part[k].astype(F32)
    cols = out.shape[1]
    ss = total[:, cols : cols + 1] + total[:, cols + 1 : cols + 2]
    out[...] = (total[:, :cols] * lax.rsqrt(ss / count + 1e-05)).astype(BF)


def per_device(
    token_ids,
    row_counts,
    code_table,
    x_weight,
    z_weight,
    dt_weight,
    bc_weight,
    dt_bias,
    head_rate,
    skip_gain,
    norm_gain,
    out_weight,
    ssm_state,
):
    rows = token_ids.shape[1]
    heads = dt_bias.shape[0]
    inner = x_weight.shape[1]
    wide = code_table.shape[1]
    y = lax.axis_index("yl")
    core = lax.axis_index("core")
    swap = []
    for z in range(8):
        for yy in range(2):
            for w in range(8):
                for c in range(2):
                    swap.append(((z * 2 + yy) * 16 + w * 2 + c, (w * 2 + yy) * 16 + z * 2 + c))
    pair = [(0, 1), (1, 0)]

    gain = norm_gain.reshape(1, inner)
    right = [(i, (i + 1) % 8) for i in range(8)]
    left = [(i, (i + 7) % 8) for i in range(8)]
    out_own = out_weight.T
    ring_r = [out_own]
    ring_l = [out_own]
    for _ in range(1, 4):
        ring_r.append(lax.ppermute(ring_r[-1], "z", right))
        ring_l.append(lax.ppermute(ring_l[-1], "z", left))
    far_r = lax.ppermute(ring_r[3][: wide // 2], "z", right)
    far_l = lax.ppermute(ring_l[3][wide // 2 :], "z", left)
    x_oth = lax.ppermute(x_weight, "yl", pair)
    z_oth = lax.ppermute(z_weight, "yl", pair)
    small_own = jnp.concatenate(
        [bc_weight.T, dt_weight.T, jnp.zeros((64 - 32 - heads, wide), BF)], 0
    )
    small_oth = lax.ppermute(small_own, "yl", pair)

    flat_ids = token_ids.reshape(-1)
    codes = jnp.arange(code_table.shape[0], dtype=jnp.int32)
    one_hot = (flat_ids[:, None] == codes[None, :]).astype(BF)
    own_embed = jnp.dot(one_hot, code_table, preferred_element_type=F32).astype(BF)
    moved = lax.ppermute(own_embed, ALL, swap)
    e_own = lax.all_to_all(
        jnp.broadcast_to(moved[None], (8,) + moved.shape), ("x", "yh"), 0, 0
    ).reshape(8 * 2 * rows, wide)
    e_oth = lax.ppermute(e_own, "core", pair)
    place = jnp.stack(
        [(y == core).astype(jnp.int32), lax.axis_index("z"), lax.axis_index("x"), lax.axis_index("yh"), core]
    )
    part_small = call(
        project_small_kernel,
        jax.ShapeDtypeStruct((8, 2 * rows, 128), BF),
        (place, e_own, e_oth, small_own, small_oth),
        in_smem=1,
        flops=2 * 16 * rows * 2 * wide * 128,
    )
    part_small = lax.all_to_all(part_small, "z", 0, 0)
    part = call(
        project_kernel,
        jax.ShapeDtypeStruct((8, 2 * rows, 2 * inner), BF),
        (place, e_own, e_oth, x_weight, x_oth, z_weight, z_oth),
        in_specs=[pl.BlockSpec(memory_space=pltpu.SMEM)]
        + [pl.BlockSpec(memory_space=pltpu.VMEM)] * 2
        + [pl.BlockSpec(memory_space=pl.ANY)] * 4,
        out_specs=pl.BlockSpec(memory_space=pl.ANY),
        scratch=[
            pltpu.VMEM((16 * rows, 2 * wide), BF),
            pltpu.VMEM((2, 2 * wide, inner), BF),
            pltpu.VMEM((2, 8, 2 * rows, inner), BF),
            pltpu.SemaphoreType.DMA((6,)),
        ],
        limit=PROJECT_LIMIT,
        flops=2 * 16 * rows * 2 * wide * 2 * inner,
    )
    part = lax.all_to_all(part, "z", 0, 0)
    bc, small = call(
        small_kernel,
        (jax.ShapeDtypeStruct((2 * rows, 128), BF), jax.ShapeDtypeStruct((2 * rows, 64), F32)),
        (part_small,),
    )
    bc2 = jnp.stack([bc, lax.ppermute(bc, "core", pair)])
    bc4 = jnp.concatenate([bc2, lax.ppermute(bc2, "yh", pair)], 0)
    bc_all = [bc4]
    for k in (1, 2, 3):
        bc_all.append(lax.ppermute(bc4, "x", [((i + k) % 4, i) for i in range(4)]))
    g, dots = call(
        state_kernel,
        (jax.ShapeDtypeStruct((rows, 8, inner), F32), jax.ShapeDtypeStruct((rows, 128), F32)),
        (place, *bc_all, ssm_state),
        in_specs=[pl.BlockSpec(memory_space=pltpu.SMEM)]
        + [pl.BlockSpec(memory_space=pltpu.VMEM)] * 4
        + [pl.BlockSpec(memory_space=pl.ANY)],
        out_specs=(pl.BlockSpec(memory_space=pltpu.VMEM), pl.BlockSpec(memory_space=pltpu.VMEM)),
        scratch=[
            pltpu.VMEM((rows, 8, 256), F32),
            pltpu.VMEM((16, 2 * rows, 128), BF),
            pltpu.VMEM(ssm_state.shape, BF),
            pltpu.SemaphoreType.DMA((8,)),
        ],
        limit=STATE_LIMIT,
        flops=2 * 8 * rows * inner * 256,
    )
    gg = call(
        decode_kernel,
        jax.ShapeDtypeStruct((2 * rows, inner), BF),
        (
            part,
            small,
            dots,
            g,
            dt_bias.reshape(1, heads),
            head_rate.reshape(1, heads),
            skip_gain.reshape(1, heads),
            gain,
        ),
    )
    gg_oth = lax.ppermute(gg, "yl", pair)
    keep, send = call(
        output_kernel,
        (
            jax.ShapeDtypeStruct((8, 2 * rows, wide + 64), F32),
            jax.ShapeDtypeStruct((8, 2 * rows, wide + 64), BF),
        ),
        (
            place,
            gg,
            gg_oth,
            gain,
            out_own,
            ring_r[1],
            ring_l[1],
            ring_r[2],
            ring_l[2],
            ring_r[3],
            ring_l[3],
            far_r,
            far_l,
        ),
        in_smem=1,
        flops=2 * 4 * rows * inner * 8 * wide,
    )
    got = lax.ppermute(send, "core", pair)
    paired = call(pair_kernel, jax.ShapeDtypeStruct((8, 2 * rows, wide + 64), BF), (keep, got))
    partial_out = lax.all_to_all(paired, ("x", "yh"), 0, 0)
    mine = call(
        functools.partial(reduce_kernel, count=float(16 * inner)),
        jax.ShapeDtypeStruct((2 * rows, wide), BF),
        (partial_out,),
    )
    back = lax.ppermute(mine, ("yl", "core"), [(0, 0), (1, 2), (2, 1), (3, 3)])
    result = (own_embed.astype(F32) + back.astype(F32)).reshape(2, rows, wide)
    live = jnp.arange(rows, dtype=jnp.int32) < row_counts[0]
    return jnp.where(live[None, :, None], result, 0.0).astype(BF)


def solution(mesh):
    fine = Mesh(mesh.devices.reshape(8, 2, 4, 2, 2), ALL)
    return jax.shard_map(
        per_device,
        mesh=fine,
        in_specs=(
            P(None, GROUP),
            P(GROUP),
            P(None, TP),
            P(GROUP, TP),
            P(GROUP, TP),
            P(GROUP, TP),
            P(GROUP, TP),
            P(TP),
            P(TP),
            P(TP),
            P(TP),
            P(TP, GROUP),
            P(GROUP, TP, None, None),
        ),
        out_specs=P(None, GROUP, TP),
        check_vma=False,
    )
```

```python
import functools

import jax
import jax.numpy as jnp
from jax import lax
from jax.experimental import pallas as pl
from jax.experimental.pallas import tpu as pltpu
from jax.sharding import Mesh
from jax.sharding import PartitionSpec as P


BF = jnp.bfloat16
F32 = jnp.float32
SCALE = 2.0**-20
GROUP = ("z", "yl")
TP = ("x", "yh", "core")
ALL = GROUP + TP
VMEM_LIMIT = 14 * 1024 * 1024
PROJECT_LIMIT = 58 * 1024 * 1024
STATE_LIMIT = 52 * 1024 * 1024

SHIFTS = (4, 3, 5, 2, 6, 1, 7)


def nt(a, b):
    return lax.dot_general(a, b, (((1,), (1,)), ((), ())), preferred_element_type=F32)


def nn(a, b):
    return jnp.dot(a, b, preferred_element_type=F32)


def call(body, out_shape, args, in_smem=0, flops=1 << 20, grid=None, in_specs=None, out_specs=None, scratch=(), limit=VMEM_LIMIT):
    if in_specs is None:
        in_specs = [pl.BlockSpec(memory_space=pltpu.SMEM)] * in_smem + [
            pl.BlockSpec(memory_space=pltpu.VMEM)
        ] * (len(args) - in_smem)
        out_specs = jax.tree.map(lambda _: pl.BlockSpec(memory_space=pltpu.VMEM), out_shape)
    kwargs = {} if grid is None else {"grid": grid}
    return pl.pallas_call(
        body,
        out_shape=out_shape,
        in_specs=in_specs,
        out_specs=out_specs,
        scratch_shapes=scratch,
        compiler_params=pltpu.CompilerParams(vmem_limit_bytes=limit),
        cost_estimate=pl.CostEstimate(flops=flops, bytes_accessed=1 << 20, transcendentals=0),
        **kwargs,
    )(*args)


def split2(v):
    hi = v.astype(BF)
    return hi, (v - hi.astype(F32)).astype(BF)


def project_small_kernel(flag, e_own, e_oth, s_own, s_oth, out):
    groups, rows, width = out.shape

    def run(ea, eb):
        ps = nt(ea[...], s_own[...]) + nt(eb[...], s_oth[...])
        hi, lo = split2(ps)
        out[...] = jnp.concatenate([hi, lo], 1).reshape(groups, rows, width)

    @pl.when(flag[0] == 1)
    def _():
        run(e_own, e_oth)

    @pl.when(flag[0] == 0)
    def _():
        run(e_oth, e_own)


def project_kernel(place, e_own, e_oth, x_own, x_oth, z_own, z_oth, *refs):
    outs, (both, held, done, sems) = refs[:8], refs[8:]
    depth, inner = x_own.shape
    groups, rows = len(outs), outs[0].shape[0]
    sources = ((x_own, x_oth), (z_own, z_oth))
    loads = [
        [
            pltpu.make_async_copy(ref, held.at[k, pl.ds(j * depth, depth)], sems.at[2 * k + j])
            for j, ref in enumerate(refs)
        ]
        for k, refs in enumerate(sources)
    ]
    for pair in loads:
        for load in pair:
            load.start()

    def fill(ea, eb):
        both[:, :depth] = ea[...]
        both[:, depth:] = eb[...]

    @pl.when(place[0] == 1)
    def _():
        fill(e_own, e_oth)

    @pl.when(place[0] == 0)
    def _():
        fill(e_oth, e_own)

    stores = []
    for k in range(2):
        for load in loads[k]:
            load.wait()
        total = nn(both[...], held[k])
        done[k] = total.astype(BF).reshape(groups, rows, inner)
        for j in range(groups):
            stores.append(
                pltpu.make_async_copy(
                    done.at[k, lax.rem(place[1] + j, groups)],
                    outs[j].at[:, pl.ds(k * inner, inner)],
                    sems.at[4 + k * groups + j],
                )
            )
            stores[-1].start()
    for store in stores:
        store.wait()


def small_kernel(part, bc, small):
    total = part[0].astype(F32)
    for k in range(1, part.shape[0]):
        total = total + part[k].astype(F32)
    total = total[:, :64] + total[:, 64:]
    hi, lo = split2(total)
    bc[...] = jnp.concatenate([hi, lo], 1)
    small[...] = total


def state_kernel(place, bc0, bc1, bc2, bc3, s, out, dots, cmat, pieces_ref, held, sems):
    rows = cmat.shape[0]
    chunks = sems.shape[0]
    step = rows // chunks
    copies = [
        pltpu.make_async_copy(
            s.at[pl.ds(k * step, step)], held.at[pl.ds(k * step, step)], sems.at[k]
        )
        for k in range(chunks)
    ]
    for copy in copies:
        copy.start()
    for shift, bc in ((0, bc0), (1, bc1), (2, bc2), (3, bc3)):
        x = lax.rem(place[2] + shift, 4)
        for k in range(4):
            yh = lax.rem(place[3] + k // 2, 2)
            core = lax.rem(place[4] + k % 2, 2)
            pieces_ref[(x * 2 + yh) * 2 + core] = bc[k]
    pieces = [pieces_ref[t] for t in range(16)]
    pieces = [p[:, :32].astype(F32) + p[:, 64:96].astype(F32) for p in pieces]
    b = jnp.concatenate(pieces[:8], 1)
    c = jnp.concatenate(pieces[8:], 1)
    b1, b2, c1, c2 = b[:rows], b[rows:], c[:rows], c[rows:]
    lane = lax.broadcasted_iota(jnp.int32, dots.shape, 1)
    b11 = jnp.sum(b1 * c1, axis=1, keepdims=True)
    b12 = jnp.sum(b1 * c2, axis=1, keepdims=True)
    b22 = jnp.sum(b2 * c2, axis=1, keepdims=True)
    dots[...] = jnp.where(lane == 0, b11, jnp.where(lane == 1, b12, b22))
    cmat[...] = jnp.zeros_like(cmat)
    for k, v in enumerate((c1, c2)):
        v = v * SCALE
        hi = v.astype(BF).astype(F32)
        cmat[:, 2 * k, :] = hi
        cmat[:, 2 * k + 1, :] = v - hi
    for k in range(chunks):
        copies[k].wait()
        for r in range(k * step, (k + 1) * step):
            m = held[r].reshape(s.shape[1] * s.shape[2], s.shape[3])
            out[r] = nt(cmat[r].astype(BF), m)


def decode_kernel(*refs):
    parts, (small, dots, g, bias, rate, skip, gain, out) = refs[:8], refs[8:]
    heads = bias.shape[1]
    inner = gain.shape[1]
    half = parts[0].shape[0] // 2
    total = parts[0][...].astype(F32)
    for part in parts[1:]:
        total = total + part[...].astype(F32)
    x_pre = total[:, :inner]
    z_pre = total[:, inner:]
    pick = (
        lax.broadcasted_iota(jnp.int32, (heads, inner), 0)
        == lax.broadcasted_iota(jnp.int32, (heads, inner), 1) // (inner // heads)
    ).astype(F32)
    expand = functools.partial(
        jnp.dot, preferred_element_type=F32, precision=lax.Precision.HIGHEST
    )
    dt_pre = expand(small[:, 32 : 32 + heads], pick)
    bias_e = expand(bias[...], pick)
    rate_e = expand(rate[...], pick)
    skip_e = expand(skip[...], pick)
    pre = dt_pre + bias_e
    dt = jnp.maximum(pre, 0.0) + jnp.log1p(jnp.exp(-jnp.abs(pre)))
    decay = jnp.exp(-dt * rate_e)
    inputs = x_pre * jax.nn.sigmoid(x_pre)
    upd = dt * inputs
    gate = z_pre * jax.nn.sigmoid(z_pre)
    b11 = dots[:, 0:1]
    b12 = dots[:, 1:2]
    b22 = dots[:, 2:3]
    gs = g[...]
    g1 = gs[:, 0, :] + gs[:, 1, :]
    g2 = gs[:, 2, :] + gs[:, 3, :]
    d1, d2 = decay[:half], decay[half:]
    u1, u2 = upd[:half], upd[half:]
    read1 = (d1 * g1) * (1.0 / SCALE) + u1 * b11 + skip_e * inputs[:half]
    read2 = d2 * ((d1 * g2) * (1.0 / SCALE) + u1 * b12) + u2 * b22 + skip_e * inputs[half:]
    lim = 1e30
    gg1 = jnp.clip(read1 * gate[:half] * gain[...], -lim, lim)
    gg2 = jnp.clip(read2 * gate[half:] * gain[...], -lim, lim)
    out[...] = jnp.concatenate([gg1, gg2], 0).astype(BF)


def output_kernel(place, mine, other, gain, own, r1, l1, r2, l2, r3, l3, r4, l4, keep, send):
    same = place[0]
    z = place[1]
    groups, rows, _ = keep.shape
    m = mine[...]
    o = other[...]
    v = jnp.concatenate([jnp.where(same == 1, m, o), jnp.where(same == 1, o, m)], 0)
    raw = v.astype(F32) / gain[...]
    ss = jnp.sum(raw * raw, axis=1, keepdims=True)
    hi = ss.astype(BF).astype(F32)
    lane = lax.broadcasted_iota(jnp.int32, (2 * rows, 64), 1)
    tail = jnp.where(lane == 0, hi, jnp.where(lane == 1, ss - hi, 0.0))
    order = ((0, own), (7, r1), (1, l1), (6, r2), (2, l2), (5, r3), (3, l3), (4, None))
    for shift, w in order:
        w = jnp.concatenate([r4[...], l4[...]], 0) if w is None else w[...]
        block = jnp.concatenate([nt(v, w), tail], 1)
        at = lax.rem(z + shift, groups)
        keep[at] = block[:rows]
        send[at] = block[rows:].astype(BF)


def pair_kernel(keep, got, out):
    total = keep[...] + got[...].astype(F32)
    cols = out.shape[2] - 64
    lane = lax.broadcasted_iota(jnp.int32, total.shape, 2)
    ss = total[:, :, cols : cols + 1] + total[:, :, cols + 1 : cols + 2]
    hi = ss.astype(BF).astype(F32)
    total = jnp.where(lane == cols, hi, jnp.where(lane == cols + 1, ss - hi, total))
    out[...] = total.astype(BF)


def reduce_kernel(part, out, *, count):
    total = part[0].astype(F32)
    for k in range(1, part.shape[0]):
        total = total + part[k].astype(F32)
    cols = out.shape[1]
    ss = total[:, cols : cols + 1] + total[:, cols + 1 : cols + 2]
    out[...] = (total[:, :cols] * lax.rsqrt(ss / count + 1e-05)).astype(BF)


def per_device(
    token_ids,
    row_counts,
    code_table,
    x_weight,
    z_weight,
    dt_weight,
    bc_weight,
    dt_bias,
    head_rate,
    skip_gain,
    norm_gain,
    out_weight,
    ssm_state,
):
    rows = token_ids.shape[1]
    heads = dt_bias.shape[0]
    inner = x_weight.shape[1]
    wide = code_table.shape[1]
    y = lax.axis_index("yl")
    core = lax.axis_index("core")
    swap = []
    for z in range(8):
        for yy in range(2):
            for w in range(8):
                for c in range(2):
                    swap.append(((z * 2 + yy) * 16 + w * 2 + c, (w * 2 + yy) * 16 + z * 2 + c))
    pair = [(0, 1), (1, 0)]

    gain = norm_gain.reshape(1, inner)
    right = [(i, (i + 1) % 8) for i in range(8)]
    left = [(i, (i + 7) % 8) for i in range(8)]
    out_own = out_weight.T
    ring_r = [out_own]
    ring_l = [out_own]
    for _ in range(1, 4):
        ring_r.append(lax.ppermute(ring_r[-1], "z", right))
        ring_l.append(lax.ppermute(ring_l[-1], "z", left))
    far_r = lax.ppermute(ring_r[3][: wide // 2], "z", right)
    far_l = lax.ppermute(ring_l[3][wide // 2 :], "z", left)
    x_oth = lax.ppermute(x_weight, "yl", pair)
    z_oth = lax.ppermute(z_weight, "yl", pair)
    small_own = jnp.concatenate(
        [bc_weight.T, dt_weight.T, jnp.zeros((64 - 32 - heads, wide), BF)], 0
    )
    small_oth = lax.ppermute(small_own, "yl", pair)

    flat_ids = token_ids.reshape(-1)
    codes = jnp.arange(code_table.shape[0], dtype=jnp.int32)
    one_hot = (flat_ids[:, None] == codes[None, :]).astype(BF)
    own_embed = jnp.dot(one_hot, code_table, preferred_element_type=F32).astype(BF)
    moved = lax.ppermute(own_embed, ALL, swap)
    e_own = lax.all_to_all(
        jnp.broadcast_to(moved[None], (8,) + moved.shape), ("x", "yh"), 0, 0
    ).reshape(8 * 2 * rows, wide)
    e_oth = lax.ppermute(e_own, "core", pair)
    place = jnp.stack(
        [(y == core).astype(jnp.int32), lax.axis_index("z"), lax.axis_index("x"), lax.axis_index("yh"), core]
    )
    part_small = call(
        project_small_kernel,
        jax.ShapeDtypeStruct((8, 2 * rows, 128), BF),
        (place, e_own, e_oth, small_own, small_oth),
        in_smem=1,
        flops=2 * 16 * rows * 2 * wide * 128,
    )
    part_small = lax.all_to_all(part_small, "z", 0, 0)
    blocks = call(
        project_kernel,
        tuple(jax.ShapeDtypeStruct((2 * rows, 2 * inner), BF) for _ in range(8)),
        (place, e_own, e_oth, x_weight, x_oth, z_weight, z_oth),
        in_specs=[pl.BlockSpec(memory_space=pltpu.SMEM)]
        + [pl.BlockSpec(memory_space=pltpu.VMEM)] * 2
        + [pl.BlockSpec(memory_space=pl.ANY)] * 4,
        out_specs=tuple(pl.BlockSpec(memory_space=pl.ANY) for _ in range(8)),
        scratch=[
            pltpu.VMEM((16 * rows, 2 * wide), BF),
            pltpu.VMEM((2, 2 * wide, inner), BF),
            pltpu.VMEM((2, 8, 2 * rows, inner), BF),
            pltpu.SemaphoreType.DMA((20,)),
        ],
        limit=PROJECT_LIMIT,
        flops=2 * 16 * rows * 2 * wide * 2 * inner,
    )
    parts = [blocks[0]]
    for k in SHIFTS:
        parts.append(lax.ppermute(blocks[k], "z", [(i, (i + k) % 8) for i in range(8)]))
    bc, small = call(
        small_kernel,
        (jax.ShapeDtypeStruct((2 * rows, 128), BF), jax.ShapeDtypeStruct((2 * rows, 64), F32)),
        (part_small,),
    )
    bc2 = jnp.stack([bc, lax.ppermute(bc, "core", pair)])
    bc4 = jnp.concatenate([bc2, lax.ppermute(bc2, "yh", pair)], 0)
    bc_all = [bc4]
    for k in (1, 2, 3):
        bc_all.append(lax.ppermute(bc4, "x", [((i + k) % 4, i) for i in range(4)]))
    g, dots = call(
        state_kernel,
        (jax.ShapeDtypeStruct((rows, 8, inner), F32), jax.ShapeDtypeStruct((rows, 128), F32)),
        (place, *bc_all, ssm_state),
        in_specs=[pl.BlockSpec(memory_space=pltpu.SMEM)]
        + [pl.BlockSpec(memory_space=pltpu.VMEM)] * 4
        + [pl.BlockSpec(memory_space=pl.ANY)],
        out_specs=(pl.BlockSpec(memory_space=pltpu.VMEM), pl.BlockSpec(memory_space=pltpu.VMEM)),
        scratch=[
            pltpu.VMEM((rows, 8, 256), F32),
            pltpu.VMEM((16, 2 * rows, 128), BF),
            pltpu.VMEM(ssm_state.shape, BF),
            pltpu.SemaphoreType.DMA((8,)),
        ],
        limit=STATE_LIMIT,
        flops=2 * 8 * rows * inner * 256,
    )
    gg = call(
        decode_kernel,
        jax.ShapeDtypeStruct((2 * rows, inner), BF),
        (
            *parts,
            small,
            dots,
            g,
            dt_bias.reshape(1, heads),
            head_rate.reshape(1, heads),
            skip_gain.reshape(1, heads),
            gain,
        ),
    )
    gg_oth = lax.ppermute(gg, "yl", pair)
    keep, send = call(
        output_kernel,
        (
            jax.ShapeDtypeStruct((8, 2 * rows, wide + 64), F32),
            jax.ShapeDtypeStruct((8, 2 * rows, wide + 64), BF),
        ),
        (
            place,
            gg,
            gg_oth,
            gain,
            out_own,
            ring_r[1],
            ring_l[1],
            ring_r[2],
            ring_l[2],
            ring_r[3],
            ring_l[3],
            far_r,
            far_l,
        ),
        in_smem=1,
        flops=2 * 4 * rows * inner * 8 * wide,
    )
    got = lax.ppermute(send, "core", pair)
    paired = call(pair_kernel, jax.ShapeDtypeStruct((8, 2 * rows, wide + 64), BF), (keep, got))
    partial_out = lax.all_to_all(paired, ("x", "yh"), 0, 0)
    mine = call(
        functools.partial(reduce_kernel, count=float(16 * inner)),
        jax.ShapeDtypeStruct((2 * rows, wide), BF),
        (partial_out,),
    )
    back = lax.ppermute(mine, ("yl", "core"), [(0, 0), (1, 2), (2, 1), (3, 3)])
    result = (own_embed.astype(F32) + back.astype(F32)).reshape(2, rows, wide)
    live = jnp.arange(rows, dtype=jnp.int32) < row_counts[0]
    return jnp.where(live[None, :, None], result, 0.0).astype(BF)


def solution(mesh):
    fine = Mesh(mesh.devices.reshape(8, 2, 4, 2, 2), ALL)
    return jax.shard_map(
        per_device,
        mesh=fine,
        in_specs=(
            P(None, GROUP),
            P(GROUP),
            P(None, TP),
            P(GROUP, TP),
            P(GROUP, TP),
            P(GROUP, TP),
            P(GROUP, TP),
            P(TP),
            P(TP),
            P(TP),
            P(TP),
            P(TP, GROUP),
            P(GROUP, TP, None, None),
        ),
        out_specs=P(None, GROUP, TP),
        check_vma=False,
    )
```

```python
import functools

import jax
import jax.numpy as jnp
from jax import lax
from jax.experimental import pallas as pl
from jax.experimental.pallas import tpu as pltpu
from jax.sharding import Mesh
from jax.sharding import PartitionSpec as P


BF = jnp.bfloat16
F32 = jnp.float32
SCALE = 2.0**-20
GROUP = ("z", "yl")
TP = ("x", "yh", "core")
ALL = GROUP + TP
VMEM_LIMIT = 14 * 1024 * 1024
PROJECT_LIMIT = 58 * 1024 * 1024
STATE_LIMIT = 52 * 1024 * 1024

SHIFTS = (4, 3, 5, 2, 6, 1, 7)


def nt(a, b):
    return lax.dot_general(a, b, (((1,), (1,)), ((), ())), preferred_element_type=F32)


def nn(a, b):
    return jnp.dot(a, b, preferred_element_type=F32)


def call(body, out_shape, args, in_smem=0, flops=1 << 20, grid=None, in_specs=None, out_specs=None, scratch=(), limit=VMEM_LIMIT):
    if in_specs is None:
        in_specs = [pl.BlockSpec(memory_space=pltpu.SMEM)] * in_smem + [
            pl.BlockSpec(memory_space=pltpu.VMEM)
        ] * (len(args) - in_smem)
        out_specs = jax.tree.map(lambda _: pl.BlockSpec(memory_space=pltpu.VMEM), out_shape)
    kwargs = {} if grid is None else {"grid": grid}
    return pl.pallas_call(
        body,
        out_shape=out_shape,
        in_specs=in_specs,
        out_specs=out_specs,
        scratch_shapes=scratch,
        compiler_params=pltpu.CompilerParams(vmem_limit_bytes=limit),
        cost_estimate=pl.CostEstimate(flops=flops, bytes_accessed=1 << 20, transcendentals=0),
        **kwargs,
    )(*args)


def split2(v):
    hi = v.astype(BF)
    return hi, (v - hi.astype(F32)).astype(BF)


def project_small_kernel(flag, e_own, e_oth, s_own, s_oth, out):
    groups, rows, width = out.shape

    def run(ea, eb):
        ps = nt(ea[...], s_own[...]) + nt(eb[...], s_oth[...])
        hi, lo = split2(ps)
        out[...] = jnp.concatenate([hi, lo], 1).reshape(groups, rows, width)

    @pl.when(flag[0] == 1)
    def _():
        run(e_own, e_oth)

    @pl.when(flag[0] == 0)
    def _():
        run(e_oth, e_own)


def project_kernel(place, e_own, e_oth, x_own, x_oth, z_own, z_oth, *refs):
    outs, (both, held, done, sems) = refs[:8], refs[8:]
    depth, inner = x_own.shape
    groups, rows = len(outs), outs[0].shape[0]
    sources = ((x_own, x_oth), (z_own, z_oth))
    loads = [
        [
            pltpu.make_async_copy(ref, held.at[k, pl.ds(j * depth, depth)], sems.at[2 * k + j])
            for j, ref in enumerate(refs)
        ]
        for k, refs in enumerate(sources)
    ]
    for pair in loads:
        for load in pair:
            load.start()

    def fill(ea, eb):
        both[:, :depth] = ea[...]
        both[:, depth:] = eb[...]

    @pl.when(place[0] == 1)
    def _():
        fill(e_own, e_oth)

    @pl.when(place[0] == 0)
    def _():
        fill(e_oth, e_own)

    stores = []
    for k in range(2):
        for load in loads[k]:
            load.wait()
        total = nn(both[...], held[k])
        done[k] = total.astype(BF).reshape(groups, rows, inner)
        for j in range(groups):
            stores.append(
                pltpu.make_async_copy(
                    done.at[k, lax.rem(place[1] + j, groups)],
                    outs[j].at[:, pl.ds(k * inner, inner)],
                    sems.at[4 + k * groups + j],
                )
            )
            stores[-1].start()
    for store in stores:
        store.wait()


def small_kernel(part, bc, small):
    total = part[0].astype(F32)
    for k in range(1, part.shape[0]):
        total = total + part[k].astype(F32)
    total = total[:, :64] + total[:, 64:]
    hi, lo = split2(total)
    bc[...] = jnp.concatenate([hi, lo], 1)
    small[...] = total


def state_kernel(place, bc0, bc1, bc2, bc3, s, out, dots, cmat, pieces_ref, held, sems):
    rows = cmat.shape[0]
    chunks = sems.shape[0]
    step = rows // chunks
    copies = [
        pltpu.make_async_copy(
            s.at[pl.ds(k * step, step)], held.at[pl.ds(k * step, step)], sems.at[k]
        )
        for k in range(chunks)
    ]
    for copy in copies:
        copy.start()
    for shift, bc in ((0, bc0), (1, bc1), (2, bc2), (3, bc3)):
        x = lax.rem(place[0] + shift, 4)
        for k in range(4):
            yh = lax.rem(place[1] + k // 2, 2)
            core = lax.rem(place[2] + k % 2, 2)
            pieces_ref[(x * 2 + yh) * 2 + core] = bc[k]
    pieces = [pieces_ref[t] for t in range(16)]
    pieces = [p[:, :32].astype(F32) + p[:, 64:96].astype(F32) for p in pieces]
    b = jnp.concatenate(pieces[:8], 1)
    c = jnp.concatenate(pieces[8:], 1)
    b1, b2, c1, c2 = b[:rows], b[rows:], c[:rows], c[rows:]
    lane = lax.broadcasted_iota(jnp.int32, dots.shape, 1)
    b11 = jnp.sum(b1 * c1, axis=1, keepdims=True)
    b12 = jnp.sum(b1 * c2, axis=1, keepdims=True)
    b22 = jnp.sum(b2 * c2, axis=1, keepdims=True)
    dots[...] = jnp.where(lane == 0, b11, jnp.where(lane == 1, b12, b22))
    cmat[...] = jnp.zeros_like(cmat)
    for k, v in enumerate((c1, c2)):
        v = v * SCALE
        hi = v.astype(BF).astype(F32)
        cmat[:, 2 * k, :] = hi
        cmat[:, 2 * k + 1, :] = v - hi
    for k in range(chunks):
        copies[k].wait()
        for r in range(k * step, (k + 1) * step):
            m = held[r].reshape(s.shape[1] * s.shape[2], s.shape[3])
            out[r] = nt(cmat[r].astype(BF), m)


def decode_kernel(*refs):
    parts, (small, dots, g, bias, rate, skip, gain, out) = refs[:8], refs[8:]
    heads = bias.shape[1]
    inner = gain.shape[1]
    half = parts[0].shape[0] // 2
    total = parts[0][...].astype(F32)
    for part in parts[1:]:
        total = total + part[...].astype(F32)
    x_pre = total[:, :inner]
    z_pre = total[:, inner:]
    pick = (
        lax.broadcasted_iota(jnp.int32, (heads, inner), 0)
        == lax.broadcasted_iota(jnp.int32, (heads, inner), 1) // (inner // heads)
    ).astype(F32)
    expand = functools.partial(
        jnp.dot, preferred_element_type=F32, precision=lax.Precision.HIGHEST
    )
    dt_pre = expand(small[:, 32 : 32 + heads], pick)
    bias_e = expand(bias[...], pick)
    rate_e = expand(rate[...], pick)
    skip_e = expand(skip[...], pick)
    pre = dt_pre + bias_e
    dt = jnp.maximum(pre, 0.0) + jnp.log1p(jnp.exp(-jnp.abs(pre)))
    decay = jnp.exp(-dt * rate_e)
    inputs = x_pre * jax.nn.sigmoid(x_pre)
    upd = dt * inputs
    gate = z_pre * jax.nn.sigmoid(z_pre)
    b11 = dots[:, 0:1]
    b12 = dots[:, 1:2]
    b22 = dots[:, 2:3]
    gs = g[...]
    g1 = gs[:, 0, :] + gs[:, 1, :]
    g2 = gs[:, 2, :] + gs[:, 3, :]
    d1, d2 = decay[:half], decay[half:]
    u1, u2 = upd[:half], upd[half:]
    read1 = (d1 * g1) * (1.0 / SCALE) + u1 * b11 + skip_e * inputs[:half]
    read2 = d2 * ((d1 * g2) * (1.0 / SCALE) + u1 * b12) + u2 * b22 + skip_e * inputs[half:]
    lim = 1e30
    gg1 = jnp.clip(read1 * gate[:half] * gain[...], -lim, lim)
    gg2 = jnp.clip(read2 * gate[half:] * gain[...], -lim, lim)
    out[...] = jnp.concatenate([gg1, gg2], 0).astype(BF)


def output_kernel(place, mine, other, gain, own, r1, l1, r2, l2, r3, l3, r4, l4, keep, send):
    z = place[0]
    same = place[1]
    groups, rows, _ = keep.shape
    m = mine[...]
    o = other[...]
    v = jnp.concatenate([jnp.where(same == 1, m, o), jnp.where(same == 1, o, m)], 0)
    raw = v.astype(F32) / gain[...]
    ss = jnp.sum(raw * raw, axis=1, keepdims=True)
    hi = ss.astype(BF).astype(F32)
    lane = lax.broadcasted_iota(jnp.int32, (2 * rows, 64), 1)
    tail = jnp.where(lane == 0, hi, jnp.where(lane == 1, ss - hi, 0.0))
    order = ((0, own), (7, r1), (1, l1), (6, r2), (2, l2), (5, r3), (3, l3), (4, None))
    for shift, w in order:
        w = jnp.concatenate([r4[...], l4[...]], 0) if w is None else w[...]
        block = jnp.concatenate([nt(v, w), tail], 1)
        at = lax.rem(z + shift, groups)
        keep[at] = block[:rows]
        send[at] = block[rows:].astype(BF)


def pair_kernel(keep, got, out):
    total = keep[...] + got[...].astype(F32)
    cols = out.shape[2] - 64
    lane = lax.broadcasted_iota(jnp.int32, total.shape, 2)
    ss = total[:, :, cols : cols + 1] + total[:, :, cols + 1 : cols + 2]
    hi = ss.astype(BF).astype(F32)
    total = jnp.where(lane == cols, hi, jnp.where(lane == cols + 1, ss - hi, total))
    out[...] = total.astype(BF)


def reduce_kernel(part, out, *, count):
    total = part[0].astype(F32)
    for k in range(1, part.shape[0]):
        total = total + part[k].astype(F32)
    cols = out.shape[1]
    ss = total[:, cols : cols + 1] + total[:, cols + 1 : cols + 2]
    out[...] = (total[:, :cols] * lax.rsqrt(ss / count + 1e-05)).astype(BF)


def per_device(
    token_ids,
    row_counts,
    code_table,
    x_weight,
    z_weight,
    dt_weight,
    bc_weight,
    dt_bias,
    head_rate,
    skip_gain,
    norm_gain,
    out_weight,
    ssm_state,
):
    rows = token_ids.shape[1]
    heads = dt_bias.shape[0]
    inner = x_weight.shape[1]
    wide = code_table.shape[1]
    y = lax.axis_index("yl")
    core = lax.axis_index("core")
    swap = []
    for z in range(8):
        for yy in range(2):
            for w in range(8):
                for c in range(2):
                    swap.append(((z * 2 + yy) * 16 + w * 2 + c, (w * 2 + yy) * 16 + z * 2 + c))
    pair = [(0, 1), (1, 0)]

    gain = norm_gain.reshape(1, inner)
    right = [(i, (i + 1) % 8) for i in range(8)]
    left = [(i, (i + 7) % 8) for i in range(8)]
    out_own = out_weight.T
    ring_r = [out_own]
    ring_l = [out_own]
    for _ in range(1, 4):
        ring_r.append(lax.ppermute(ring_r[-1], "z", right))
        ring_l.append(lax.ppermute(ring_l[-1], "z", left))
    far_r = lax.ppermute(ring_r[3][: wide // 2], "z", right)
    far_l = lax.ppermute(ring_l[3][wide // 2 :], "z", left)
    x_oth = lax.ppermute(x_weight, "yl", pair)
    z_oth = lax.ppermute(z_weight, "yl", pair)
    small_own = jnp.concatenate(
        [bc_weight.T, dt_weight.T, jnp.zeros((64 - 32 - heads, wide), BF)], 0
    )
    small_oth = lax.ppermute(small_own, "yl", pair)

    flat_ids = token_ids.reshape(-1)
    codes = jnp.arange(code_table.shape[0], dtype=jnp.int32)
    one_hot = (flat_ids[:, None] == codes[None, :]).astype(BF)
    own_embed = jnp.dot(one_hot, code_table, preferred_element_type=F32).astype(BF)
    moved = lax.ppermute(own_embed, ALL, swap)
    e_own = lax.all_to_all(
        jnp.broadcast_to(moved[None], (8,) + moved.shape), ("x", "yh"), 0, 0
    ).reshape(8 * 2 * rows, wide)
    e_oth = lax.ppermute(e_own, "core", pair)
    same = (y == core).astype(jnp.int32)
    z = lax.axis_index("z")
    place = jnp.stack([same, z])
    plane = jnp.stack([lax.axis_index("x"), lax.axis_index("yh"), core])
    turned = jnp.stack([z, same])
    part_small = call(
        project_small_kernel,
        jax.ShapeDtypeStruct((8, 2 * rows, 128), BF),
        (place, e_own, e_oth, small_own, small_oth),
        in_smem=1,
        flops=2 * 16 * rows * 2 * wide * 128,
    )
    part_small = lax.all_to_all(part_small, "z", 0, 0)
    blocks = call(
        project_kernel,
        tuple(jax.ShapeDtypeStruct((2 * rows, 2 * inner), BF) for _ in range(8)),
        (place, e_own, e_oth, x_weight, x_oth, z_weight, z_oth),
        in_specs=[pl.BlockSpec(memory_space=pltpu.SMEM)]
        + [pl.BlockSpec(memory_space=pltpu.VMEM)] * 2
        + [pl.BlockSpec(memory_space=pl.ANY)] * 4,
        out_specs=tuple(pl.BlockSpec(memory_space=pl.ANY) for _ in range(8)),
        scratch=[
            pltpu.VMEM((16 * rows, 2 * wide), BF),
            pltpu.VMEM((2, 2 * wide, inner), BF),
            pltpu.VMEM((2, 8, 2 * rows, inner), BF),
            pltpu.SemaphoreType.DMA((20,)),
        ],
        limit=PROJECT_LIMIT,
        flops=2 * 16 * rows * 2 * wide * 2 * inner,
    )
    parts = [blocks[0]]
    for k in SHIFTS:
        parts.append(lax.ppermute(blocks[k], "z", [(i, (i + k) % 8) for i in range(8)]))
    bc, small = call(
        small_kernel,
        (jax.ShapeDtypeStruct((2 * rows, 128), BF), jax.ShapeDtypeStruct((2 * rows, 64), F32)),
        (part_small,),
    )
    bc2 = jnp.stack([bc, lax.ppermute(bc, "core", pair)])
    bc4 = jnp.concatenate([bc2, lax.ppermute(bc2, "yh", pair)], 0)
    bc_all = [bc4]
    for k in (1, 2, 3):
        bc_all.append(lax.ppermute(bc4, "x", [((i + k) % 4, i) for i in range(4)]))
    g, dots = call(
        state_kernel,
        (jax.ShapeDtypeStruct((rows, 8, inner), F32), jax.ShapeDtypeStruct((rows, 128), F32)),
        (plane, *bc_all, ssm_state),
        in_specs=[pl.BlockSpec(memory_space=pltpu.SMEM)]
        + [pl.BlockSpec(memory_space=pltpu.VMEM)] * 4
        + [pl.BlockSpec(memory_space=pl.ANY)],
        out_specs=(pl.BlockSpec(memory_space=pltpu.VMEM), pl.BlockSpec(memory_space=pltpu.VMEM)),
        scratch=[
            pltpu.VMEM((rows, 8, 256), F32),
            pltpu.VMEM((16, 2 * rows, 128), BF),
            pltpu.VMEM(ssm_state.shape, BF),
            pltpu.SemaphoreType.DMA((8,)),
        ],
        limit=STATE_LIMIT,
        flops=2 * 8 * rows * inner * 256,
    )
    gg = call(
        decode_kernel,
        jax.ShapeDtypeStruct((2 * rows, inner), BF),
        (
            *parts,
            small,
            dots,
            g,
            dt_bias.reshape(1, heads),
            head_rate.reshape(1, heads),
            skip_gain.reshape(1, heads),
            gain,
        ),
    )
    gg_oth = lax.ppermute(gg, "yl", pair)
    keep, send = call(
        output_kernel,
        (
            jax.ShapeDtypeStruct((8, 2 * rows, wide + 64), F32),
            jax.ShapeDtypeStruct((8, 2 * rows, wide + 64), BF),
        ),
        (
            turned,
            gg,
            gg_oth,
            gain,
            out_own,
            ring_r[1],
            ring_l[1],
            ring_r[2],
            ring_l[2],
            ring_r[3],
            ring_l[3],
            far_r,
            far_l,
        ),
        in_smem=1,
        flops=2 * 4 * rows * inner * 8 * wide,
    )
    got = lax.ppermute(send, "core", pair)
    paired = call(pair_kernel, jax.ShapeDtypeStruct((8, 2 * rows, wide + 64), BF), (keep, got))
    partial_out = lax.all_to_all(paired, ("x", "yh"), 0, 0)
    mine = call(
        functools.partial(reduce_kernel, count=float(16 * inner)),
        jax.ShapeDtypeStruct((2 * rows, wide), BF),
        (partial_out,),
    )
    back = lax.ppermute(mine, ("yl", "core"), [(0, 0), (1, 2), (2, 1), (3, 3)])
    result = (own_embed.astype(F32) + back.astype(F32)).reshape(2, rows, wide)
    live = jnp.arange(rows, dtype=jnp.int32) < row_counts[0]
    return jnp.where(live[None, :, None], result, 0.0).astype(BF)


def solution(mesh):
    fine = Mesh(mesh.devices.reshape(8, 2, 4, 2, 2), ALL)
    return jax.shard_map(
        per_device,
        mesh=fine,
        in_specs=(
            P(None, GROUP),
            P(GROUP),
            P(None, TP),
            P(GROUP, TP),
            P(GROUP, TP),
            P(GROUP, TP),
            P(GROUP, TP),
            P(TP),
            P(TP),
            P(TP),
            P(TP),
            P(TP, GROUP),
            P(GROUP, TP, None, None),
        ),
        out_specs=P(None, GROUP, TP),
        check_vma=False,
    )
```

```python
import functools

import jax
import jax.numpy as jnp
from jax import lax
from jax.experimental import pallas as pl
from jax.experimental.pallas import tpu as pltpu
from jax.sharding import Mesh
from jax.sharding import PartitionSpec as P


BF = jnp.bfloat16
F32 = jnp.float32
SCALE = 2.0**-20
GROUP = ("z", "yl")
TP = ("x", "yh", "core")
ALL = GROUP + TP
VMEM_LIMIT = 14 * 1024 * 1024
PROJECT_LIMIT = 58 * 1024 * 1024
STATE_LIMIT = 52 * 1024 * 1024

SHIFTS = (3, 2, 5, 6, 1, 7)


def nt(a, b):
    return lax.dot_general(a, b, (((1,), (1,)), ((), ())), preferred_element_type=F32)


def nn(a, b):
    return jnp.dot(a, b, preferred_element_type=F32)


def call(body, out_shape, args, in_smem=0, flops=1 << 20, grid=None, in_specs=None, out_specs=None, scratch=(), limit=VMEM_LIMIT):
    if in_specs is None:
        in_specs = [pl.BlockSpec(memory_space=pltpu.SMEM)] * in_smem + [
            pl.BlockSpec(memory_space=pltpu.VMEM)
        ] * (len(args) - in_smem)
        out_specs = jax.tree.map(lambda _: pl.BlockSpec(memory_space=pltpu.VMEM), out_shape)
    kwargs = {} if grid is None else {"grid": grid}
    return pl.pallas_call(
        body,
        out_shape=out_shape,
        in_specs=in_specs,
        out_specs=out_specs,
        scratch_shapes=scratch,
        compiler_params=pltpu.CompilerParams(vmem_limit_bytes=limit),
        cost_estimate=pl.CostEstimate(flops=flops, bytes_accessed=1 << 20, transcendentals=0),
        **kwargs,
    )(*args)


def split2(v):
    hi = v.astype(BF)
    return hi, (v - hi.astype(F32)).astype(BF)


def project_small_kernel(flag, e_own, e_oth, s_own, s_oth, out):
    groups, rows, width = out.shape

    def run(ea, eb):
        ps = nt(ea[...], s_own[...]) + nt(eb[...], s_oth[...])
        hi, lo = split2(ps)
        out[...] = jnp.concatenate([hi, lo], 1).reshape(groups, rows, width)

    @pl.when(flag[0] == 1)
    def _():
        run(e_own, e_oth)

    @pl.when(flag[0] == 0)
    def _():
        run(e_oth, e_own)


def project_kernel(place, e_own, e_oth, x_own, x_oth, z_own, z_oth, *refs):
    outs, (both, held, done, sems) = refs[:8], refs[8:]
    depth, inner = x_own.shape
    groups, rows = len(outs), outs[0].shape[0]
    sources = ((x_own, x_oth), (z_own, z_oth))
    loads = [
        [
            pltpu.make_async_copy(ref, held.at[k, pl.ds(j * depth, depth)], sems.at[2 * k + j])
            for j, ref in enumerate(refs)
        ]
        for k, refs in enumerate(sources)
    ]
    for pair in loads:
        for load in pair:
            load.start()

    def fill(ea, eb):
        both[:, :depth] = ea[...]
        both[:, depth:] = eb[...]

    @pl.when(place[0] == 1)
    def _():
        fill(e_own, e_oth)

    @pl.when(place[0] == 0)
    def _():
        fill(e_oth, e_own)

    stores = []
    for k in range(2):
        for load in loads[k]:
            load.wait()
        total = nn(both[...], held[k])
        done[k] = total.astype(BF).reshape(groups, rows, inner)
        for j in range(groups):
            stores.append(
                pltpu.make_async_copy(
                    done.at[k, lax.rem(place[1] + j, groups)],
                    outs[j].at[:, pl.ds(k * inner, inner)],
                    sems.at[4 + k * groups + j],
                )
            )
            stores[-1].start()
    for store in stores:
        store.wait()


def join_kernel(own, passed, out):
    out[...] = (own[...].astype(F32) + passed[...].astype(F32)).astype(BF)


def small_kernel(part, bc, small):
    total = part[0].astype(F32)
    for k in range(1, part.shape[0]):
        total = total + part[k].astype(F32)
    total = total[:, :64] + total[:, 64:]
    hi, lo = split2(total)
    bc[...] = jnp.concatenate([hi, lo], 1)
    small[...] = total


def state_kernel(place, bc0, bc1, bc2, bc3, s, out, dots, cmat, pieces_ref, held, sems):
    rows = cmat.shape[0]
    chunks = sems.shape[0]
    step = rows // chunks
    copies = [
        pltpu.make_async_copy(
            s.at[pl.ds(k * step, step)], held.at[pl.ds(k * step, step)], sems.at[k]
        )
        for k in range(chunks)
    ]
    for copy in copies:
        copy.start()
    for shift, bc in ((0, bc0), (1, bc1), (2, bc2), (3, bc3)):
        x = lax.rem(place[0] + shift, 4)
        for k in range(4):
            yh = lax.rem(place[1] + k // 2, 2)
            core = lax.rem(place[2] + k % 2, 2)
            pieces_ref[(x * 2 + yh) * 2 + core] = bc[k]
    pieces = [pieces_ref[t] for t in range(16)]
    pieces = [p[:, :32].astype(F32) + p[:, 64:96].astype(F32) for p in pieces]
    b = jnp.concatenate(pieces[:8], 1)
    c = jnp.concatenate(pieces[8:], 1)
    b1, b2, c1, c2 = b[:rows], b[rows:], c[:rows], c[rows:]
    lane = lax.broadcasted_iota(jnp.int32, dots.shape, 1)
    b11 = jnp.sum(b1 * c1, axis=1, keepdims=True)
    b12 = jnp.sum(b1 * c2, axis=1, keepdims=True)
    b22 = jnp.sum(b2 * c2, axis=1, keepdims=True)
    dots[...] = jnp.where(lane == 0, b11, jnp.where(lane == 1, b12, b22))
    cmat[...] = jnp.zeros_like(cmat)
    for k, v in enumerate((c1, c2)):
        v = v * SCALE
        hi = v.astype(BF).astype(F32)
        cmat[:, 2 * k, :] = hi
        cmat[:, 2 * k + 1, :] = v - hi
    for k in range(chunks):
        copies[k].wait()
        for r in range(k * step, (k + 1) * step):
            m = held[r].reshape(s.shape[1] * s.shape[2], s.shape[3])
            out[r] = nt(cmat[r].astype(BF), m)


def decode_kernel(*refs):
    parts, (small, dots, g, bias, rate, skip, gain, out) = refs[:7], refs[7:]
    heads = bias.shape[1]
    inner = gain.shape[1]
    half = parts[0].shape[0] // 2
    total = parts[0][...].astype(F32)
    for part in parts[1:]:
        total = total + part[...].astype(F32)
    x_pre = total[:, :inner]
    z_pre = total[:, inner:]
    pick = (
        lax.broadcasted_iota(jnp.int32, (heads, inner), 0)
        == lax.broadcasted_iota(jnp.int32, (heads, inner), 1) // (inner // heads)
    ).astype(F32)
    expand = functools.partial(
        jnp.dot, preferred_element_type=F32, precision=lax.Precision.HIGHEST
    )
    dt_pre = expand(small[:, 32 : 32 + heads], pick)
    bias_e = expand(bias[...], pick)
    rate_e = expand(rate[...], pick)
    skip_e = expand(skip[...], pick)
    pre = dt_pre + bias_e
    dt = jnp.maximum(pre, 0.0) + jnp.log1p(jnp.exp(-jnp.abs(pre)))
    decay = jnp.exp(-dt * rate_e)
    inputs = x_pre * jax.nn.sigmoid(x_pre)
    upd = dt * inputs
    gate = z_pre * jax.nn.sigmoid(z_pre)
    b11 = dots[:, 0:1]
    b12 = dots[:, 1:2]
    b22 = dots[:, 2:3]
    gs = g[...]
    g1 = gs[:, 0, :] + gs[:, 1, :]
    g2 = gs[:, 2, :] + gs[:, 3, :]
    d1, d2 = decay[:half], decay[half:]
    u1, u2 = upd[:half], upd[half:]
    read1 = (d1 * g1) * (1.0 / SCALE) + u1 * b11 + skip_e * inputs[:half]
    read2 = d2 * ((d1 * g2) * (1.0 / SCALE) + u1 * b12) + u2 * b22 + skip_e * inputs[half:]
    lim = 1e30
    gg1 = jnp.clip(read1 * gate[:half] * gain[...], -lim, lim)
    gg2 = jnp.clip(read2 * gate[half:] * gain[...], -lim, lim)
    out[...] = jnp.concatenate([gg1, gg2], 0).astype(BF)


def output_kernel(place, mine, other, gain, own, r1, l1, r2, l2, r3, l3, r4, l4, keep, send):
    z = place[0]
    same = place[1]
    groups, rows, _ = keep.shape
    m = mine[...]
    o = other[...]
    v = jnp.concatenate([jnp.where(same == 1, m, o), jnp.where(same == 1, o, m)], 0)
    raw = v.astype(F32) / gain[...]
    ss = jnp.sum(raw * raw, axis=1, keepdims=True)
    hi = ss.astype(BF).astype(F32)
    lane = lax.broadcasted_iota(jnp.int32, (2 * rows, 64), 1)
    tail = jnp.where(lane == 0, hi, jnp.where(lane == 1, ss - hi, 0.0))
    order = ((0, own), (7, r1), (1, l1), (6, r2), (2, l2), (5, r3), (3, l3), (4, None))
    for shift, w in order:
        w = jnp.concatenate([r4[...], l4[...]], 0) if w is None else w[...]
        block = jnp.concatenate([nt(v, w), tail], 1)
        at = lax.rem(z + shift, groups)
        keep[at] = block[:rows]
        send[at] = block[rows:].astype(BF)


def pair_kernel(keep, got, out):
    total = keep[...] + got[...].astype(F32)
    cols = out.shape[2] - 64
    lane = lax.broadcasted_iota(jnp.int32, total.shape, 2)
    ss = total[:, :, cols : cols + 1] + total[:, :, cols + 1 : cols + 2]
    hi = ss.astype(BF).astype(F32)
    total = jnp.where(lane == cols, hi, jnp.where(lane == cols + 1, ss - hi, total))
    out[...] = total.astype(BF)


def reduce_kernel(part, out, *, count):
    total = part[0].astype(F32)
    for k in range(1, part.shape[0]):
        total = total + part[k].astype(F32)
    cols = out.shape[1]
    ss = total[:, cols : cols + 1] + total[:, cols + 1 : cols + 2]
    out[...] = (total[:, :cols] * lax.rsqrt(ss / count + 1e-05)).astype(BF)


def per_device(
    token_ids,
    row_counts,
    code_table,
    x_weight,
    z_weight,
    dt_weight,
    bc_weight,
    dt_bias,
    head_rate,
    skip_gain,
    norm_gain,
    out_weight,
    ssm_state,
):
    rows = token_ids.shape[1]
    heads = dt_bias.shape[0]
    inner = x_weight.shape[1]
    wide = code_table.shape[1]
    y = lax.axis_index("yl")
    core = lax.axis_index("core")
    swap = []
    for z in range(8):
        for yy in range(2):
            for w in range(8):
                for c in range(2):
                    swap.append(((z * 2 + yy) * 16 + w * 2 + c, (w * 2 + yy) * 16 + z * 2 + c))
    pair = [(0, 1), (1, 0)]

    gain = norm_gain.reshape(1, inner)
    right = [(i, (i + 1) % 8) for i in range(8)]
    left = [(i, (i + 7) % 8) for i in range(8)]
    out_own = out_weight.T
    ring_r = [out_own]
    ring_l = [out_own]
    for _ in range(1, 4):
        ring_r.append(lax.ppermute(ring_r[-1], "z", right))
        ring_l.append(lax.ppermute(ring_l[-1], "z", left))
    far_r = lax.ppermute(ring_r[3][: wide // 2], "z", right)
    far_l = lax.ppermute(ring_l[3][wide // 2 :], "z", left)
    x_oth = lax.ppermute(x_weight, "yl", pair)
    z_oth = lax.ppermute(z_weight, "yl", pair)
    small_own = jnp.concatenate(
        [bc_weight.T, dt_weight.T, jnp.zeros((64 - 32 - heads, wide), BF)], 0
    )
    small_oth = lax.ppermute(small_own, "yl", pair)

    flat_ids = token_ids.reshape(-1)
    codes = jnp.arange(code_table.shape[0], dtype=jnp.int32)
    one_hot = (flat_ids[:, None] == codes[None, :]).astype(BF)
    own_embed = jnp.dot(one_hot, code_table, preferred_element_type=F32).astype(BF)
    moved = lax.ppermute(own_embed, ALL, swap)
    e_own = lax.all_to_all(
        jnp.broadcast_to(moved[None], (8,) + moved.shape), ("x", "yh"), 0, 0
    ).reshape(8 * 2 * rows, wide)
    e_oth = lax.ppermute(e_own, "core", pair)
    same = (y == core).astype(jnp.int32)
    z = lax.axis_index("z")
    place = jnp.stack([same, z])
    plane = jnp.stack([lax.axis_index("x"), lax.axis_index("yh"), core])
    turned = jnp.stack([z, same])
    part_small = call(
        project_small_kernel,
        jax.ShapeDtypeStruct((8, 2 * rows, 128), BF),
        (place, e_own, e_oth, small_own, small_oth),
        in_smem=1,
        flops=2 * 16 * rows * 2 * wide * 128,
    )
    part_small = lax.all_to_all(part_small, "z", 0, 0)
    blocks = call(
        project_kernel,
        tuple(jax.ShapeDtypeStruct((2 * rows, 2 * inner), BF) for _ in range(8)),
        (place, e_own, e_oth, x_weight, x_oth, z_weight, z_oth),
        in_specs=[pl.BlockSpec(memory_space=pltpu.SMEM)]
        + [pl.BlockSpec(memory_space=pltpu.VMEM)] * 2
        + [pl.BlockSpec(memory_space=pl.ANY)] * 4,
        out_specs=tuple(pl.BlockSpec(memory_space=pl.ANY) for _ in range(8)),
        scratch=[
            pltpu.VMEM((16 * rows, 2 * wide), BF),
            pltpu.VMEM((2, 2 * wide, inner), BF),
            pltpu.VMEM((2, 8, 2 * rows, inner), BF),
            pltpu.SemaphoreType.DMA((20,)),
        ],
        limit=PROJECT_LIMIT,
        flops=2 * 16 * rows * 2 * wide * 2 * inner,
    )
    blocks = list(blocks)
    passed = lax.ppermute(blocks[4], "z", left)
    blocks[5] = call(join_kernel, jax.ShapeDtypeStruct(blocks[5].shape, BF), (blocks[5], passed))
    parts = [blocks[0]]
    for k in SHIFTS:
        parts.append(lax.ppermute(blocks[k], "z", [(i, (i + k) % 8) for i in range(8)]))
    bc, small = call(
        small_kernel,
        (jax.ShapeDtypeStruct((2 * rows, 128), BF), jax.ShapeDtypeStruct((2 * rows, 64), F32)),
        (part_small,),
    )
    bc2 = jnp.stack([bc, lax.ppermute(bc, "core", pair)])
    bc4 = jnp.concatenate([bc2, lax.ppermute(bc2, "yh", pair)], 0)
    bc_all = [bc4]
    for k in (1, 2, 3):
        bc_all.append(lax.ppermute(bc4, "x", [((i + k) % 4, i) for i in range(4)]))
    g, dots = call(
        state_kernel,
        (jax.ShapeDtypeStruct((rows, 8, inner), F32), jax.ShapeDtypeStruct((rows, 128), F32)),
        (plane, *bc_all, ssm_state),
        in_specs=[pl.BlockSpec(memory_space=pltpu.SMEM)]
        + [pl.BlockSpec(memory_space=pltpu.VMEM)] * 4
        + [pl.BlockSpec(memory_space=pl.ANY)],
        out_specs=(pl.BlockSpec(memory_space=pltpu.VMEM), pl.BlockSpec(memory_space=pltpu.VMEM)),
        scratch=[
            pltpu.VMEM((rows, 8, 256), F32),
            pltpu.VMEM((16, 2 * rows, 128), BF),
            pltpu.VMEM(ssm_state.shape, BF),
            pltpu.SemaphoreType.DMA((8,)),
        ],
        limit=STATE_LIMIT,
        flops=2 * 8 * rows * inner * 256,
    )
    gg = call(
        decode_kernel,
        jax.ShapeDtypeStruct((2 * rows, inner), BF),
        (
            *parts,
            small,
            dots,
            g,
            dt_bias.reshape(1, heads),
            head_rate.reshape(1, heads),
            skip_gain.reshape(1, heads),
            gain,
        ),
    )
    gg_oth = lax.ppermute(gg, "yl", pair)
    keep, send = call(
        output_kernel,
        (
            jax.ShapeDtypeStruct((8, 2 * rows, wide + 64), F32),
            jax.ShapeDtypeStruct((8, 2 * rows, wide + 64), BF),
        ),
        (
            turned,
            gg,
            gg_oth,
            gain,
            out_own,
            ring_r[1],
            ring_l[1],
            ring_r[2],
            ring_l[2],
            ring_r[3],
            ring_l[3],
            far_r,
            far_l,
        ),
        in_smem=1,
        flops=2 * 4 * rows * inner * 8 * wide,
    )
    got = lax.ppermute(send, "core", pair)
    paired = call(pair_kernel, jax.ShapeDtypeStruct((8, 2 * rows, wide + 64), BF), (keep, got))
    partial_out = lax.all_to_all(paired, ("x", "yh"), 0, 0)
    mine = call(
        functools.partial(reduce_kernel, count=float(16 * inner)),
        jax.ShapeDtypeStruct((2 * rows, wide), BF),
        (partial_out,),
    )
    back = lax.ppermute(mine, ("yl", "core"), [(0, 0), (1, 2), (2, 1), (3, 3)])
    result = (own_embed.astype(F32) + back.astype(F32)).reshape(2, rows, wide)
    live = jnp.arange(rows, dtype=jnp.int32) < row_counts[0]
    return jnp.where(live[None, :, None], result, 0.0).astype(BF)


def solution(mesh):
    fine = Mesh(mesh.devices.reshape(8, 2, 4, 2, 2), ALL)
    return jax.shard_map(
        per_device,
        mesh=fine,
        in_specs=(
            P(None, GROUP),
            P(GROUP),
            P(None, TP),
            P(GROUP, TP),
            P(GROUP, TP),
            P(GROUP, TP),
            P(GROUP, TP),
            P(TP),
            P(TP),
            P(TP),
            P(TP),
            P(TP, GROUP),
            P(GROUP, TP, None, None),
        ),
        out_specs=P(None, GROUP, TP),
        check_vma=False,
    )
```

```python
import functools

import jax
import jax.numpy as jnp
from jax import lax
from jax.experimental import pallas as pl
from jax.experimental.pallas import tpu as pltpu
from jax.sharding import Mesh
from jax.sharding import PartitionSpec as P


BF = jnp.bfloat16
F32 = jnp.float32
SCALE = 2.0**-20
GROUP = ("z", "yl")
TP = ("x", "yh", "core")
ALL = GROUP + TP
VMEM_LIMIT = 14 * 1024 * 1024
PROJECT_LIMIT = 58 * 1024 * 1024
STATE_LIMIT = 52 * 1024 * 1024

SHIFTS = (3, 2, 5, 6, 1, 7)


def nt(a, b):
    return lax.dot_general(a, b, (((1,), (1,)), ((), ())), preferred_element_type=F32)


def nn(a, b):
    return jnp.dot(a, b, preferred_element_type=F32)


def call(body, out_shape, args, in_smem=0, flops=1 << 20, grid=None, in_specs=None, out_specs=None, scratch=(), limit=VMEM_LIMIT):
    if in_specs is None:
        in_specs = [pl.BlockSpec(memory_space=pltpu.SMEM)] * in_smem + [
            pl.BlockSpec(memory_space=pltpu.VMEM)
        ] * (len(args) - in_smem)
        out_specs = jax.tree.map(lambda _: pl.BlockSpec(memory_space=pltpu.VMEM), out_shape)
    kwargs = {} if grid is None else {"grid": grid}
    return pl.pallas_call(
        body,
        out_shape=out_shape,
        in_specs=in_specs,
        out_specs=out_specs,
        scratch_shapes=scratch,
        compiler_params=pltpu.CompilerParams(vmem_limit_bytes=limit),
        cost_estimate=pl.CostEstimate(flops=flops, bytes_accessed=1 << 20, transcendentals=0),
        **kwargs,
    )(*args)


def split2(v):
    hi = v.astype(BF)
    return hi, (v - hi.astype(F32)).astype(BF)


def project_small_kernel(flag, e_own, e_oth, s_own, s_oth, out):
    groups, rows, width = out.shape

    def run(ea, eb):
        ps = nt(ea[...], s_own[...]) + nt(eb[...], s_oth[...])
        hi, lo = split2(ps)
        out[...] = jnp.concatenate([hi, lo], 1).reshape(groups, rows, width)

    @pl.when(flag[0] == 1)
    def _():
        run(e_own, e_oth)

    @pl.when(flag[0] == 0)
    def _():
        run(e_oth, e_own)


def project_kernel(place, e_own, e_oth, x_own, x_oth, z_own, z_oth, *refs):
    outs, (both, held, done, sems) = refs[:8], refs[8:]
    depth, inner = x_own.shape
    groups, rows = len(outs), outs[0].shape[0]
    sources = ((x_own, x_oth), (z_own, z_oth))
    loads = [
        [
            pltpu.make_async_copy(ref, held.at[k, pl.ds(j * depth, depth)], sems.at[2 * k + j])
            for j, ref in enumerate(refs)
        ]
        for k, refs in enumerate(sources)
    ]
    for pair in loads:
        for load in pair:
            load.start()

    def fill(ea, eb):
        both[:, :depth] = ea[...]
        both[:, depth:] = eb[...]

    @pl.when(place[0] == 1)
    def _():
        fill(e_own, e_oth)

    @pl.when(place[0] == 0)
    def _():
        fill(e_oth, e_own)

    stores = []
    for k in range(2):
        for load in loads[k]:
            load.wait()
        total = nn(both[...], held[k])
        done[k] = total.astype(BF).reshape(groups, rows, inner)
        for j in range(groups):
            stores.append(
                pltpu.make_async_copy(
                    done.at[k, lax.rem(place[1] + j, groups)],
                    outs[j].at[:, pl.ds(k * inner, inner)],
                    sems.at[4 + k * groups + j],
                )
            )
            stores[-1].start()
    for store in stores:
        store.wait()


def join_kernel(own, passed, out):
    out[...] = (own[...].astype(F32) + passed[...].astype(F32)).astype(BF)


def small_kernel(part, bc, small):
    total = part[0].astype(F32)
    for k in range(1, part.shape[0]):
        total = total + part[k].astype(F32)
    total = total[:, :64] + total[:, 64:]
    hi, lo = split2(total)
    bc[...] = jnp.concatenate([hi, lo], 1)
    small[...] = total


def state_kernel(place, bc0, bc1, bc2, bc3, s, out, dots, cmat, pieces_ref, held, sems):
    rows = cmat.shape[0]
    chunks = sems.shape[0]
    step = rows // chunks
    copies = [
        pltpu.make_async_copy(
            s.at[pl.ds(k * step, step)], held.at[pl.ds(k * step, step)], sems.at[k]
        )
        for k in range(chunks)
    ]
    for copy in copies:
        copy.start()
    for shift, bc in ((0, bc0), (1, bc1), (2, bc2), (3, bc3)):
        x = lax.rem(place[0] + shift, 4)
        for k in range(4):
            yh = lax.rem(place[1] + k // 2, 2)
            core = lax.rem(place[2] + k % 2, 2)
            pieces_ref[(x * 2 + yh) * 2 + core] = bc[k]
    pieces = [pieces_ref[t] for t in range(16)]
    pieces = [p[:, :32].astype(F32) + p[:, 64:96].astype(F32) for p in pieces]
    b = jnp.concatenate(pieces[:8], 1)
    c = jnp.concatenate(pieces[8:], 1)
    b1, b2, c1, c2 = b[:rows], b[rows:], c[:rows], c[rows:]
    lane = lax.broadcasted_iota(jnp.int32, dots.shape, 1)
    b11 = jnp.sum(b1 * c1, axis=1, keepdims=True)
    b12 = jnp.sum(b1 * c2, axis=1, keepdims=True)
    b22 = jnp.sum(b2 * c2, axis=1, keepdims=True)
    dots[...] = jnp.where(lane == 0, b11, jnp.where(lane == 1, b12, b22))
    cmat[...] = jnp.zeros_like(cmat)
    for k, v in enumerate((c1, c2)):
        v = v * SCALE
        hi = v.astype(BF).astype(F32)
        cmat[:, 2 * k, :] = hi
        cmat[:, 2 * k + 1, :] = v - hi
    for k in range(chunks):
        copies[k].wait()
        for r in range(k * step, (k + 1) * step):
            m = held[r].reshape(s.shape[1] * s.shape[2], s.shape[3])
            out[r] = nt(cmat[r].astype(BF), m)


def decode_kernel(*refs):
    parts, (small, dots, g, bias, rate, skip, gain, out) = refs[:7], refs[7:]
    heads = bias.shape[1]
    inner = gain.shape[1]
    half = parts[0].shape[0] // 2
    total = parts[0][...].astype(F32)
    for part in parts[1:]:
        total = total + part[...].astype(F32)
    x_pre = total[:, :inner]
    z_pre = total[:, inner:]
    pick = (
        lax.broadcasted_iota(jnp.int32, (heads, inner), 0)
        == lax.broadcasted_iota(jnp.int32, (heads, inner), 1) // (inner // heads)
    ).astype(F32)
    expand = functools.partial(
        jnp.dot, preferred_element_type=F32, precision=lax.Precision.HIGHEST
    )
    dt_pre = expand(small[:, 32 : 32 + heads], pick)
    bias_e = expand(bias[...], pick)
    rate_e = expand(rate[...], pick)
    skip_e = expand(skip[...], pick)
    pre = dt_pre + bias_e
    dt = jnp.maximum(pre, 0.0) + jnp.log1p(jnp.exp(-jnp.abs(pre)))
    decay = jnp.exp(-dt * rate_e)
    inputs = x_pre * jax.nn.sigmoid(x_pre)
    upd = dt * inputs
    gate = z_pre * jax.nn.sigmoid(z_pre)
    b11 = dots[:, 0:1]
    b12 = dots[:, 1:2]
    b22 = dots[:, 2:3]
    gs = g[...]
    g1 = gs[:, 0, :] + gs[:, 1, :]
    g2 = gs[:, 2, :] + gs[:, 3, :]
    d1, d2 = decay[:half], decay[half:]
    u1, u2 = upd[:half], upd[half:]
    read1 = (d1 * g1) * (1.0 / SCALE) + u1 * b11 + skip_e * inputs[:half]
    read2 = d2 * ((d1 * g2) * (1.0 / SCALE) + u1 * b12) + u2 * b22 + skip_e * inputs[half:]
    lim = 1e30
    gg1 = jnp.clip(read1 * gate[:half] * gain[...], -lim, lim)
    gg2 = jnp.clip(read2 * gate[half:] * gain[...], -lim, lim)
    out[...] = jnp.concatenate([gg1, gg2], 0).astype(BF)


def output_kernel(place, mine, other, gain, own, r1, l1, r2, l2, r3, l3, r4, keep, send):
    z = place[0]
    same = place[1]
    groups, rows, _ = keep.shape
    m = mine[...]
    o = other[...]
    v = jnp.concatenate([jnp.where(same == 1, m, o), jnp.where(same == 1, o, m)], 0)
    raw = v.astype(F32) / gain[...]
    ss = jnp.sum(raw * raw, axis=1, keepdims=True)
    hi = ss.astype(BF).astype(F32)
    lane = lax.broadcasted_iota(jnp.int32, (2 * rows, 64), 1)
    tail = jnp.where(lane == 0, hi, jnp.where(lane == 1, ss - hi, 0.0))
    order = ((0, own), (7, r1), (1, l1), (6, r2), (2, l2), (5, r3), (3, l3), (4, r4))
    for shift, w in order:
        block = jnp.concatenate([nt(v, w[...]), tail], 1)
        at = lax.rem(z + shift, groups)
        keep[at] = block[:rows]
        send[at] = block[rows:].astype(BF)


def pair_kernel(keep, got, out):
    total = keep[...] + got[...].astype(F32)
    cols = out.shape[2] - 64
    lane = lax.broadcasted_iota(jnp.int32, total.shape, 2)
    ss = total[:, :, cols : cols + 1] + total[:, :, cols + 1 : cols + 2]
    hi = ss.astype(BF).astype(F32)
    total = jnp.where(lane == cols, hi, jnp.where(lane == cols + 1, ss - hi, total))
    out[...] = total.astype(BF)


def reduce_kernel(part, out, *, count):
    total = part[0].astype(F32)
    for k in range(1, part.shape[0]):
        total = total + part[k].astype(F32)
    cols = out.shape[1]
    ss = total[:, cols : cols + 1] + total[:, cols + 1 : cols + 2]
    out[...] = (total[:, :cols] * lax.rsqrt(ss / count + 1e-05)).astype(BF)


def per_device(
    token_ids,
    row_counts,
    code_table,
    x_weight,
    z_weight,
    dt_weight,
    bc_weight,
    dt_bias,
    head_rate,
    skip_gain,
    norm_gain,
    out_weight,
    ssm_state,
):
    rows = token_ids.shape[1]
    heads = dt_bias.shape[0]
    inner = x_weight.shape[1]
    wide = code_table.shape[1]
    y = lax.axis_index("yl")
    core = lax.axis_index("core")
    swap = []
    for z in range(8):
        for yy in range(2):
            for w in range(8):
                for c in range(2):
                    swap.append(((z * 2 + yy) * 16 + w * 2 + c, (w * 2 + yy) * 16 + z * 2 + c))
    pair = [(0, 1), (1, 0)]

    gain = norm_gain.reshape(1, inner)
    right = [(i, (i + 1) % 8) for i in range(8)]
    left = [(i, (i + 7) % 8) for i in range(8)]
    out_own = out_weight.T
    ring_r = [out_own]
    ring_l = [out_own]
    for _ in range(1, 4):
        ring_r.append(lax.ppermute(ring_r[-1], "z", right))
        ring_l.append(lax.ppermute(ring_l[-1], "z", left))
    ring_r.append(lax.ppermute(ring_r[3], "z", right))
    x_oth = lax.ppermute(x_weight, "yl", pair)
    z_oth = lax.ppermute(z_weight, "yl", pair)
    small_own = jnp.concatenate(
        [bc_weight.T, dt_weight.T, jnp.zeros((64 - 32 - heads, wide), BF)], 0
    )
    small_oth = lax.ppermute(small_own, "yl", pair)

    flat_ids = token_ids.reshape(-1)
    codes = jnp.arange(code_table.shape[0], dtype=jnp.int32)
    one_hot = (flat_ids[:, None] == codes[None, :]).astype(BF)
    own_embed = jnp.dot(one_hot, code_table, preferred_element_type=F32).astype(BF)
    moved = lax.ppermute(own_embed, ALL, swap)
    e_own = lax.all_to_all(
        jnp.broadcast_to(moved[None], (8,) + moved.shape), ("x", "yh"), 0, 0
    ).reshape(8 * 2 * rows, wide)
    e_oth = lax.ppermute(e_own, "core", pair)
    same = (y == core).astype(jnp.int32)
    z = lax.axis_index("z")
    place = jnp.stack([same, z])
    plane = jnp.stack([lax.axis_index("x"), lax.axis_index("yh"), core])
    turned = jnp.stack([z, same])
    part_small = call(
        project_small_kernel,
        jax.ShapeDtypeStruct((8, 2 * rows, 128), BF),
        (place, e_own, e_oth, small_own, small_oth),
        in_smem=1,
        flops=2 * 16 * rows * 2 * wide * 128,
    )
    part_small = lax.all_to_all(part_small, "z", 0, 0)
    blocks = call(
        project_kernel,
        tuple(jax.ShapeDtypeStruct((2 * rows, 2 * inner), BF) for _ in range(8)),
        (place, e_own, e_oth, x_weight, x_oth, z_weight, z_oth),
        in_specs=[pl.BlockSpec(memory_space=pltpu.SMEM)]
        + [pl.BlockSpec(memory_space=pltpu.VMEM)] * 2
        + [pl.BlockSpec(memory_space=pl.ANY)] * 4,
        out_specs=tuple(pl.BlockSpec(memory_space=pl.ANY) for _ in range(8)),
        scratch=[
            pltpu.VMEM((16 * rows, 2 * wide), BF),
            pltpu.VMEM((2, 2 * wide, inner), BF),
            pltpu.VMEM((2, 8, 2 * rows, inner), BF),
            pltpu.SemaphoreType.DMA((20,)),
        ],
        limit=PROJECT_LIMIT,
        flops=2 * 16 * rows * 2 * wide * 2 * inner,
    )
    blocks = list(blocks)
    passed = lax.ppermute(blocks[4], "z", left)
    blocks[5] = call(join_kernel, jax.ShapeDtypeStruct(blocks[5].shape, BF), (blocks[5], passed))
    parts = [blocks[0]]
    for k in SHIFTS:
        parts.append(lax.ppermute(blocks[k], "z", [(i, (i + k) % 8) for i in range(8)]))
    bc, small = call(
        small_kernel,
        (jax.ShapeDtypeStruct((2 * rows, 128), BF), jax.ShapeDtypeStruct((2 * rows, 64), F32)),
        (part_small,),
    )
    bc2 = jnp.stack([bc, lax.ppermute(bc, "core", pair)])
    bc4 = jnp.concatenate([bc2, lax.ppermute(bc2, "yh", pair)], 0)
    bc_all = [bc4]
    for k in (1, 2, 3):
        bc_all.append(lax.ppermute(bc4, "x", [((i + k) % 4, i) for i in range(4)]))
    g, dots = call(
        state_kernel,
        (jax.ShapeDtypeStruct((rows, 8, inner), F32), jax.ShapeDtypeStruct((rows, 128), F32)),
        (plane, *bc_all, ssm_state),
        in_specs=[pl.BlockSpec(memory_space=pltpu.SMEM)]
        + [pl.BlockSpec(memory_space=pltpu.VMEM)] * 4
        + [pl.BlockSpec(memory_space=pl.ANY)],
        out_specs=(pl.BlockSpec(memory_space=pltpu.VMEM), pl.BlockSpec(memory_space=pltpu.VMEM)),
        scratch=[
            pltpu.VMEM((rows, 8, 256), F32),
            pltpu.VMEM((16, 2 * rows, 128), BF),
            pltpu.VMEM(ssm_state.shape, BF),
            pltpu.SemaphoreType.DMA((8,)),
        ],
        limit=STATE_LIMIT,
        flops=2 * 8 * rows * inner * 256,
    )
    gg = call(
        decode_kernel,
        jax.ShapeDtypeStruct((2 * rows, inner), BF),
        (
            *parts,
            small,
            dots,
            g,
            dt_bias.reshape(1, heads),
            head_rate.reshape(1, heads),
            skip_gain.reshape(1, heads),
            gain,
        ),
    )
    gg_oth = lax.ppermute(gg, "yl", pair)
    keep, send = call(
        output_kernel,
        (
            jax.ShapeDtypeStruct((8, 2 * rows, wide + 64), F32),
            jax.ShapeDtypeStruct((8, 2 * rows, wide + 64), BF),
        ),
        (
            turned,
            gg,
            gg_oth,
            gain,
            out_own,
            ring_r[1],
            ring_l[1],
            ring_r[2],
            ring_l[2],
            ring_r[3],
            ring_l[3],
            ring_r[4],
        ),
        in_smem=1,
        flops=2 * 4 * rows * inner * 8 * wide,
    )
    got = lax.ppermute(send, "core", pair)
    paired = call(pair_kernel, jax.ShapeDtypeStruct((8, 2 * rows, wide + 64), BF), (keep, got))
    partial_out = lax.all_to_all(paired, ("x", "yh"), 0, 0)
    mine = call(
        functools.partial(reduce_kernel, count=float(16 * inner)),
        jax.ShapeDtypeStruct((2 * rows, wide), BF),
        (partial_out,),
    )
    back = lax.ppermute(mine, ("yl", "core"), [(0, 0), (1, 2), (2, 1), (3, 3)])
    result = (own_embed.astype(F32) + back.astype(F32)).reshape(2, rows, wide)
    live = jnp.arange(rows, dtype=jnp.int32) < row_counts[0]
    return jnp.where(live[None, :, None], result, 0.0).astype(BF)


def solution(mesh):
    fine = Mesh(mesh.devices.reshape(8, 2, 4, 2, 2), ALL)
    return jax.shard_map(
        per_device,
        mesh=fine,
        in_specs=(
            P(None, GROUP),
            P(GROUP),
            P(None, TP),
            P(GROUP, TP),
            P(GROUP, TP),
            P(GROUP, TP),
            P(GROUP, TP),
            P(TP),
            P(TP),
            P(TP),
            P(TP),
            P(TP, GROUP),
            P(GROUP, TP, None, None),
        ),
        out_specs=P(None, GROUP, TP),
        check_vma=False,
    )
```

```python
import functools

import jax
import jax.numpy as jnp
from jax import lax
from jax.experimental import pallas as pl
from jax.experimental.pallas import tpu as pltpu
from jax.sharding import Mesh
from jax.sharding import PartitionSpec as P


BF = jnp.bfloat16
F32 = jnp.float32
SCALE = 2.0**-20
GROUP = ("z", "yl")
TP = ("x", "yh", "core")
ALL = GROUP + TP
VMEM_LIMIT = 14 * 1024 * 1024
PROJECT_LIMIT = 58 * 1024 * 1024
STATE_LIMIT = 52 * 1024 * 1024

SHIFTS = (3, 2, 5, 6, 1, 7)


def nt(a, b):
    return lax.dot_general(a, b, (((1,), (1,)), ((), ())), preferred_element_type=F32)


def nn(a, b):
    return jnp.dot(a, b, preferred_element_type=F32)


def call(body, out_shape, args, in_smem=0, flops=1 << 20, grid=None, in_specs=None, out_specs=None, scratch=(), limit=VMEM_LIMIT):
    if in_specs is None:
        in_specs = [pl.BlockSpec(memory_space=pltpu.SMEM)] * in_smem + [
            pl.BlockSpec(memory_space=pltpu.VMEM)
        ] * (len(args) - in_smem)
        out_specs = jax.tree.map(lambda _: pl.BlockSpec(memory_space=pltpu.VMEM), out_shape)
    kwargs = {} if grid is None else {"grid": grid}
    return pl.pallas_call(
        body,
        out_shape=out_shape,
        in_specs=in_specs,
        out_specs=out_specs,
        scratch_shapes=scratch,
        compiler_params=pltpu.CompilerParams(vmem_limit_bytes=limit),
        cost_estimate=pl.CostEstimate(flops=flops, bytes_accessed=1 << 20, transcendentals=0),
        **kwargs,
    )(*args)


def split2(v):
    hi = v.astype(BF)
    return hi, (v - hi.astype(F32)).astype(BF)


def project_small_kernel(flag, e_own, e_oth, s_own, s_oth, out):
    groups, rows, width = out.shape

    def run(ea, eb):
        ps = nt(ea[...], s_own[...]) + nt(eb[...], s_oth[...])
        hi, lo = split2(ps)
        out[...] = jnp.concatenate([hi, lo], 1).reshape(groups, rows, width)

    @pl.when(flag[0] == 1)
    def _():
        run(e_own, e_oth)

    @pl.when(flag[0] == 0)
    def _():
        run(e_oth, e_own)


def project_kernel(place, e_own, e_oth, x_own, x_oth, z_own, z_oth, *refs):
    outs, (both, held, done, sems) = refs[:8], refs[8:]
    depth, inner = x_own.shape
    groups, rows = len(outs), outs[0].shape[0]
    sources = ((x_own, x_oth), (z_own, z_oth))
    loads = [
        [
            pltpu.make_async_copy(ref, held.at[k, pl.ds(j * depth, depth)], sems.at[2 * k + j])
            for j, ref in enumerate(refs)
        ]
        for k, refs in enumerate(sources)
    ]
    for pair in loads:
        for load in pair:
            load.start()

    def fill(ea, eb):
        both[:, :depth] = ea[...]
        both[:, depth:] = eb[...]

    @pl.when(place[0] == 1)
    def _():
        fill(e_own, e_oth)

    @pl.when(place[0] == 0)
    def _():
        fill(e_oth, e_own)

    stores = []
    for k in range(2):
        for load in loads[k]:
            load.wait()
        total = nn(both[...], held[k])
        done[k] = total.astype(BF).reshape(groups, rows, inner)
        for j in range(groups):
            stores.append(
                pltpu.make_async_copy(
                    done.at[k, lax.rem(place[1] + j, groups)],
                    outs[j].at[:, pl.ds(k * inner, inner)],
                    sems.at[4 + k * groups + j],
                )
            )
            stores[-1].start()
    for store in stores:
        store.wait()


def join_kernel(own, passed, out):
    out[...] = (own[...].astype(F32) + passed[...].astype(F32)).astype(BF)


def small_kernel(part, bc, small):
    total = part[0].astype(F32)
    for k in range(1, part.shape[0]):
        total = total + part[k].astype(F32)
    total = total[:, :64] + total[:, 64:]
    hi, lo = split2(total)
    bc[...] = jnp.concatenate([hi, lo], 1)
    small[...] = total


def state_kernel(place, bc0, bc1, bc2, bc3, s, out, dots, cmat, pieces_ref, held, sems):
    rows = cmat.shape[0]
    chunks = sems.shape[0]
    step = rows // chunks
    copies = [
        pltpu.make_async_copy(
            s.at[pl.ds(k * step, step)], held.at[pl.ds(k * step, step)], sems.at[k]
        )
        for k in range(chunks)
    ]
    for copy in copies:
        copy.start()
    for shift, bc in ((0, bc0), (1, bc1), (2, bc2), (3, bc3)):
        x = lax.rem(place[0] + shift, 4)
        for k in range(4):
            yh = lax.rem(place[1] + k // 2, 2)
            core = lax.rem(place[2] + k % 2, 2)
            pieces_ref[(x * 2 + yh) * 2 + core] = bc[k]
    pieces = [pieces_ref[t] for t in range(16)]
    pieces = [p[:, :32].astype(F32) + p[:, 64:96].astype(F32) for p in pieces]
    b = jnp.concatenate(pieces[:8], 1)
    c = jnp.concatenate(pieces[8:], 1)
    b1, b2, c1, c2 = b[:rows], b[rows:], c[:rows], c[rows:]
    lane = lax.broadcasted_iota(jnp.int32, dots.shape, 1)
    b11 = jnp.sum(b1 * c1, axis=1, keepdims=True)
    b12 = jnp.sum(b1 * c2, axis=1, keepdims=True)
    b22 = jnp.sum(b2 * c2, axis=1, keepdims=True)
    dots[...] = jnp.where(lane == 0, b11, jnp.where(lane == 1, b12, b22))
    cmat[...] = jnp.zeros_like(cmat)
    for k, v in enumerate((c1, c2)):
        v = v * SCALE
        hi = v.astype(BF).astype(F32)
        cmat[:, 2 * k, :] = hi
        cmat[:, 2 * k + 1, :] = v - hi
    for k in range(chunks):
        copies[k].wait()
        for r in range(k * step, (k + 1) * step):
            m = held[r].reshape(s.shape[1] * s.shape[2], s.shape[3])
            out[r] = nt(cmat[r].astype(BF), m)


def decode_kernel(*refs):
    parts, (small, dots, g, bias, rate, skip, gain, out) = refs[:7], refs[7:]
    heads = bias.shape[1]
    inner = gain.shape[1]
    half = parts[0].shape[0] // 2
    total = parts[0][...].astype(F32)
    for part in parts[1:]:
        total = total + part[...].astype(F32)
    x_pre = total[:, :inner]
    z_pre = total[:, inner:]
    pick = (
        lax.broadcasted_iota(jnp.int32, (heads, inner), 0)
        == lax.broadcasted_iota(jnp.int32, (heads, inner), 1) // (inner // heads)
    ).astype(F32)
    expand = functools.partial(
        jnp.dot, preferred_element_type=F32, precision=lax.Precision.HIGHEST
    )
    dt_pre = expand(small[:, 32 : 32 + heads], pick)
    bias_e = expand(bias[...], pick)
    rate_e = expand(rate[...], pick)
    skip_e = expand(skip[...], pick)
    pre = dt_pre + bias_e
    dt = jnp.maximum(pre, 0.0) + jnp.log1p(jnp.exp(-jnp.abs(pre)))
    decay = jnp.exp(-dt * rate_e)
    inputs = x_pre * jax.nn.sigmoid(x_pre)
    upd = dt * inputs
    gate = z_pre * jax.nn.sigmoid(z_pre)
    b11 = dots[:, 0:1]
    b12 = dots[:, 1:2]
    b22 = dots[:, 2:3]
    gs = g[...]
    g1 = gs[:, 0, :] + gs[:, 1, :]
    g2 = gs[:, 2, :] + gs[:, 3, :]
    d1, d2 = decay[:half], decay[half:]
    u1, u2 = upd[:half], upd[half:]
    read1 = (d1 * g1) * (1.0 / SCALE) + u1 * b11 + skip_e * inputs[:half]
    read2 = d2 * ((d1 * g2) * (1.0 / SCALE) + u1 * b12) + u2 * b22 + skip_e * inputs[half:]
    lim = 1e30
    gg1 = jnp.clip(read1 * gate[:half] * gain[...], -lim, lim)
    gg2 = jnp.clip(read2 * gate[half:] * gain[...], -lim, lim)
    out[...] = jnp.concatenate([gg1, gg2], 0).astype(BF)


def output_kernel(place, mine, other, gain, own, r1, l1, r2, l2, r3, l3, r4, keep, send):
    z = place[0]
    same = place[1]
    groups, rows, _ = keep.shape
    m = mine[...]
    o = other[...]
    v = jnp.concatenate([jnp.where(same == 1, m, o), jnp.where(same == 1, o, m)], 0)
    raw = v.astype(F32) / gain[...]
    ss = jnp.sum(raw * raw, axis=1, keepdims=True)
    hi = ss.astype(BF).astype(F32)
    lane = lax.broadcasted_iota(jnp.int32, (2 * rows, 64), 1)
    tail = jnp.where(lane == 0, hi, jnp.where(lane == 1, ss - hi, 0.0))
    order = ((0, own), (7, r1), (1, l1), (6, r2), (2, l2), (5, r3), (3, l3), (4, r4))
    for shift, w in order:
        block = jnp.concatenate([nt(v, w[...]), tail], 1)
        at = lax.rem(z + shift, groups)
        keep[at] = block[:rows]
        send[at] = block[rows:].astype(BF)


def pair_kernel(keep, got, out):
    total = keep[...] + got[...].astype(F32)
    cols = out.shape[2] - 64
    lane = lax.broadcasted_iota(jnp.int32, total.shape, 2)
    ss = total[:, :, cols : cols + 1] + total[:, :, cols + 1 : cols + 2]
    hi = ss.astype(BF).astype(F32)
    total = jnp.where(lane == cols, hi, jnp.where(lane == cols + 1, ss - hi, total))
    out[...] = total.astype(BF)


def reduce_kernel(part, out, *, count):
    total = part[0].astype(F32)
    for k in range(1, part.shape[0]):
        total = total + part[k].astype(F32)
    cols = out.shape[1]
    ss = total[:, cols : cols + 1] + total[:, cols + 1 : cols + 2]
    out[...] = (total[:, :cols] * lax.rsqrt(ss / count + 1e-05)).astype(BF)


def final_kernel(counts, own, back, out):
    total = (own[...].astype(F32) + back[...].astype(F32)).reshape(out.shape)
    live = lax.broadcasted_iota(jnp.int32, out.shape, 1) < counts[0]
    out[...] = jnp.where(live, total, 0.0).astype(BF)


def per_device(
    token_ids,
    row_counts,
    code_table,
    x_weight,
    z_weight,
    dt_weight,
    bc_weight,
    dt_bias,
    head_rate,
    skip_gain,
    norm_gain,
    out_weight,
    ssm_state,
):
    rows = token_ids.shape[1]
    heads = dt_bias.shape[0]
    inner = x_weight.shape[1]
    wide = code_table.shape[1]
    y = lax.axis_index("yl")
    core = lax.axis_index("core")
    swap = []
    for z in range(8):
        for yy in range(2):
            for w in range(8):
                for c in range(2):
                    swap.append(((z * 2 + yy) * 16 + w * 2 + c, (w * 2 + yy) * 16 + z * 2 + c))
    pair = [(0, 1), (1, 0)]

    gain = norm_gain.reshape(1, inner)
    right = [(i, (i + 1) % 8) for i in range(8)]
    left = [(i, (i + 7) % 8) for i in range(8)]
    out_own = out_weight.T
    ring_r = [out_own]
    ring_l = [out_own]
    for _ in range(1, 4):
        ring_r.append(lax.ppermute(ring_r[-1], "z", right))
        ring_l.append(lax.ppermute(ring_l[-1], "z", left))
    ring_r.append(lax.ppermute(ring_r[3], "z", right))
    x_oth = lax.ppermute(x_weight, "yl", pair)
    z_oth = lax.ppermute(z_weight, "yl", pair)
    small_own = jnp.concatenate(
        [bc_weight.T, dt_weight.T, jnp.zeros((64 - 32 - heads, wide), BF)], 0
    )
    small_oth = lax.ppermute(small_own, "yl", pair)

    flat_ids = token_ids.reshape(-1)
    codes = jnp.arange(code_table.shape[0], dtype=jnp.int32)
    one_hot = (flat_ids[:, None] == codes[None, :]).astype(BF)
    own_embed = jnp.dot(one_hot, code_table, preferred_element_type=F32).astype(BF)
    moved = lax.ppermute(own_embed, ALL, swap)
    e_own = lax.all_to_all(
        jnp.broadcast_to(moved[None], (8,) + moved.shape), ("x", "yh"), 0, 0
    ).reshape(8 * 2 * rows, wide)
    e_oth = lax.ppermute(e_own, "core", pair)
    same = (y == core).astype(jnp.int32)
    z = lax.axis_index("z")
    place = jnp.stack([same, z])
    plane = jnp.stack([lax.axis_index("x"), lax.axis_index("yh"), core])
    turned = jnp.stack([z, same])
    part_small = call(
        project_small_kernel,
        jax.ShapeDtypeStruct((8, 2 * rows, 128), BF),
        (place, e_own, e_oth, small_own, small_oth),
        in_smem=1,
        flops=2 * 16 * rows * 2 * wide * 128,
    )
    part_small = lax.all_to_all(part_small, "z", 0, 0)
    blocks = call(
        project_kernel,
        tuple(jax.ShapeDtypeStruct((2 * rows, 2 * inner), BF) for _ in range(8)),
        (place, e_own, e_oth, x_weight, x_oth, z_weight, z_oth),
        in_specs=[pl.BlockSpec(memory_space=pltpu.SMEM)]
        + [pl.BlockSpec(memory_space=pltpu.VMEM)] * 2
        + [pl.BlockSpec(memory_space=pl.ANY)] * 4,
        out_specs=tuple(pl.BlockSpec(memory_space=pl.ANY) for _ in range(8)),
        scratch=[
            pltpu.VMEM((16 * rows, 2 * wide), BF),
            pltpu.VMEM((2, 2 * wide, inner), BF),
            pltpu.VMEM((2, 8, 2 * rows, inner), BF),
            pltpu.SemaphoreType.DMA((20,)),
        ],
        limit=PROJECT_LIMIT,
        flops=2 * 16 * rows * 2 * wide * 2 * inner,
    )
    blocks = list(blocks)
    passed = lax.ppermute(blocks[4], "z", left)
    blocks[5] = call(join_kernel, jax.ShapeDtypeStruct(blocks[5].shape, BF), (blocks[5], passed))
    parts = [blocks[0]]
    for k in SHIFTS:
        parts.append(lax.ppermute(blocks[k], "z", [(i, (i + k) % 8) for i in range(8)]))
    bc, small = call(
        small_kernel,
        (jax.ShapeDtypeStruct((2 * rows, 128), BF), jax.ShapeDtypeStruct((2 * rows, 64), F32)),
        (part_small,),
    )
    bc2 = jnp.stack([bc, lax.ppermute(bc, "core", pair)])
    bc4 = jnp.concatenate([bc2, lax.ppermute(bc2, "yh", pair)], 0)
    bc_all = [bc4]
    for k in (1, 2, 3):
        bc_all.append(lax.ppermute(bc4, "x", [((i + k) % 4, i) for i in range(4)]))
    g, dots = call(
        state_kernel,
        (jax.ShapeDtypeStruct((rows, 8, inner), F32), jax.ShapeDtypeStruct((rows, 128), F32)),
        (plane, *bc_all, ssm_state),
        in_specs=[pl.BlockSpec(memory_space=pltpu.SMEM)]
        + [pl.BlockSpec(memory_space=pltpu.VMEM)] * 4
        + [pl.BlockSpec(memory_space=pl.ANY)],
        out_specs=(pl.BlockSpec(memory_space=pltpu.VMEM), pl.BlockSpec(memory_space=pltpu.VMEM)),
        scratch=[
            pltpu.VMEM((rows, 8, 256), F32),
            pltpu.VMEM((16, 2 * rows, 128), BF),
            pltpu.VMEM(ssm_state.shape, BF),
            pltpu.SemaphoreType.DMA((8,)),
        ],
        limit=STATE_LIMIT,
        flops=2 * 8 * rows * inner * 256,
    )
    gg = call(
        decode_kernel,
        jax.ShapeDtypeStruct((2 * rows, inner), BF),
        (
            *parts,
            small,
            dots,
            g,
            dt_bias.reshape(1, heads),
            head_rate.reshape(1, heads),
            skip_gain.reshape(1, heads),
            gain,
        ),
    )
    gg_oth = lax.ppermute(gg, "yl", pair)
    keep, send = call(
        output_kernel,
        (
            jax.ShapeDtypeStruct((8, 2 * rows, wide + 64), F32),
            jax.ShapeDtypeStruct((8, 2 * rows, wide + 64), BF),
        ),
        (
            turned,
            gg,
            gg_oth,
            gain,
            out_own,
            ring_r[1],
            ring_l[1],
            ring_r[2],
            ring_l[2],
            ring_r[3],
            ring_l[3],
            ring_r[4],
        ),
        in_smem=1,
        flops=2 * 4 * rows * inner * 8 * wide,
    )
    got = lax.ppermute(send, "core", pair)
    paired = call(pair_kernel, jax.ShapeDtypeStruct((8, 2 * rows, wide + 64), BF), (keep, got))
    partial_out = lax.all_to_all(paired, ("x", "yh"), 0, 0)
    mine = call(
        functools.partial(reduce_kernel, count=float(16 * inner)),
        jax.ShapeDtypeStruct((2 * rows, wide), BF),
        (partial_out,),
    )
    back = lax.ppermute(mine, ("yl", "core"), [(0, 0), (1, 2), (2, 1), (3, 3)])
    return call(
        final_kernel,
        jax.ShapeDtypeStruct((2, rows, wide), BF),
        (row_counts, own_embed, back),
        in_smem=1,
    )


def solution(mesh):
    fine = Mesh(mesh.devices.reshape(8, 2, 4, 2, 2), ALL)
    return jax.shard_map(
        per_device,
        mesh=fine,
        in_specs=(
            P(None, GROUP),
            P(GROUP),
            P(None, TP),
            P(GROUP, TP),
            P(GROUP, TP),
            P(GROUP, TP),
            P(GROUP, TP),
            P(TP),
            P(TP),
            P(TP),
            P(TP),
            P(TP, GROUP),
            P(GROUP, TP, None, None),
        ),
        out_specs=P(None, GROUP, TP),
        check_vma=False,
    )
```
